128 devices in a mesh: blk: 32 (over x, z, core), sim: 4 (over y).
Axes of the slice: x: 4, y: 4, z: 4, core: 2. Of those that a mesh axis runs over, the one named last changes fastest.
Arguments:
- sky_maps: float32 [2, 32, 64, 4096], P(None, 'sim', 'blk'), may hold values from -30 to 30
- noise_weight: float32 [64, 4096], P('blk'), may hold values from 0.5 to 2
- signal_inverse: float32 [2048], replicated, may hold values from 0.1 to 3
- legendre: bfloat16 [1088, 16, 64, 128], P('blk'), may hold values from -4 to 4, as said below
- m_groups: int32 [32, 4], replicated, may hold values from 0 to 127, as said below
- block_list: int32 [1088, 2], P('blk'), may hold values from 0 to 15, as said below
- band_of_ell: int32 [2048], replicated, may hold values from 0 to 31, never falling along the last dimension, each value on 1 to 128 neighbouring positions
Outputs:
- filtered: bfloat16 [1088, 16, 2, 32, 2, 128], P('blk', None, None, 'sim')
- band_proj: float32 [32, 32], P('sim')
- fisher: float32 [32, 32], replicated
The draws below stay inside these ranges and needn't reach their ends.
Inputs may be any that keep to these rules, and one draw needn't show every extreme that they name: `m_groups`: each index of blk owns 4 distinct groups of 16 orders, in pairs k and 127 - k; every group of 0 to 127 is owned once. `block_list`: rows d * 34 to (d + 1) * 34 - 1 list, in some order and each once, the pairs (slot s, degree block e) of index d of blk with e at least 16 * m_groups[d, s] // 128. `legendre`: entries with degree below order are zero.
All inputs are finite; a program needn't handle non-finite values.
Results may differ from the reference program's by a relative error of at most 0.014.
Values may be sent and summed in bfloat16 or wider, within the bound.
No kernel may reach another device: no remote copies, remote signals or barrier semaphores. Data moves between devices by JAX's collectives and lax.ppermute only.
A program may use at most 192 MiB of HBM per device.

```python
import math
import jax
import jax.numpy as jnp
import numpy as np
from jax import lax

L = 2048
NPHI = 4096
LB = 128
MG = 16
BANDS = 32
ITERS = 4
CYCLES = 64
SIMS = 32
NG = 128
GDEV = 4
NLB = 16
NBD = 34
NBLOCKS = 1088


def mode_layout(key):
    pair_count = NG // 2
    pair_ids = jax.random.permutation(jax.random.fold_in(key, 11), pair_count).astype(jnp.int32)
    pair_ids = pair_ids.reshape(NG // GDEV, GDEV // 2)
    groups = jnp.concatenate([pair_ids, NG - 1 - pair_ids], axis=1)
    scores = jax.random.randint(jax.random.fold_in(key, 12), groups.shape, 0, 1 << 20, dtype=jnp.int32) * GDEV
    scores = scores + jnp.arange(GDEV, dtype=jnp.int32)[None, :]
    shuffle = jnp.argsort(scores, axis=1).astype(jnp.int32)
    groups = jnp.take_along_axis(groups, shuffle, axis=1)
    first_block = groups * MG // LB
    degree_range = jnp.arange(NLB, dtype=jnp.int32)
    usable = (degree_range[None, None, :] >= first_block[:, :, None]).reshape(NG // GDEV, GDEV * NLB)
    width = GDEV * NLB
    candidate = jax.random.randint(jax.random.fold_in(key, 13), usable.shape, 0, 1 << 16, dtype=jnp.int32) * width
    candidate = candidate + jnp.arange(width, dtype=jnp.int32)[None, :]
    candidate = jnp.where(usable, candidate, candidate + (1 << 16) * width)
    picked = jnp.argsort(candidate, axis=1)[:, :NBD].astype(jnp.int32)
    slot_ids = picked // NLB
    degree_ids = picked % NLB
    blocks = jnp.stack([slot_ids, degree_ids], axis=-1).reshape(NBLOCKS, 2)
    return (groups, blocks)


def draw_m_groups(key, part):
    return mode_layout(key)[0]


def draw_block_list(key, part):
    return mode_layout(key)[1]


def draw_legendre(key, part):
    groups, blocks = mode_layout(key)
    jitter = jax.random.uniform(jax.random.fold_in(key, 14), (CYCLES,), jnp.float32, -0.3, 0.3)
    spacing = 0.2 / CYCLES
    cosine = -0.1 + spacing * (jnp.arange(CYCLES, dtype=jnp.float32) + 0.5 + jitter)
    log_sine = 0.5 * jnp.log(1.0 - cosine * cosine)
    orders = jnp.arange(L, dtype=jnp.float32)
    log_norm = 0.5 * (jnp.log(2.0 * orders + 1.0) - math.log(4.0 * math.pi) + lax.lgamma(2.0 * orders + 1.0) - 2.0 * orders * math.log(2.0) - 2.0 * lax.lgamma(orders + 1.0))
    diagonal = jnp.exp(log_norm[:, None] + orders[:, None] * log_sine[None, :])
    cycle_weight = math.sqrt(2.0 * math.pi * spacing)

    def advance(previous, degree):
        latest, before = previous
        degree_value = degree.astype(jnp.float32)
        is_below = orders < degree_value
        denominator = jnp.where(is_below, degree_value * degree_value - orders * orders, 1.0)
        rise_coeff = jnp.where(is_below, jnp.sqrt((4.0 * degree_value * degree_value - 1.0) / denominator), 0.0)
        prior_degree = degree_value - 1.0
        below_prior = orders < prior_degree
        fall_coeff = jnp.where(below_prior, jnp.sqrt(jnp.maximum(prior_degree * prior_degree - orders * orders, 0.0) / jnp.maximum(4.0 * prior_degree * prior_degree - 1.0, 1.0)), 0.0)
        recurred = rise_coeff[:, None] * (cosine[None, :] * latest - fall_coeff[:, None] * before)
        current = jnp.where((orders == degree_value)[:, None], diagonal, jnp.where(is_below[:, None], recurred, 0.0))
        return ((current, latest), (current * cycle_weight).astype(jnp.bfloat16))
    start_rows = jnp.zeros((L, CYCLES), jnp.float32)
    _, values = lax.scan(advance, (start_rows, start_rows), jnp.arange(L, dtype=jnp.int32))
    device = jnp.arange(NBLOCKS, dtype=jnp.int32) // NBD
    group_ids = groups[device, blocks[:, 0]]
    order_index = MG * group_ids[:, None] + jnp.arange(MG, dtype=jnp.int32)[None, :]
    degree_index = LB * blocks[:, 1][:, None] + jnp.arange(LB, dtype=jnp.int32)[None, :]
    cycle_index = jnp.arange(CYCLES, dtype=jnp.int32)
    return values[degree_index[:, None, None, :], order_index[:, :, None, None], cycle_index[None, None, :, None]]


def steps_of(stream_key, extent, pieces, smallest, top_value):
    def one(position, blocks):
        steps = jax.random.uniform(jax.random.fold_in(jax.random.fold_in(stream_key, 6), position), (blocks,), jnp.float32, smallest / len(pieces), top_value / len(pieces))
        return jnp.repeat(jnp.exp(steps), extent[position] // blocks).reshape((-1,) + (1,) * (len(extent) - position - 1))

    gain = one(*pieces[0])
    for cut in pieces[1:]:
        gain = gain * one(*cut)
    return gain


def length_profile(count, total, reach, lean):
    portions = [(1 << 20) // math.isqrt(rank ** lean) + 1 for rank in range(2, count + 1)]
    rest, counts = total - reach - (count - 1), [1] * (count - 1)
    while rest > 0:
        free = [i for i in range(count - 1) if counts[i] < reach]
        whole, left = sum([portions[i] for i in free]), rest
        for i in free:
            addition = min(reach - counts[i], max(1, left * portions[i] // whole), rest)
            counts[i] = counts[i] + addition
            rest = rest - addition
    return np.array([reach] + counts)


def uneven(stream_key, count, total, reach, slope):
    if count == 2:
        one = jax.random.randint(stream_key, (), max(1, total - reach), min(reach, total - 1) + 1)
        return jnp.stack([one, total - one])
    lengths = jnp.asarray(length_profile(count, total, reach, slope), jnp.int32)
    twos = (count - 1) // 2
    giver, sink = lengths[1:1 + 2 * twos:2], lengths[2:2 + 2 * twos:2]
    slack = jnp.minimum(giver - 1, reach - sink)
    passed = jax.random.randint(jax.random.fold_in(stream_key, 1), (twos,), 0, 1 << 20) % (slack + 1)
    lengths = lengths.at[1:1 + 2 * twos:2].set(giver - passed).at[2:2 + 2 * twos:2].set(sink + passed)
    return lengths[jax.random.permutation(jax.random.fold_in(stream_key, 2), count)]


def noise(stream_key, shape, spread, most, split=(), held_as=jnp.bfloat16):
    entries = spread * jax.random.normal(stream_key, shape, jnp.float32)
    if split:
        entries = entries * steps_of(stream_key, shape, split, -0.22, 0.18)
    return jnp.clip(entries, -most, most).astype(held_as)


def setup_inputs(seed: int = 0) -> dict:
    key_list = jax.random.split(jax.random.key(seed), 8)
    return {
        "sky_maps": noise(key_list[0], (2, SIMS, CYCLES, NPHI), 5.0, 30.0, ((1, 4), (2, 32)), jnp.float32),
        "noise_weight": jnp.clip(jnp.exp(math.log(2.0) - 1.3862944 * jax.random.uniform(key_list[1], (CYCLES, NPHI), jnp.float32) ** steps_of(key_list[1], (CYCLES, NPHI), ((0, 32),), -0.2, 0.2)), 0.5, 2.0),
        "signal_inverse": jnp.clip(jnp.exp(jax.random.uniform(key_list[2], (L,), jnp.float32, math.log(0.1), math.log(3.0))), 0.1, 3.0),
        "legendre": draw_legendre(jax.random.fold_in(key_list[7], 71), 0),
        "m_groups": draw_m_groups(jax.random.fold_in(key_list[7], 71), 0),
        "block_list": draw_block_list(jax.random.fold_in(key_list[7], 71), 0),
        "band_of_ell": jnp.searchsorted(jnp.cumsum(uneven(key_list[6], BANDS, L, 2 * L // BANDS, 0)), jnp.arange(L), side="right").astype(jnp.int32),
    }


PRECISE = lax.Precision.HIGHEST

def cycle_scale_vector():
    orders = jnp.arange(L, dtype=jnp.int32)
    return jnp.where(orders == 0, math.sqrt(1.0 / NPHI), math.sqrt(2.0 / NPHI)).astype(jnp.float32)

def cycle_coeffs(pixel_field):
    spectrum = jnp.fft.rfft(pixel_field, axis=-1)[..., :L]
    scaling = cycle_scale_vector()
    return jnp.stack([jnp.real(spectrum) * scaling, jnp.imag(spectrum) * scaling], axis=-1)

def cycle_field(coeffs):
    orders = jnp.arange(L, dtype=jnp.int32)
    factor = jnp.where(orders == 0, float(NPHI), NPHI / 2.0).astype(jnp.float32) * cycle_scale_vector()
    spectrum = lax.complex(coeffs[..., 0] * factor, coeffs[..., 1] * factor)
    padding = NPHI // 2 + 1 - L
    spectrum = jnp.pad(spectrum, [(0, 0)] * (spectrum.ndim - 1) + [(0, padding)])
    return jnp.fft.irfft(spectrum, n=NPHI, axis=-1)

def reference(sky_maps, noise_weight, signal_inverse, legendre, m_groups, block_list, band_of_ell):
    block_total = legendre.shape[0]
    owner_device = jnp.arange(block_total, dtype=jnp.int32) // NBD
    group_ids = m_groups[owner_device, block_list[:, 0]]
    first_order = (MG * group_ids).astype(jnp.int32)
    degrees = LB * block_list[:, 1][:, None] + jnp.arange(LB, dtype=jnp.int32)[None, :]
    signal_blk = signal_inverse[degrees]
    precond = 1.0 / (2.0 + signal_blk)
    signal_b = signal_blk[:, None, None, None, None, :]
    precond_b = precond[:, None, None, None, None, :]

    def analysis(pixel_field):
        coeffs = lax.optimization_barrier(cycle_coeffs(pixel_field).astype(jnp.bfloat16))

        def project_block(inputs):
            legendre_block, first_index = inputs
            coeff_slice = lax.dynamic_slice_in_dim(coeffs, first_index, MG, axis=3).astype(jnp.float32)
            return jnp.einsum('sdrip,irl->isdpl', coeff_slice, legendre_block.astype(jnp.float32), precision=PRECISE)
        return lax.map(project_block, (legendre, first_order))

    def synthesis(harmonic_state):
        rounded = harmonic_state.astype(jnp.bfloat16)

        def accumulate(running, inputs):
            legendre_block, first_index, state_block = inputs
            block_term = jnp.einsum('isdpl,irl->sdrip', state_block.astype(jnp.float32), legendre_block.astype(jnp.float32), precision=PRECISE)
            previous = lax.dynamic_slice_in_dim(running, first_index, MG, axis=3)
            return (lax.dynamic_update_slice_in_dim(running, previous + block_term, first_index, axis=3), None)
        empty_coeffs = jnp.zeros((2, SIMS, CYCLES, L, 2), jnp.float32)
        running, _ = lax.scan(accumulate, empty_coeffs, (legendre, first_order, rounded))
        rounded_coeffs = lax.optimization_barrier(running.astype(jnp.bfloat16))
        return cycle_field(rounded_coeffs.astype(jnp.float32))
    harmonic_state = precond_b * analysis(noise_weight[None, None] * sky_maps)
    for sweep_index in range(ITERS - 1):
        residual = noise_weight[None, None] * (sky_maps - synthesis(harmonic_state))
        harmonic = analysis(residual)
        harmonic_state = harmonic_state + precond_b * (harmonic - signal_b * harmonic_state)
    products = harmonic_state[:, :, 0, :, 0, :] * harmonic_state[:, :, 1, :, 0, :] + harmonic_state[:, :, 0, :, 1, :] * harmonic_state[:, :, 1, :, 1, :]
    orders = first_order[:, None] + jnp.arange(MG, dtype=jnp.int32)[None, :]
    mode_weight = jnp.where(orders == 0, 1.0, 2.0).astype(jnp.float32)
    band_ids = band_of_ell[degrees]
    onehot = (band_ids[..., None] == jnp.arange(BANDS, dtype=jnp.int32)).astype(jnp.float32)
    band_raw = jnp.einsum('bisl,bi,blk->sk', products, mode_weight, onehot, precision=PRECISE)
    all_onehot = (band_of_ell[:, None] == jnp.arange(BANDS, dtype=jnp.int32)[None, :]).astype(jnp.float32)
    ell_weight = (2 * jnp.arange(L, dtype=jnp.int32) + 1).astype(jnp.float32)
    mode_count = jnp.dot(ell_weight, all_onehot, precision=PRECISE)
    band_proj = band_raw * (1.0 / jnp.sqrt(mode_count))[None, :]
    sim_mean = lax.optimization_barrier(jnp.mean(band_proj, axis=0))
    center = band_proj - sim_mean[None, :]
    fisher = jnp.dot(center.T, center, precision=PRECISE) / SIMS
    return (harmonic_state.astype(jnp.bfloat16), band_proj, fisher)
```

```python
import math

import jax
import jax.numpy as jnp
import numpy as np
from jax import lax
from jax.experimental import pallas as pl
from jax.experimental.pallas import tpu as pltpu
from jax.sharding import PartitionSpec as P

NPHI = 4096
BANDS = 32
ITERS = 4
BLK = 32
CYC = 2
VEC = 16
OUTER = 32
INNER = 128
MG = 16
SLOTS = 4
NQ = 4
F32 = jnp.float32
BF16 = jnp.bfloat16
PRECISE = lax.Precision.HIGHEST
STEP_BLOCKS = 2
NT = (((1,), (1,)), ((), ()))
TN = (((0,), (0,)), ((), ()))
NN = (((1,), (0,)), ((), ()))


def split(value):
    high = value.astype(BF16)
    return high, (value - high.astype(F32)).astype(BF16)


def dot(left, right, dims=NN):
    return lax.dot_general(left, right, dims, preferred_element_type=F32)


def dot3(left, right, dims=NN):
    return (
        dot(left[0], right[0], dims) + dot(left[0], right[1], dims) + dot(left[1], right[0], dims)
    )


def np_split(value):
    high = value.astype(np.float32).astype(jnp.bfloat16)
    low = (value - high.astype(np.float64)).astype(np.float32).astype(jnp.bfloat16)
    return np.stack([high, low])


def constant_tables():
    k = np.arange(OUTER).reshape(2, 1, MG)
    k_rows = np.broadcast_to(k, (2, CYC, MG)).reshape(-1)
    cycle_rows = np.broadcast_to(np.arange(CYC).reshape(1, CYC, 1), (2, CYC, MG)).reshape(-1)
    a_cols = np.repeat(np.arange(OUTER), CYC)
    cycle_cols = np.tile(np.arange(CYC), OUTER)
    angle = 2.0 * np.pi * (k_rows[:, None] * a_cols[None, :] % OUTER) / OUTER
    same = cycle_rows[:, None] == cycle_cols[None, :]
    outer = np.concatenate([np.cos(angle) * same, -np.sin(angle) * same], axis=0)
    twist = 2.0 * np.pi * (k_rows[:, None] * np.arange(INNER)[None, :]) / NPHI
    twist_table = np.stack([np.cos(twist), np.sin(twist)]).astype(np.float32)
    q = np.arange(BLK * CYC)
    cycle_of = 2 * (q % BLK) + q // BLK
    place = np.zeros((NQ, BLK * CYC, NQ * BLK * CYC), np.float32)
    for i in range(NQ):
        place[i, q, i * BLK * CYC + cycle_of] = 1.0
    spread = np.zeros((BLK * CYC, 2 * BLK * CYC), np.float32)
    spread[q, cycle_of] = 1.0
    spread[q, BLK * CYC + cycle_of] = 1.0
    return (
        np_split(outer),
        np_split(outer.T),
        twist_table,
        place.astype(jnp.bfloat16),
        spread.astype(jnp.bfloat16),
    )


def column(half, j, p, h):
    return ((half * 2 + j) * 2 + p) * 2 + h


def forward_part(field_of, outer_ref, twist_ref, inner_ref, zero_ref, out_ref, turned, staged):
    outer = (outer_ref[0], outer_ref[1])
    cos_twist, sin_twist = twist_ref[0], twist_ref[1]
    for v in range(VEC):
        first = dot3(outer, split(field_of(v)))
        real, imag = first[:64], first[64:]
        turned_real = split(real * cos_twist + imag * sin_twist)
        turned_imag = split(imag * cos_twist - real * sin_twist)
        for half in range(2):
            for cycle in range(CYC):
                rows = slice((half * 2 + cycle) * MG, (half * 2 + cycle + 1) * MG)
                at = cycle * 256 + v * MG
                for part in range(2):
                    turned[part, half, at : at + MG, 0:128] = turned_real[part][rows]
                    turned[part, half, at : at + MG, 128:256] = turned_imag[part][rows]
    for half in range(2):
        inner = (inner_ref[0, half], inner_ref[1, half])
        coeffs = dot3(inner, (turned[0, half], turned[1, half]), NT)
        if half == 0:
            coeffs = coeffs * zero_scale(zero_ref)
        for j in range(2):
            for p in range(2):
                for h in range(2):
                    for cycle in range(CYC):
                        row = column(half, j, p, h) * 2 + cycle
                        lanes = cycle * 256 + h * 128
                        staged[:, row, :] = coeffs[
                            (j * 2 + p) * 32 : (j * 2 + p + 1) * 32, lanes : lanes + 128
                        ]
    out_ref[...] = staged[...].astype(BF16)


def zero_scale(zero_ref):
    lane = lax.broadcasted_iota(jnp.int32, (128, 512), 1)
    own = jnp.broadcast_to(zero_ref[...], (128, 512))
    return jnp.where(jnp.logical_and(lane % MG == 0, own > 0.0), math.sqrt(0.5), 1.0)


def first_rows_kernel(
    sky_ref, noise_ref, outer_ref, twist_ref, inner_ref, zero_ref, out_ref, turned, staged
):
    noise = noise_ref[...]
    forward_part(
        lambda v: noise * sky_ref[v],
        outer_ref, twist_ref, inner_ref, zero_ref, out_ref, turned, staged,
    )


def rows_kernel(
    sky_ref, noise_ref, outer_ref, outer_t_ref, twist_ref, inner_ref, zero_ref, coeff_ref,
    out_ref, turned, staged, spectrum,
):
    staged[...] = coeff_ref[...].astype(F32)
    for half in range(2):
        rows = []
        for j in range(2):
            for p in range(2):
                rows.append(
                    jnp.concatenate(
                        [
                            staged[:, column(half, j, p, h) * 2 + cycle, :]
                            for cycle in range(CYC)
                            for h in range(2)
                        ],
                        axis=1,
                    )
                )
        coeffs = jnp.concatenate(rows, axis=0)
        if half == 0:
            coeffs = coeffs * zero_scale(zero_ref)
        coeffs = coeffs.astype(BF16)
        inner = dot(coeffs, inner_ref[0, half], TN) + dot(coeffs, inner_ref[1, half], TN)
        shaped = inner.reshape(CYC * VEC, MG, 256)
        real, imag = shaped[:, :, :128], shaped[:, :, 128:]
        base = half * CYC * MG
        cos_twist = twist_ref[0, base : base + MG][None]
        sin_twist = twist_ref[1, base : base + MG][None]
        turned_real = split(real * cos_twist - imag * sin_twist)
        turned_imag = split(real * sin_twist + imag * cos_twist)
        for part in range(2):
            for cycle in range(CYC):
                at = (half * CYC + cycle) * MG
                spectrum[part, :, at : at + MG] = turned_real[part][cycle * VEC : (cycle + 1) * VEC]
                spectrum[part, :, 64 + at : 64 + at + MG] = turned_imag[part][
                    cycle * VEC : (cycle + 1) * VEC
                ]
    noise = noise_ref[...]
    outer_t = (outer_t_ref[0], outer_t_ref[1])

    def field_of(v):
        pixels = dot3(outer_t, (spectrum[0, v], spectrum[1, v]))
        return noise * (sky_ref[v] - pixels)

    forward_part(field_of, outer_ref, twist_ref, inner_ref, zero_ref, out_ref, turned, staged)


def modes_kernel(first, last, *refs):
    slot_ref, degree_ref, zero_ref = refs[:3]
    refs = refs[3:]
    coeff_ref, legendre_ref, signal_ref, place_ref, spread_ref = refs[:5]
    refs = refs[5:]
    if not first:
        state_ref, refs = refs[0], refs[1:]
    if last:
        band_ref, state_out, band_out, staged, ordered, packed, products = refs
    else:
        state_out, out_ref, staged, ordered, packed, sums = refs
    step = pl.program_id(0)

    @pl.when(step == 0)
    def _():
        staged[...] = coeff_ref[...].astype(F32)
        for c in range(16):
            slot, p, h = c // 4, (c // 2) % 2, c % 2
            pair = jnp.concatenate([staged[:, 2 * c, :], staged[:, 2 * c + 1, :]], axis=0)
            turned = pair.T
            for v in range(8):
                at = ((slot * VEC + h * 8 + v) * 2 + p) * MG
                ordered[at : at + MG, 0:64] = turned[v * MG : (v + 1) * MG]
        for i4 in range(NQ):
            rows = jnp.concatenate(
                [
                    ordered[pl.ds(slot * 512 + iq * 4 + i4, 32, stride=MG), 0:64]
                    for slot in range(SLOTS)
                    for iq in range(NQ)
                ],
                axis=0,
            )
            spreaded = dot(rows.astype(BF16), place_ref[i4]).astype(BF16)
            packed[:, i4 * 32 : (i4 + 1) * 32, :] = spreaded.reshape(16, 32, 256)
        if last:
            products[...] = jnp.zeros_like(products)
        else:
            sums[...] = jnp.zeros_like(sums)

    blanks = jnp.zeros((32, 128), BF16)
    for k in range(STEP_BLOCKS):
        block = step * STEP_BLOCKS + k
        slot = slot_ref[block]
        degree = degree_ref[block]
        precond = 1.0 / (2.0 + signal_ref[pl.ds(degree, 1), :])
        total = jnp.zeros((32, 128), F32)
        for iq in range(NQ):
            table = [legendre_ref[k, iq * 4 + i4] for i4 in range(NQ)]
            harmonic = dot(packed[slot * NQ + iq], jnp.concatenate(table, axis=0))
            if first:
                state = precond * harmonic
            else:
                before = state_ref[k, iq * 128 : (iq + 1) * 128].astype(F32)
                state = precond * (2.0 * before + harmonic)
            rounded = state.astype(BF16)
            state_out[k, iq * 128 : (iq + 1) * 128] = rounded
            if last:
                for i4 in range(NQ):
                    row = i4 * 32
                    one = state[row : row + 16] * state[row + 16 : row + 32]
                    if iq == 0 and i4 == 0:
                        weight = jnp.where(zero_ref[block] > 0, 0.5, 1.0)
                        one = one * weight
                    total = total + jnp.concatenate([one, jnp.zeros_like(one)], axis=0)
            else:
                left = jnp.concatenate(
                    [
                        jnp.concatenate(
                            [rounded[i4 * 32 : (i4 + 1) * 32], blanks]
                            if i4 % 2 == 0
                            else [blanks, rounded[i4 * 32 : (i4 + 1) * 32]],
                            axis=1,
                        )
                        for i4 in range(NQ)
                    ],
                    axis=0,
                )
                right = jnp.concatenate(
                    [
                        jnp.concatenate([table[0], table[1]], axis=1),
                        jnp.concatenate([table[2], table[3]], axis=1),
                    ],
                    axis=0,
                )
                sums[slot * NQ + iq] += dot(left, right, NT)
        if last:
            products[degree] += 2.0 * total[:16]

    @pl.when(step == pl.num_programs(0) - 1)
    def _():
        if last:
            raw = jnp.zeros((VEC, BANDS), F32)
            counts = jnp.zeros((VEC, BANDS), F32)
            bins = lax.broadcasted_iota(jnp.int32, (BANDS, 128), 0)
            lane = lax.broadcasted_iota(jnp.int32, (VEC, 128), 1)
            for e in range(16):
                member = (jnp.broadcast_to(band_ref[e : e + 1, :], (BANDS, 128)) == bins).astype(F32)
                raw = raw + lax.dot_general(
                    products[e], member, NT, precision=PRECISE, preferred_element_type=F32
                )
                weight = (2 * (e * 128 + lane) + 1).astype(F32)
                counts = counts + lax.dot_general(
                    weight, member, NT, precision=PRECISE, preferred_element_type=F32
                )
            band_out[...] = raw * (1.0 / jnp.sqrt(counts))
        else:
            lane = lax.broadcasted_iota(jnp.int32, (128, 128), 1)
            order = lax.broadcasted_iota(jnp.int32, (128, 128), 0) % MG
            keep = (order % 4) // 2 == lane // 64
            for slot in range(SLOTS):
                for i in range(MG):
                    ordered[pl.ds(slot * 512 + i, 32, stride=MG), :] = sums[
                        slot * NQ + i // 4, (i % 4) * 32 : (i % 4 + 1) * 32, :
                    ]
            for c in range(16):
                slot, p, h = c // 4, (c // 2) % 2, c % 2
                rows = []
                for v in range(8):
                    at = ((slot * VEC + h * 8 + v) * 2 + p) * MG
                    rows.append(ordered[at : at + MG, :])
                whole = jnp.where(keep, jnp.concatenate(rows, axis=0), 0.0).astype(BF16)
                turned = dot(spread_ref[...], whole, NT)
                staged[:, 2 * c, :] = turned[:32]
                staged[:, 2 * c + 1, :] = turned[32:]
            out_ref[...] = staged[...].astype(BF16)


def params(megabytes, **more):
    return pltpu.CompilerParams(vmem_limit_bytes=megabytes << 20, **more)


def row_transforms(sky, noise, outer, outer_t, twist, inner, zero_rows, coeffs):
    result = jax.ShapeDtypeStruct((BLK, 32, 128), BF16)
    scratch = [
        pltpu.VMEM((2, 2, 512, 256), BF16),
        pltpu.VMEM((BLK, 32, 128), F32),
    ]
    if coeffs is None:
        return pl.pallas_call(
            first_rows_kernel,
            out_shape=result,
            scratch_shapes=scratch,
            compiler_params=params(32),
            name="first_rows",
        )(sky, noise, outer, twist, inner, zero_rows)
    return pl.pallas_call(
        rows_kernel,
        out_shape=result,
        scratch_shapes=scratch + [pltpu.VMEM((2, VEC, 128, 128), BF16)],
        compiler_params=params(32),
        name="rows",
    )(sky, noise, outer, outer_t, twist, inner, zero_rows, coeffs)


def mode_step(first, last, scalars, coeffs, legendre, signal, place, spread, state, bands):
    block_count = legendre.shape[0]
    assert block_count % STEP_BLOCKS == 0
    grid = (block_count // STEP_BLOCKS,)
    state_spec = pl.BlockSpec((STEP_BLOCKS, 512, 128), lambda g, *_: (g, 0, 0))

    def whole(shape):
        return pl.BlockSpec(shape, lambda g, *_: (0,) * len(shape))

    operands = [coeffs, legendre, signal, place, spread]
    specs = [
        whole((BLK, 32, 128)),
        pl.BlockSpec((STEP_BLOCKS, MG, 64, 128), lambda g, *_: (g, 0, 0, 0)),
        whole((16, 128)),
        whole((NQ, 64, 256)),
        whole((64, 128)),
    ]
    if not first:
        operands.append(state)
        specs.append(state_spec)
    out_shapes = [jax.ShapeDtypeStruct((block_count, 512, 128), BF16)]
    out_specs = [state_spec]
    scratch = [
        pltpu.VMEM((BLK, 32, 128), F32),
        pltpu.VMEM((SLOTS * 512, 128), F32),
        pltpu.VMEM((SLOTS * NQ, 128, 256), BF16),
    ]
    if last:
        operands.append(bands)
        specs.append(whole((16, 128)))
        out_shapes.append(jax.ShapeDtypeStruct((VEC, BANDS), F32))
        out_specs.append(whole((VEC, BANDS)))
        scratch.append(pltpu.VMEM((16, VEC, 128), F32))
    else:
        out_shapes.append(jax.ShapeDtypeStruct((BLK, 32, 128), BF16))
        out_specs.append(whole((BLK, 32, 128)))
        scratch.append(pltpu.VMEM((SLOTS * NQ, 128, 128), F32))

    def body(*refs):
        modes_kernel(first, last, *refs)

    return pl.pallas_call(
        body,
        out_shape=out_shapes,
        grid_spec=pltpu.PrefetchScalarGridSpec(
            num_scalar_prefetch=3,
            grid=grid,
            in_specs=specs,
            out_specs=out_specs,
            scratch_shapes=scratch,
        ),
        compiler_params=params(32, dimension_semantics=("arbitrary",)),
        name="modes_last" if last else "modes_first" if first else "modes",
    )(*scalars, *operands)


def exchange(rows):
    return lax.all_to_all(rows, "blk", 0, 0, tiled=True)


def shards(sky_maps, noise_weight, signal_inverse, legendre, m_groups, block_list, band_of_ell):
    blk_index = lax.axis_index("blk")
    set_count, sim_local, cycle_local, cycle_pixels = sky_maps.shape
    block_count = legendre.shape[0]
    outer, outer_t, twist, place, spread = [jnp.asarray(t) for t in constant_tables()]
    sky = sky_maps.reshape(set_count, sim_local, cycle_local, OUTER, INNER)
    sky = sky.transpose(0, 1, 3, 2, 4).reshape(VEC, OUTER * CYC, INNER)
    noise = noise_weight.reshape(CYC, OUTER, INNER).transpose(1, 0, 2).reshape(OUTER * CYC, INNER)
    half_of = m_groups % 2
    upper_of = m_groups // 2
    earlier = jnp.tril(jnp.ones((SLOTS, SLOTS), jnp.int32), -1)
    rank = jnp.sum(
        (half_of[:, :, None] == half_of[:, None, :]).astype(jnp.int32) * earlier[None], axis=2
    )
    new_slot = 2 * half_of + rank
    chosen = new_slot[:, :, None] == jnp.arange(SLOTS, dtype=jnp.int32)[None, None, :]
    upper = jnp.sum(jnp.where(chosen, upper_of[:, :, None], 0), axis=1)
    upper_rows = upper.T.reshape(2, 2, 1, BLK, 1)
    angle = (2.0 * math.pi / 128.0) * (
        upper_rows * jnp.arange(128, dtype=jnp.int32) % 128
    ).astype(F32)
    cos_inner = math.sqrt(2.0 / NPHI) * jnp.cos(angle)
    sin_inner = math.sqrt(2.0 / NPHI) * jnp.sin(angle)
    inner = jnp.concatenate(
        [
            jnp.concatenate([cos_inner, sin_inner], axis=-1),
            jnp.concatenate([-sin_inner, cos_inner], axis=-1),
        ],
        axis=2,
    ).reshape(2, 128, 256)
    inner = jnp.stack(split(inner))
    zero_rows = jnp.broadcast_to(
        (upper[:, :2].T == 0).astype(F32)[:, None, :], (2, 2, BLK)
    ).reshape(128, 1)
    slot_ids = block_list[:, 0]
    degree_ids = block_list[:, 1]
    slot_hot = slot_ids[:, None] == jnp.arange(SLOTS, dtype=jnp.int32)[None, :]
    own_slot = lax.dynamic_index_in_dim(new_slot, blk_index, 0, keepdims=False)
    own_groups = lax.dynamic_index_in_dim(m_groups, blk_index, 0, keepdims=False)
    block_slot = jnp.sum(jnp.where(slot_hot, own_slot[None, :], 0), axis=1)
    block_zero = jnp.sum(
        jnp.where(slot_hot, (own_groups == 0).astype(jnp.int32)[None, :], 0), axis=1
    )
    scalars = (block_slot, degree_ids, block_zero)
    signal = signal_inverse.reshape(16, 128)
    bands = band_of_ell.reshape(16, 128)

    state = None
    rows = row_transforms(sky, noise, outer, outer_t, twist, inner, zero_rows, None)
    for sweep in range(ITERS):
        received = exchange(rows)
        last = sweep == ITERS - 1
        state, result = mode_step(
            sweep == 0, last, scalars, received, legendre, signal, place, spread, state, bands
        )
        if not last:
            rows = row_transforms(
                sky, noise, outer, outer_t, twist, inner, zero_rows, exchange(result)
            )
    partial = result.reshape(sim_local, 2, BANDS).sum(axis=1)
    copies = jnp.broadcast_to(partial[None], (BLK, sim_local, BANDS))
    band_proj = jnp.sum(lax.all_to_all(copies, "blk", 0, 0, tiled=True), axis=0)
    all_proj = lax.all_gather(band_proj, "sim", axis=0, tiled=True)
    sim_mean = jnp.mean(all_proj, axis=0)
    center = all_proj - sim_mean[None, :]
    fisher = jnp.dot(center.T, center, precision=PRECISE) / all_proj.shape[0]
    filtered = state.reshape(block_count, MG, set_count, sim_local, 2, 128)
    return (filtered, band_proj, fisher)


def solution(mesh):
    return jax.shard_map(
        shards,
        mesh=mesh,
        in_specs=(
            P(None, "sim", "blk", None),
            P("blk", None),
            P(),
            P("blk", None, None, None),
            P(),
            P("blk", None),
            P(),
        ),
        out_specs=(P("blk", None, None, "sim", None, None), P("sim", None), P()),
        check_vma=False,
    )
```

```python
import math

import jax
import jax.numpy as jnp
import numpy as np
from jax import lax
from jax.experimental import pallas as pl
from jax.experimental.pallas import tpu as pltpu
from jax.sharding import PartitionSpec as P

NPHI = 4096
BANDS = 32
ITERS = 4
BLK = 32
CYC = 2
VEC = 16
OUTER = 32
INNER = 128
MG = 16
SLOTS = 4
PAIRS = 18
F32 = jnp.float32
BF16 = jnp.bfloat16
PRECISE = lax.Precision.HIGHEST
NT = (((1,), (1,)), ((), ()))
TN = (((0,), (0,)), ((), ()))
NN = (((1,), (0,)), ((), ()))


def split(value):
    high = value.astype(BF16)
    return high, (value - high.astype(F32)).astype(BF16)


def dot(left, right, dims=NN):
    return lax.dot_general(left, right, dims, preferred_element_type=F32)


def dot3(left, right, dims=NN):
    return (
        dot(left[0], right[0], dims) + dot(left[0], right[1], dims) + dot(left[1], right[0], dims)
    )


def np_split(value):
    high = value.astype(np.float32).astype(jnp.bfloat16)
    low = (value - high.astype(np.float64)).astype(np.float32).astype(jnp.bfloat16)
    return np.stack([high, low])


def constant_tables():
    k = np.arange(OUTER).reshape(2, 1, MG)
    k_rows = np.broadcast_to(k, (2, CYC, MG)).reshape(-1)
    cycle_rows = np.broadcast_to(np.arange(CYC).reshape(1, CYC, 1), (2, CYC, MG)).reshape(-1)
    a_cols = np.repeat(np.arange(OUTER), CYC)
    cycle_cols = np.tile(np.arange(CYC), OUTER)
    angle = 2.0 * np.pi * (k_rows[:, None] * a_cols[None, :] % OUTER) / OUTER
    same = cycle_rows[:, None] == cycle_cols[None, :]
    outer = np.concatenate([np.cos(angle) * same, -np.sin(angle) * same], axis=0)
    twist = 2.0 * np.pi * (k_rows[:, None] * np.arange(INNER)[None, :]) / NPHI
    twist_table = np.stack([np.cos(twist), np.sin(twist)]).astype(np.float32)
    return np_split(outer), np_split(outer.T), twist_table


def column(half, j, p, upper):
    return ((half * 2 + j) * 2 + p) * 2 + upper


def forward_part(field_of, outer_ref, twist_ref, inner_ref, zero_ref, out_ref, turned, staged):
    outer = (outer_ref[0], outer_ref[1])
    cos_twist, sin_twist = twist_ref[0], twist_ref[1]
    for v in range(VEC):
        first = dot3(outer, split(field_of(v)))
        real, imag = first[:64], first[64:]
        turned_real = real * cos_twist + imag * sin_twist
        turned_imag = imag * cos_twist - real * sin_twist
        for half in range(2):
            for cycle in range(CYC):
                at = (half * 2 + cycle) * MG
                rows = pl.ds(cycle * 256 + v, MG, stride=VEC)
                turned[half, 0, rows, :] = turned_real[at : at + MG]
                turned[half, 1, rows, :] = turned_imag[at : at + MG]
    for half in range(2):
        inner = (inner_ref[0, half], inner_ref[1, half])
        both = jnp.concatenate([turned[half, 0], turned[half, 1]], axis=1)
        coeffs = dot3(inner, split(both), NT)
        if half == 0:
            coeffs = coeffs * zero_scale(zero_ref)
        for j in range(2):
            for p in range(2):
                for upper in range(2):
                    for cycle in range(CYC):
                        row = column(half, j, p, upper) * 2 + cycle
                        lanes = cycle * 256 + upper * 128
                        staged[:, row, :] = coeffs[
                            (j * 2 + p) * 32 : (j * 2 + p + 1) * 32, lanes : lanes + 128
                        ]
    out_ref[...] = staged[...].astype(BF16)


def zero_scale(zero_ref):
    lane = lax.broadcasted_iota(jnp.int32, (128, 512), 1)
    own = jnp.broadcast_to(zero_ref[...], (128, 512))
    return jnp.where(jnp.logical_and(lane % 256 < VEC, own > 0.0), math.sqrt(0.5), 1.0)


def first_rows_kernel(
    sky_ref, noise_ref, outer_ref, twist_ref, inner_ref, zero_ref, out_ref, turned, staged
):
    noise = noise_ref[...]
    forward_part(
        lambda v: noise * sky_ref[v],
        outer_ref, twist_ref, inner_ref, zero_ref, out_ref, turned, staged,
    )


def rows_kernel(
    sky_ref, noise_ref, outer_ref, outer_t_ref, twist_ref, inner_ref, zero_ref, coeff_ref,
    out_ref, turned, staged,
):
    staged[...] = coeff_ref[...].astype(F32)
    for half in range(2):
        rows = []
        for j in range(2):
            for p in range(2):
                rows.append(
                    jnp.concatenate(
                        [
                            staged[:, column(half, j, p, upper) * 2 + cycle, :]
                            for cycle in range(CYC)
                            for upper in range(2)
                        ],
                        axis=1,
                    )
                )
        coeffs = jnp.concatenate(rows, axis=0)
        if half == 0:
            coeffs = coeffs * zero_scale(zero_ref)
        coeffs = coeffs.astype(BF16)
        inner = dot(coeffs, inner_ref[0, half], TN) + dot(coeffs, inner_ref[1, half], TN)
        for i in range(MG):
            at = half * CYC * MG + i
            cos_twist = jnp.broadcast_to(twist_ref[0, at : at + 1], (VEC, 128))
            sin_twist = jnp.broadcast_to(twist_ref[1, at : at + 1], (VEC, 128))
            for cycle in range(CYC):
                rows = slice(cycle * 256 + i * VEC, cycle * 256 + (i + 1) * VEC)
                real, imag = inner[rows, :128], inner[rows, 128:]
                turned[half, 0, rows, :] = real * cos_twist - imag * sin_twist
                turned[half, 1, rows, :] = real * sin_twist + imag * cos_twist
    noise = noise_ref[...]
    outer_t = (outer_t_ref[0], outer_t_ref[1])
    fields = []
    for v in range(VEC):
        spectrum = jnp.concatenate(
            [
                turned[half, part, pl.ds(cycle * 256 + v, MG, stride=VEC), :]
                for part in range(2)
                for half in range(2)
                for cycle in range(CYC)
            ],
            axis=0,
        )
        fields.append(noise * (sky_ref[v] - dot3(outer_t, split(spectrum))))
    forward_part(
        lambda v: fields[v],
        outer_ref, twist_ref, inner_ref, zero_ref, out_ref, turned, staged,
    )


def find_pairs(group_ref, block_ref, own_ref, order, pair_slot, pair_live, pair_zero, counter):
    own = own_ref[0]
    groups = [group_ref[own, s] for s in range(SLOTS)]
    base = jnp.int32(0)
    for s in range(SLOTS):
        half = groups[s] % 2
        rank = jnp.int32(0)
        for earlier in range(s):
            rank = rank + jnp.where(groups[earlier] % 2 == half, 1, 0)
        slot = 2 * half + rank
        is_zero = jnp.where(groups[s] == 0, 1, 0)
        count = 16 - groups[s] // 8
        pairs = (count + 1) // 2
        counter[s] = 2 * base

        def mark(pair, carry, slot=slot, is_zero=is_zero):
            pair_slot[pair] = slot
            pair_zero[pair] = is_zero
            pair_live[pair] = 1
            return carry

        lax.fori_loop(base, base + pairs, mark, 0)
        base = base + pairs

    def place(block, carry):
        slot = block_ref[block, 0]
        at = counter[slot]
        order[at] = block
        counter[slot] = at + 1
        return carry

    lax.fori_loop(0, 34, place, 0)
    for s in range(SLOTS):
        at = counter[s]

        @pl.when(at % 2 == 1)
        def _():
            order[at] = order[at - 1]
            pair_live[at // 2] = 0


def block_copy(legendre_ref, table, arrived, order, at):
    block = order[at]
    return pltpu.make_async_copy(legendre_ref.at[block], table.at[block], arrived.at[at])


def start_blocks(legendre_ref, table, arrived, order, pair_live):
    def start(pair, carry):
        block_copy(legendre_ref, table, arrived, order, 2 * pair).start()

        @pl.when(pair_live[pair] == 1)
        def _():
            block_copy(legendre_ref, table, arrived, order, 2 * pair + 1).start()

        return carry

    lax.fori_loop(0, PAIRS, start, 0)


def wait_blocks(legendre_ref, table, arrived, order, pair_live, pair):
    block_copy(legendre_ref, table, arrived, order, 2 * pair).wait()

    @pl.when(pair_live[pair] == 1)
    def _():
        block_copy(legendre_ref, table, arrived, order, 2 * pair + 1).wait()


def products_kernel(
    group_ref, block_ref, own_ref, legendre_ref, signal_ref, out_ref,
    table, sums, order, pair_slot, pair_live, pair_zero, counter, arrived,
):
    find_pairs(group_ref, block_ref, own_ref, order, pair_slot, pair_live, pair_zero, counter)
    start_blocks(legendre_ref, table, arrived, order, pair_live)
    sums[...] = jnp.zeros_like(sums)

    def pair_step(pair, carry):
        wait_blocks(legendre_ref, table, arrived, order, pair_live, pair)
        first, second = order[2 * pair], order[2 * pair + 1]
        live = pair_live[pair].astype(F32)
        precond_first = 1.0 / (2.0 + signal_ref[pl.ds(block_ref[first, 1], 1), :])
        precond_second = 1.0 / (2.0 + signal_ref[pl.ds(block_ref[second, 1], 1), :])
        precond = jnp.concatenate([precond_first, precond_second], axis=1)
        weight = jnp.concatenate([precond_first, precond_second * live], axis=1)
        weights = []
        for _ in range(ITERS - 1):
            weights.append(jnp.broadcast_to(weight, (64, 256)))
            weight = weight * (2.0 * precond)
        for i in range(MG):
            values = jnp.concatenate([table[first, i], table[second, i]], axis=1)
            wide = values.astype(F32)
            scaled = jnp.concatenate([(wide * w).astype(BF16) for w in weights], axis=0)
            sums[pair_slot[pair] * MG + i] += dot(values, scaled, NT)
        return carry

    lax.fori_loop(0, PAIRS, pair_step, 0)
    for at in range(SLOTS * MG):
        out_ref[at // 8, (at % 8) * 64 : (at % 8 + 1) * 64, :] = sums[at].astype(BF16)


def apply_kernel(count, *refs):
    coeff_ref, product_ref = refs[:2]
    earlier = refs[2 : 1 + count]
    kept_ref, out_ref, staged, ordered = refs[1 + count :]
    staged[...] = coeff_ref[...].astype(F32)
    for c in range(16):
        for cycle in range(CYC):
            ordered[c, pl.ds(cycle, BLK, stride=2), :] = staged[:, 2 * c + cycle, :]
    kept_ref[...] = ordered[...].astype(BF16)
    history = [kept_ref] + list(earlier)[::-1]
    lane = lax.broadcasted_iota(jnp.int32, (64, 256), 1) % 128 // VEC
    for slot in range(SLOTS):
        for upper in range(2):
            at = [(slot * 2 + p) * 2 + upper for p in range(2)]
            right = jnp.concatenate(
                [jnp.concatenate([ref[at[0]], ref[at[1]]], axis=1) for ref in history], axis=0
            )
            mixed = dot(product_ref[slot * 2 + upper, :, : 64 * count], right)
            result = mixed[:64]
            for i in range(1, 8):
                result = jnp.where(lane == i, mixed[i * 64 : (i + 1) * 64], result)
            ordered[at[0]] = result[:, :128]
            ordered[at[1]] = result[:, 128:]
    for c in range(16):
        for cycle in range(CYC):
            staged[:, 2 * c + cycle, :] = ordered[c, pl.ds(cycle, BLK, stride=2), :]
    out_ref[...] = staged[...].astype(BF16)


def last_kernel(
    group_ref, block_ref, own_ref, coeff_ref, kept0_ref, kept1_ref, kept2_ref, legendre_ref,
    signal_ref, band_ref, state_ref, band_out,
    table, staged, mixed, packed, products, outgoing,
    order, pair_slot, pair_live, pair_zero, counter, arrived, sent,
):
    find_pairs(group_ref, block_ref, own_ref, order, pair_slot, pair_live, pair_zero, counter)
    start_blocks(legendre_ref, table, arrived, order, pair_live)
    products[...] = jnp.zeros_like(products)
    staged[...] = coeff_ref[...].astype(F32)
    blank = jnp.zeros((64, 128), BF16)
    unit = (
        lax.broadcasted_iota(jnp.int32, (128, 128), 0)
        == lax.broadcasted_iota(jnp.int32, (128, 128), 1)
    ).astype(BF16)
    for slot in range(SLOTS):
        for upper in range(2):
            for sweep in range(ITERS):
                for p in range(2):
                    c = (slot * 2 + p) * 2 + upper
                    if sweep < ITERS - 1:
                        tile = (kept0_ref, kept1_ref, kept2_ref)[sweep][c]
                    else:
                        for cycle in range(CYC):
                            mixed[0, pl.ds(cycle, BLK, stride=2), :] = staged[:, 2 * c + cycle, :]
                        tile = mixed[0, 0:64, :].astype(BF16)
                    turned = dot(unit, jnp.concatenate([tile, blank], axis=0), NT)
                    for i in range(8):
                        rows = pl.ds(sweep * 32 + p, VEC, stride=2)
                        mixed[1 + i, rows, :] = turned[i * VEC : (i + 1) * VEC]
            for i in range(8):
                packed[slot * MG + upper * 8 + i] = mixed[1 + i, :, 0:64].astype(BF16)

    def out_copy(pair, which):
        slot = pair % 2
        return pltpu.make_async_copy(
            outgoing.at[slot, which],
            state_ref.at[order[2 * pair + which]],
            sent.at[slot, which],
        )

    def wait_out(pair):
        out_copy(pair, 0).wait()

        @pl.when(pair_live[pair] == 1)
        def _():
            out_copy(pair, 1).wait()

    def pair_step(pair, carry):
        wait_blocks(legendre_ref, table, arrived, order, pair_live, pair)

        @pl.when(pair >= 2)
        def _():
            wait_out(pair - 2)

        first, second = order[2 * pair], order[2 * pair + 1]
        degrees = (block_ref[first, 1], block_ref[second, 1])
        precond = jnp.concatenate(
            [1.0 / (2.0 + signal_ref[pl.ds(degree, 1), :]) for degree in degrees], axis=1
        )
        damp = 2.0 * precond
        total = jnp.zeros((VEC, 256), F32)
        for i in range(MG):
            values = jnp.concatenate([table[first, i], table[second, i]], axis=1)
            harmonic = dot(packed[pair_slot[pair] * MG + i], values)
            state = harmonic[0:32]
            for sweep in range(1, ITERS):
                state = harmonic[sweep * 32 : (sweep + 1) * 32] + damp * state
            state = precond * state
            rounded = state.astype(BF16)
            outgoing[pair % 2, 0, i * 32 : (i + 1) * 32, :] = rounded[:, :128]
            outgoing[pair % 2, 1, i * 32 : (i + 1) * 32, :] = rounded[:, 128:]
            one = state[:VEC] * state[VEC:]
            if i == 0:
                one = one * jnp.where(pair_zero[pair] > 0, 0.5, 1.0)
            total = total + one
        total = 2.0 * total
        products[degrees[0]] += total[:, :128]
        out_copy(pair, 0).start()

        @pl.when(pair_live[pair] == 1)
        def _():
            products[degrees[1]] += total[:, 128:]
            out_copy(pair, 1).start()

        return carry

    lax.fori_loop(0, PAIRS, pair_step, 0)
    raw = jnp.zeros((VEC, BANDS), F32)
    counts = jnp.zeros((VEC, BANDS), F32)
    bins = lax.broadcasted_iota(jnp.int32, (BANDS, 128), 0)
    lane = lax.broadcasted_iota(jnp.int32, (VEC, 128), 1)
    for e in range(16):
        member = (jnp.broadcast_to(band_ref[e : e + 1, :], (BANDS, 128)) == bins).astype(F32)
        raw = raw + lax.dot_general(
            products[e], member, NT, precision=PRECISE, preferred_element_type=F32
        )
        weight = (2 * (e * 128 + lane) + 1).astype(F32)
        counts = counts + lax.dot_general(
            weight, member, NT, precision=PRECISE, preferred_element_type=F32
        )
    band_out[...] = raw * (1.0 / jnp.sqrt(counts))
    wait_out(PAIRS - 2)
    wait_out(PAIRS - 1)


def params(megabytes, **more):
    return pltpu.CompilerParams(vmem_limit_bytes=megabytes << 20, **more)


SENT = jax.ShapeDtypeStruct((BLK, 32, 128), BF16)
KEPT = jax.ShapeDtypeStruct((16, 64, 128), BF16)
SMEM = pl.BlockSpec(memory_space=pltpu.SMEM)
VMEM = pl.BlockSpec(memory_space=pltpu.VMEM)
ANY = pl.BlockSpec(memory_space=pl.ANY)


def row_transforms(sky, noise, outer, outer_t, twist, inner, zero_rows, coeffs):
    scratch = [pltpu.VMEM((2, 2, 512, 128), F32), pltpu.VMEM((BLK, 32, 128), F32)]
    if coeffs is None:
        return pl.pallas_call(
            first_rows_kernel,
            out_shape=SENT,
            scratch_shapes=scratch,
            compiler_params=params(32),
            name="first_rows",
        )(sky, noise, outer, twist, inner, zero_rows)
    return pl.pallas_call(
        rows_kernel,
        out_shape=SENT,
        scratch_shapes=scratch,
        compiler_params=params(32),
        name="rows",
    )(sky, noise, outer, outer_t, twist, inner, zero_rows, coeffs)


def pair_scratch():
    return [
        pltpu.SMEM((2 * PAIRS,), jnp.int32),
        pltpu.SMEM((PAIRS,), jnp.int32),
        pltpu.SMEM((PAIRS,), jnp.int32),
        pltpu.SMEM((PAIRS,), jnp.int32),
        pltpu.SMEM((SLOTS,), jnp.int32),
        pltpu.SemaphoreType.DMA((2 * PAIRS,)),
    ]


def cycle_products(scalars, legendre, signal):
    return pl.pallas_call(
        products_kernel,
        out_shape=jax.ShapeDtypeStruct((8, 512, 192), BF16),
        in_specs=[SMEM, SMEM, SMEM, ANY, VMEM],
        scratch_shapes=[
            pltpu.VMEM(legendre.shape, BF16),
            pltpu.VMEM((SLOTS * MG, 64, 192), F32),
        ]
        + pair_scratch(),
        compiler_params=params(40),
        name="cycle_products",
    )(*scalars, legendre, signal)


def apply_products(coeffs, products, kept):
    count = len(kept) + 1

    def body(*refs):
        apply_kernel(count, *refs)

    return pl.pallas_call(
        body,
        out_shape=(KEPT, SENT),
        scratch_shapes=[pltpu.VMEM((BLK, 32, 128), F32), pltpu.VMEM((16, 64, 128), F32)],
        compiler_params=params(32),
        name="apply_products_" + str(count),
    )(coeffs, products, *kept)


def last_step(scalars, coeffs, kept, legendre, signal, bands):
    return pl.pallas_call(
        last_kernel,
        out_shape=(
            jax.ShapeDtypeStruct((legendre.shape[0], 512, 128), BF16),
            jax.ShapeDtypeStruct((VEC, BANDS), F32),
        ),
        in_specs=[SMEM] * 3 + [VMEM] * 4 + [ANY, VMEM, VMEM],
        out_specs=(ANY, VMEM),
        scratch_shapes=[
            pltpu.VMEM(legendre.shape, BF16),
            pltpu.VMEM((BLK, 32, 128), F32),
            pltpu.VMEM((9, 128, 128), F32),
            pltpu.VMEM((SLOTS * MG, 128, 64), BF16),
            pltpu.VMEM((16, VEC, 128), F32),
            pltpu.VMEM((2, 2, 512, 128), BF16),
        ]
        + pair_scratch()
        + [pltpu.SemaphoreType.DMA((2, 2))],
        compiler_params=params(40),
        name="last_modes",
    )(*scalars, coeffs, *kept, legendre, signal, bands)


def exchange(rows):
    return lax.all_to_all(rows, "blk", 0, 0, tiled=True)


def shards(sky_maps, noise_weight, signal_inverse, legendre, m_groups, block_list, band_of_ell):
    blk_index = lax.axis_index("blk")
    set_count, sim_local, cycle_local, cycle_pixels = sky_maps.shape
    block_count = legendre.shape[0]
    outer, outer_t, twist = [jnp.asarray(t) for t in constant_tables()]
    sky = sky_maps.reshape(set_count, sim_local, cycle_local, OUTER, INNER)
    sky = sky.transpose(0, 1, 3, 2, 4).reshape(VEC, OUTER * CYC, INNER)
    noise = noise_weight.reshape(CYC, OUTER, INNER).transpose(1, 0, 2).reshape(OUTER * CYC, INNER)
    half_of = m_groups % 2
    upper_of = m_groups // 2
    earlier = jnp.tril(jnp.ones((SLOTS, SLOTS), jnp.int32), -1)
    rank = jnp.sum(
        (half_of[:, :, None] == half_of[:, None, :]).astype(jnp.int32) * earlier[None], axis=2
    )
    new_slot = 2 * half_of + rank
    chosen = new_slot[:, :, None] == jnp.arange(SLOTS, dtype=jnp.int32)[None, None, :]
    upper = jnp.sum(jnp.where(chosen, upper_of[:, :, None], 0), axis=1)
    upper_rows = upper.T.reshape(2, 2, 1, BLK, 1)
    angle = (2.0 * math.pi / 128.0) * (
        upper_rows * jnp.arange(128, dtype=jnp.int32) % 128
    ).astype(F32)
    cos_inner = math.sqrt(2.0 / NPHI) * jnp.cos(angle)
    sin_inner = math.sqrt(2.0 / NPHI) * jnp.sin(angle)
    inner = jnp.concatenate(
        [
            jnp.concatenate([cos_inner, sin_inner], axis=-1),
            jnp.concatenate([-sin_inner, cos_inner], axis=-1),
        ],
        axis=2,
    ).reshape(2, 128, 256)
    inner = jnp.stack(split(inner))
    zero_rows = jnp.broadcast_to(
        (upper[:, :2].T == 0).astype(F32)[:, None, :], (2, 2, BLK)
    ).reshape(128, 1)
    scalars = (m_groups, block_list, blk_index.astype(jnp.int32).reshape(1))
    signal = signal_inverse.reshape(16, 128)
    bands = band_of_ell.reshape(16, 128)

    rows = row_transforms(sky, noise, outer, outer_t, twist, inner, zero_rows, None)
    products = cycle_products(scalars, legendre, signal)
    kept = []
    for sweep in range(ITERS - 1):
        coeffs, rows = apply_products(exchange(rows), products, kept)
        kept.append(coeffs)
        rows = row_transforms(
            sky, noise, outer, outer_t, twist, inner, zero_rows, exchange(rows)
        )
    state, result = last_step(scalars, exchange(rows), kept, legendre, signal, bands)
    partial = result.reshape(sim_local, 2, BANDS).sum(axis=1)
    devices = BLK * lax.axis_size("sim")
    copies = jnp.broadcast_to(partial[None], (devices, sim_local, BANDS))
    terms = lax.all_to_all(copies, ("blk", "sim"), 0, 0, tiled=True)
    all_proj = jnp.sum(terms.reshape(BLK, -1, BANDS), axis=0)
    band_proj = lax.dynamic_slice_in_dim(all_proj, lax.axis_index("sim") * sim_local, sim_local, 0)
    sim_mean = jnp.mean(all_proj, axis=0)
    center = all_proj - sim_mean[None, :]
    fisher = jnp.dot(center.T, center, precision=PRECISE) / all_proj.shape[0]
    filtered = state.reshape(block_count, MG, set_count, sim_local, 2, 128)
    return (filtered, band_proj, fisher)


def solution(mesh):
    return jax.shard_map(
        shards,
        mesh=mesh,
        in_specs=(
            P(None, "sim", "blk", None),
            P("blk", None),
            P(),
            P("blk", None, None, None),
            P(),
            P("blk", None),
            P(),
        ),
        out_specs=(P("blk", None, None, "sim", None, None), P("sim", None), P()),
        check_vma=False,
    )
```

```python
import math

import jax
import jax.numpy as jnp
import numpy as np
from jax import lax
from jax.experimental import pallas as pl
from jax.experimental.pallas import tpu as pltpu
from jax.sharding import PartitionSpec as P

NPHI = 4096
BANDS = 32
ITERS = 4
BLK = 32
CYC = 2
VEC = 16
OUTER = 32
INNER = 128
MG = 16
SLOTS = 4
PAIRS = 18
PAIR_GROUP = 3
GROUP = 6
F32 = jnp.float32
BF16 = jnp.bfloat16
PRECISE = lax.Precision.HIGHEST
NT = (((1,), (1,)), ((), ()))
TN = (((0,), (0,)), ((), ()))
NN = (((1,), (0,)), ((), ()))


def split(value):
    high = value.astype(BF16)
    return high, (value - high.astype(F32)).astype(BF16)


def dot(left, right, dims=NN):
    return lax.dot_general(left, right, dims, preferred_element_type=F32)


def dot3(left, right, dims=NN):
    return (
        dot(left[0], right[0], dims) + dot(left[0], right[1], dims) + dot(left[1], right[0], dims)
    )


def np_split(value):
    high = value.astype(np.float32).astype(jnp.bfloat16)
    low = (value - high.astype(np.float64)).astype(np.float32).astype(jnp.bfloat16)
    return np.stack([high, low])


def constant_tables():
    k = np.arange(OUTER).reshape(2, 1, MG)
    k_rows = np.broadcast_to(k, (2, CYC, MG)).reshape(-1)
    cycle_rows = np.broadcast_to(np.arange(CYC).reshape(1, CYC, 1), (2, CYC, MG)).reshape(-1)
    a_cols = np.repeat(np.arange(OUTER), CYC)
    cycle_cols = np.tile(np.arange(CYC), OUTER)
    angle = 2.0 * np.pi * (k_rows[:, None] * a_cols[None, :] % OUTER) / OUTER
    same = cycle_rows[:, None] == cycle_cols[None, :]
    outer = np.concatenate([np.cos(angle) * same, -np.sin(angle) * same], axis=0)
    twist = 2.0 * np.pi * (k_rows[:, None] * np.arange(INNER)[None, :]) / NPHI
    twist_table = np.stack([np.cos(twist), np.sin(twist)]).astype(np.float32)
    return np_split(outer), np_split(outer.T), twist_table


def column(half, j, p, upper):
    return ((half * 2 + j) * 2 + p) * 2 + upper


def forward_part(field_of, outer_ref, twist_ref, inner_ref, zero_ref, out_ref, turned, staged):
    outer = (outer_ref[0], outer_ref[1])
    cos_twist, sin_twist = twist_ref[0], twist_ref[1]
    for v in range(VEC):
        first = dot3(outer, split(field_of(v)))
        real, imag = first[:64], first[64:]
        turned_real = real * cos_twist + imag * sin_twist
        turned_imag = imag * cos_twist - real * sin_twist
        for half in range(2):
            for cycle in range(CYC):
                at = (half * 2 + cycle) * MG
                rows = pl.ds(cycle * 256 + v, MG, stride=VEC)
                turned[half, 0, rows, :] = turned_real[at : at + MG]
                turned[half, 1, rows, :] = turned_imag[at : at + MG]
    for half in range(2):
        inner = (inner_ref[0, half], inner_ref[1, half])
        both = jnp.concatenate([turned[half, 0], turned[half, 1]], axis=1)
        coeffs = dot3(inner, split(both), NT)
        if half == 0:
            coeffs = coeffs * zero_scale(zero_ref)
        for j in range(2):
            for p in range(2):
                for upper in range(2):
                    for cycle in range(CYC):
                        row = column(half, j, p, upper) * 2 + cycle
                        lanes = cycle * 256 + upper * 128
                        staged[:, row, :] = coeffs[
                            (j * 2 + p) * 32 : (j * 2 + p + 1) * 32, lanes : lanes + 128
                        ]
    out_ref[...] = staged[...].astype(BF16)


def zero_scale(zero_ref):
    lane = lax.broadcasted_iota(jnp.int32, (128, 512), 1)
    own = jnp.broadcast_to(zero_ref[...], (128, 512))
    return jnp.where(jnp.logical_and(lane % 256 < VEC, own > 0.0), math.sqrt(0.5), 1.0)


def first_rows_kernel(
    sky_ref, noise_ref, outer_ref, twist_ref, inner_ref, zero_ref, out_ref, turned, staged
):
    noise = noise_ref[...]
    forward_part(
        lambda v: noise * sky_ref[v],
        outer_ref, twist_ref, inner_ref, zero_ref, out_ref, turned, staged,
    )


def rows_kernel(
    sky_ref, noise_ref, outer_ref, outer_t_ref, twist_ref, inner_ref, zero_ref, coeff_ref,
    out_ref, turned, staged,
):
    staged[...] = coeff_ref[...].astype(F32)
    for half in range(2):
        rows = []
        for j in range(2):
            for p in range(2):
                rows.append(
                    jnp.concatenate(
                        [
                            staged[:, column(half, j, p, upper) * 2 + cycle, :]
                            for cycle in range(CYC)
                            for upper in range(2)
                        ],
                        axis=1,
                    )
                )
        coeffs = jnp.concatenate(rows, axis=0)
        if half == 0:
            coeffs = coeffs * zero_scale(zero_ref)
        coeffs = coeffs.astype(BF16)
        inner = dot(coeffs, inner_ref[0, half], TN) + dot(coeffs, inner_ref[1, half], TN)
        for i in range(MG):
            at = half * CYC * MG + i
            cos_twist = jnp.broadcast_to(twist_ref[0, at : at + 1], (VEC, 128))
            sin_twist = jnp.broadcast_to(twist_ref[1, at : at + 1], (VEC, 128))
            for cycle in range(CYC):
                rows = slice(cycle * 256 + i * VEC, cycle * 256 + (i + 1) * VEC)
                real, imag = inner[rows, :128], inner[rows, 128:]
                turned[half, 0, rows, :] = real * cos_twist - imag * sin_twist
                turned[half, 1, rows, :] = real * sin_twist + imag * cos_twist
    noise = noise_ref[...]
    outer_t = (outer_t_ref[0], outer_t_ref[1])
    fields = []
    for v in range(VEC):
        spectrum = jnp.concatenate(
            [
                turned[half, part, pl.ds(cycle * 256 + v, MG, stride=VEC), :]
                for part in range(2)
                for half in range(2)
                for cycle in range(CYC)
            ],
            axis=0,
        )
        fields.append(noise * (sky_ref[v] - dot3(outer_t, split(spectrum))))
    forward_part(
        lambda v: fields[v],
        outer_ref, twist_ref, inner_ref, zero_ref, out_ref, turned, staged,
    )


def own_slots(group_ref, own_ref):
    own = own_ref[0]
    groups = [group_ref[s, own] for s in range(SLOTS)]
    slots = []
    for s in range(SLOTS):
        half = groups[s] % 2
        rank = jnp.int32(0)
        for earlier in range(s):
            rank = rank + jnp.where(groups[earlier] % 2 == half, 1, 0)
        slots.append((2 * half + rank, groups[s]))
    return slots


def table_copy(legendre_ref, table, arrived, group, size):
    blocks = pl.ds(group * GROUP, size)
    return pltpu.make_async_copy(legendre_ref.at[blocks], table.at[blocks], arrived.at[group])


def by_groups(blocks, step):
    def body(group, carry):
        step(group, GROUP)
        return carry

    lax.fori_loop(0, blocks // GROUP, body, 0)
    if blocks % GROUP:
        step(blocks // GROUP, blocks % GROUP)


def mark_slots(group_ref, own_ref, new_slot, zero_slot):
    for s, (slot, group) in enumerate(own_slots(group_ref, own_ref)):
        new_slot[s] = slot
        zero_slot[s] = jnp.where(group == 0, 1, 0)


def find_pairs(group_ref, block_ref, own_ref, order, pair_slot, pair_live, counter):
    base = jnp.int32(0)
    for s, (slot, group) in enumerate(own_slots(group_ref, own_ref)):
        count = 16 - group // 8
        pairs = (count + 1) // 2
        counter[s] = 2 * base

        def mark(pair, carry, slot=slot):
            pair_slot[pair] = slot
            pair_live[pair] = 1
            return carry

        lax.fori_loop(base, base + pairs, mark, 0)
        base = base + pairs

    def place(block, carry):
        slot = block_ref[0, block]
        at = counter[slot]
        order[at] = block
        counter[slot] = at + 1
        return carry

    lax.fori_loop(0, block_ref.shape[1], place, 0)
    for s in range(SLOTS):
        at = counter[s]

        @pl.when(at % 2 == 1)
        def _():
            order[at] = order[at - 1]
            pair_live[at // 2] = 0


def products_kernel(
    power, group_ref, block_ref, own_ref, legendre_ref, signal_ref, out_ref,
    table, sums, order, pair_slot, pair_live, counter, arrived,
):
    find_pairs(group_ref, block_ref, own_ref, order, pair_slot, pair_live, counter)

    def place_copy(at):
        return pltpu.make_async_copy(legendre_ref.at[order[at]], table.at[at], arrived.at[at])

    def fetch(at, carry):
        place_copy(at).start()
        return carry

    lax.fori_loop(0, 2 * PAIRS, fetch, 0)
    sums[...] = jnp.zeros_like(sums)

    def pair_step(group, carry):
        pairs = [group * PAIR_GROUP + n for n in range(PAIR_GROUP)]
        for pair in pairs:
            place_copy(2 * pair).wait()
            place_copy(2 * pair + 1).wait()
        slots = [pair_slot[pair] for pair in pairs]
        lives = [pair_live[pair].astype(F32) for pair in pairs]
        degrees = [
            (block_ref[1, order[2 * pair]], block_ref[1, order[2 * pair + 1]]) for pair in pairs
        ]
        for pair, slot, live, (first, second) in zip(pairs, slots, lives, degrees):
            precond = [1.0 / (2.0 + signal_ref[pl.ds(degree, 1), :]) for degree in (first, second)]
            precond = jnp.concatenate(precond, axis=1)
            lane = lax.broadcasted_iota(jnp.int32, (1, 256), 1)
            weight = precond * jnp.where(lane < 128, 1.0, live)
            for _ in range(power):
                weight = weight * (2.0 * precond)
            weight = jnp.broadcast_to(weight, (64, 256))
            for i in range(MG):
                values = jnp.concatenate([table[2 * pair, i], table[2 * pair + 1, i]], axis=1)
                scaled = (values.astype(F32) * weight).astype(BF16)
                sums[slot * MG + i] += dot(values, scaled, NT)
        return carry

    lax.fori_loop(0, PAIRS // PAIR_GROUP, pair_step, 0)
    for at in range(SLOTS * MG):
        out_ref[at // 8, (at % 8) * 64 : (at % 8 + 1) * 64, :] = sums[at].astype(BF16)


def apply_kernel(count, *refs):
    coeff_ref = refs[0]
    product_refs = refs[1 : 1 + count]
    earlier = refs[1 + count : 2 * count]
    kept_ref, out_ref, staged, ordered = refs[2 * count :]
    staged[...] = coeff_ref[...].astype(F32)
    for c in range(16):
        for cycle in range(CYC):
            ordered[c, pl.ds(cycle, BLK, stride=2), :] = staged[:, 2 * c + cycle, :]
    kept_ref[...] = ordered[...].astype(BF16)
    history = [kept_ref] + list(earlier)[::-1]
    lane = lax.broadcasted_iota(jnp.int32, (64, 256), 1) % 128 // VEC
    for slot in range(SLOTS):
        for upper in range(2):
            at = [(slot * 2 + p) * 2 + upper for p in range(2)]
            mixed = None
            for product_ref, ref in zip(product_refs, history):
                right = jnp.concatenate([ref[at[0]], ref[at[1]]], axis=1)
                term = dot(product_ref[slot * 2 + upper], right)
                mixed = term if mixed is None else mixed + term
            result = mixed[:64]
            for i in range(1, 8):
                result = jnp.where(lane == i, mixed[i * 64 : (i + 1) * 64], result)
            ordered[at[0]] = result[:, :128]
            ordered[at[1]] = result[:, 128:]
    for c in range(16):
        for cycle in range(CYC):
            staged[:, 2 * c + cycle, :] = ordered[c, pl.ds(cycle, BLK, stride=2), :]
    out_ref[...] = staged[...].astype(BF16)


def last_kernel(
    group_ref, block_ref, own_ref, coeff_ref, kept0_ref, kept1_ref, kept2_ref, legendre_ref,
    signal_ref, band_ref, state_ref, band_out,
    table, staged, mixed, packed, products, outgoing, new_slot, zero_slot, arrived, sent,
):
    blocks = legendre_ref.shape[0]

    by_groups(blocks, lambda g, n: table_copy(legendre_ref, table, arrived, g, n).start())
    mark_slots(group_ref, own_ref, new_slot, zero_slot)
    products[...] = jnp.zeros_like(products)
    staged[...] = coeff_ref[...].astype(F32)
    blank = jnp.zeros((64, 128), BF16)
    unit = (
        lax.broadcasted_iota(jnp.int32, (128, 128), 0)
        == lax.broadcasted_iota(jnp.int32, (128, 128), 1)
    ).astype(BF16)
    for slot in range(SLOTS):
        for upper in range(2):
            for sweep in range(ITERS):
                for p in range(2):
                    c = (slot * 2 + p) * 2 + upper
                    if sweep < ITERS - 1:
                        tile = (kept0_ref, kept1_ref, kept2_ref)[sweep][c]
                    else:
                        for cycle in range(CYC):
                            mixed[0, pl.ds(cycle, BLK, stride=2), :] = staged[:, 2 * c + cycle, :]
                        tile = mixed[0, 0:64, :].astype(BF16)
                    turned = dot(unit, jnp.concatenate([tile, blank], axis=0), NT)
                    for i in range(8):
                        rows = pl.ds(sweep * 32 + p, VEC, stride=2)
                        mixed[1 + i, rows, :] = turned[i * VEC : (i + 1) * VEC]
            for i in range(8):
                packed[slot * MG + upper * 8 + i] = mixed[1 + i, :, 0:64].astype(BF16)

    def out_copy(group, size):
        some = pl.ds(group * GROUP, size)
        return pltpu.make_async_copy(outgoing.at[some], state_ref.at[some], sent.at[group])

    def step(group, size):
        table_copy(legendre_ref, table, arrived, group, size).wait()
        some = [group * GROUP + n for n in range(size)]
        slots = [new_slot[block_ref[0, block]] for block in some]
        halves = [
            jnp.where(zero_slot[block_ref[0, block]] > 0, 0.5, 1.0) for block in some
        ]
        degrees = [block_ref[1, block] for block in some]
        for block, slot, half, degree in zip(some, slots, halves, degrees):
            precond = jnp.broadcast_to(1.0 / (2.0 + signal_ref[pl.ds(degree, 1), :]), (32, 128))
            damp = 2.0 * precond
            total = jnp.zeros((VEC, 128), F32)
            for i in range(MG):
                harmonic = dot(packed[slot * MG + i], table[block, i])
                state = harmonic[0:32]
                for sweep in range(1, ITERS):
                    state = harmonic[sweep * 32 : (sweep + 1) * 32] + damp * state
                state = precond * state
                outgoing[block, i * 32 : (i + 1) * 32, :] = state.astype(BF16)
                one = state[:VEC] * state[VEC:]
                if i == 0:
                    one = one * half
                total = total + one
            products[degree] += 2.0 * total
        out_copy(group, size).start()

    by_groups(blocks, step)
    raw = jnp.zeros((VEC, BANDS), F32)
    counts = jnp.zeros((VEC, BANDS), F32)
    bins = lax.broadcasted_iota(jnp.int32, (BANDS, 128), 0)
    lane = lax.broadcasted_iota(jnp.int32, (VEC, 128), 1)
    for e in range(16):
        member = (jnp.broadcast_to(band_ref[e : e + 1, :], (BANDS, 128)) == bins).astype(F32)
        raw = raw + lax.dot_general(
            products[e], member, NT, precision=PRECISE, preferred_element_type=F32
        )
        weight = (2 * (e * 128 + lane) + 1).astype(F32)
        counts = counts + lax.dot_general(
            weight, member, NT, precision=PRECISE, preferred_element_type=F32
        )
    band_out[...] = raw * (1.0 / jnp.sqrt(counts))

    by_groups(blocks, lambda g, n: out_copy(g, n).wait())


def params(megabytes, **more):
    return pltpu.CompilerParams(vmem_limit_bytes=megabytes << 20, **more)


SENT = jax.ShapeDtypeStruct((BLK, 32, 128), BF16)
KEPT = jax.ShapeDtypeStruct((16, 64, 128), BF16)
SMEM = pl.BlockSpec(memory_space=pltpu.SMEM)
VMEM = pl.BlockSpec(memory_space=pltpu.VMEM)
ANY = pl.BlockSpec(memory_space=pl.ANY)


def row_transforms(sky, noise, outer, outer_t, twist, inner, zero_rows, coeffs):
    scratch = [pltpu.VMEM((2, 2, 512, 128), F32), pltpu.VMEM((BLK, 32, 128), F32)]
    if coeffs is None:
        return pl.pallas_call(
            first_rows_kernel,
            out_shape=SENT,
            scratch_shapes=scratch,
            compiler_params=params(32),
            name="first_rows",
        )(sky, noise, outer, twist, inner, zero_rows)
    return pl.pallas_call(
        rows_kernel,
        out_shape=SENT,
        scratch_shapes=scratch,
        compiler_params=params(32),
        name="rows",
    )(sky, noise, outer, outer_t, twist, inner, zero_rows, coeffs)


def cycle_products(power, scalars, legendre, signal):
    def body(*refs):
        products_kernel(power, *refs)

    return pl.pallas_call(
        body,
        out_shape=jax.ShapeDtypeStruct((8, 512, 64), BF16),
        in_specs=[SMEM, SMEM, SMEM, ANY, VMEM],
        scratch_shapes=[
            pltpu.VMEM((2 * PAIRS,) + legendre.shape[1:], BF16),
            pltpu.VMEM((SLOTS * MG, 64, 64), F32),
            pltpu.SMEM((2 * PAIRS,), jnp.int32),
            pltpu.SMEM((PAIRS,), jnp.int32),
            pltpu.SMEM((PAIRS,), jnp.int32),
            pltpu.SMEM((SLOTS,), jnp.int32),
            pltpu.SemaphoreType.DMA((2 * PAIRS,)),
        ],
        compiler_params=params(52),
        name="cycle_products_" + str(power),
    )(*scalars, legendre, signal)


def apply_products(coeffs, products, kept):
    count = len(products)

    def body(*refs):
        apply_kernel(count, *refs)

    return pl.pallas_call(
        body,
        out_shape=(KEPT, SENT),
        scratch_shapes=[pltpu.VMEM((BLK, 32, 128), F32), pltpu.VMEM((16, 64, 128), F32)],
        compiler_params=params(32),
        name="apply_products_" + str(count),
    )(coeffs, *products, *kept)


def last_step(scalars, coeffs, kept, legendre, signal, bands):
    return pl.pallas_call(
        last_kernel,
        out_shape=(
            jax.ShapeDtypeStruct((legendre.shape[0], 512, 128), BF16),
            jax.ShapeDtypeStruct((VEC, BANDS), F32),
        ),
        in_specs=[SMEM] * 3 + [VMEM] * 4 + [ANY, VMEM, VMEM],
        out_specs=(ANY, VMEM),
        scratch_shapes=[
            pltpu.VMEM(legendre.shape, BF16),
            pltpu.VMEM((BLK, 32, 128), F32),
            pltpu.VMEM((9, 128, 128), F32),
            pltpu.VMEM((SLOTS * MG, 128, 64), BF16),
            pltpu.VMEM((16, VEC, 128), F32),
            pltpu.VMEM((legendre.shape[0], 512, 128), BF16),
        ]
        + [
            pltpu.SMEM((SLOTS,), jnp.int32),
            pltpu.SMEM((SLOTS,), jnp.int32),
            pltpu.SemaphoreType.DMA((-(-legendre.shape[0] // GROUP),)),
            pltpu.SemaphoreType.DMA((-(-legendre.shape[0] // GROUP),)),
        ],
        compiler_params=params(52),
        name="last_modes",
    )(*scalars, coeffs, *kept, legendre, signal, bands)


def exchange(rows):
    return lax.all_to_all(rows, "blk", 0, 0, tiled=True)


def shards(sky_maps, noise_weight, signal_inverse, legendre, m_groups, block_list, band_of_ell):
    blk_index = lax.axis_index("blk")
    set_count, sim_local, cycle_local, cycle_pixels = sky_maps.shape
    block_count = legendre.shape[0]
    outer, outer_t, twist = [jnp.asarray(t) for t in constant_tables()]
    sky = sky_maps.reshape(set_count, sim_local, cycle_local, OUTER, INNER)
    sky = sky.transpose(0, 1, 3, 2, 4).reshape(VEC, OUTER * CYC, INNER)
    noise = noise_weight.reshape(CYC, OUTER, INNER).transpose(1, 0, 2).reshape(OUTER * CYC, INNER)
    half_of = m_groups % 2
    upper_of = m_groups // 2
    earlier = jnp.tril(jnp.ones((SLOTS, SLOTS), jnp.int32), -1)
    rank = jnp.sum(
        (half_of[:, :, None] == half_of[:, None, :]).astype(jnp.int32) * earlier[None], axis=2
    )
    new_slot = 2 * half_of + rank
    chosen = new_slot[:, :, None] == jnp.arange(SLOTS, dtype=jnp.int32)[None, None, :]
    upper = jnp.sum(jnp.where(chosen, upper_of[:, :, None], 0), axis=1)
    upper_rows = upper.T.reshape(2, 2, 1, BLK, 1)
    angle = (2.0 * math.pi / 128.0) * (
        upper_rows * jnp.arange(128, dtype=jnp.int32) % 128
    ).astype(F32)
    cos_inner = math.sqrt(2.0 / NPHI) * jnp.cos(angle)
    sin_inner = math.sqrt(2.0 / NPHI) * jnp.sin(angle)
    inner = jnp.concatenate(
        [
            jnp.concatenate([cos_inner, sin_inner], axis=-1),
            jnp.concatenate([-sin_inner, cos_inner], axis=-1),
        ],
        axis=2,
    ).reshape(2, 128, 256)
    inner = jnp.stack(split(inner))
    zero_rows = jnp.broadcast_to(
        (upper[:, :2].T == 0).astype(F32)[:, None, :], (2, 2, BLK)
    ).reshape(128, 1)
    scalars = (m_groups.T, block_list.T, blk_index.astype(jnp.int32).reshape(1))
    signal = signal_inverse.reshape(16, 128)
    bands = band_of_ell.reshape(16, 128)

    rows = row_transforms(sky, noise, outer, outer_t, twist, inner, zero_rows, None)
    kept = []
    products = []
    for sweep in range(ITERS - 1):
        own, rows = lax.optimization_barrier((scalars[2], rows))
        products.append(cycle_products(sweep, scalars[:2] + (own,), legendre, signal))
        coeffs, rows = apply_products(exchange(rows), products, kept)
        kept.append(coeffs)
        rows = row_transforms(
            sky, noise, outer, outer_t, twist, inner, zero_rows, exchange(rows)
        )
    state, result = last_step(scalars, exchange(rows), kept, legendre, signal, bands)
    partial = result.reshape(sim_local, 2, BANDS).sum(axis=1)
    devices = BLK * lax.axis_size("sim")
    copies = jnp.broadcast_to(partial[None], (devices, sim_local, BANDS))
    terms = lax.all_to_all(copies, ("blk", "sim"), 0, 0, tiled=True)
    all_proj = jnp.sum(terms.reshape(BLK, -1, BANDS), axis=0)
    band_proj = lax.dynamic_slice_in_dim(all_proj, lax.axis_index("sim") * sim_local, sim_local, 0)
    sim_mean = jnp.mean(all_proj, axis=0)
    center = all_proj - sim_mean[None, :]
    fisher = jnp.dot(center.T, center, precision=PRECISE) / all_proj.shape[0]
    filtered = state.reshape(block_count, MG, set_count, sim_local, 2, 128)
    return (filtered, band_proj, fisher)


def solution(mesh):
    return jax.shard_map(
        shards,
        mesh=mesh,
        in_specs=(
            P(None, "sim", "blk", None),
            P("blk", None),
            P(),
            P("blk", None, None, None),
            P(),
            P("blk", None),
            P(),
        ),
        out_specs=(P("blk", None, None, "sim", None, None), P("sim", None), P()),
        check_vma=False,
    )
```

```python
import math

import jax
import jax.numpy as jnp
import numpy as np
from jax import lax
from jax.experimental import pallas as pl
from jax.experimental.pallas import tpu as pltpu
from jax.sharding import PartitionSpec as P

NPHI = 4096
BANDS = 32
ITERS = 4
BLK = 32
CYC = 2
VEC = 16
OUTER = 32
INNER = 128
MG = 16
SLOTS = 4
PAIRS = 18
PAIR_GROUP = 3
GROUP = 6
F32 = jnp.float32
BF16 = jnp.bfloat16
PRECISE = lax.Precision.HIGHEST
NT = (((1,), (1,)), ((), ()))
TN = (((0,), (0,)), ((), ()))
NN = (((1,), (0,)), ((), ()))


def split(value):
    high = value.astype(BF16)
    return high, (value - high.astype(F32)).astype(BF16)


def dot(left, right, dims=NN):
    return lax.dot_general(left, right, dims, preferred_element_type=F32)


def dot3(left, right, dims=NN):
    return (
        dot(left[0], right[0], dims) + dot(left[0], right[1], dims) + dot(left[1], right[0], dims)
    )


def precise(left, right, dims=NN):
    return lax.dot_general(left, right, dims, precision=PRECISE, preferred_element_type=F32)


def np_split(value):
    high = value.astype(np.float32).astype(jnp.bfloat16)
    low = (value - high.astype(np.float64)).astype(np.float32).astype(jnp.bfloat16)
    return np.stack([high, low])


def constant_tables():
    k = np.arange(OUTER).reshape(2, 1, MG)
    k_rows = np.broadcast_to(k, (2, CYC, MG)).reshape(-1)
    cycle_rows = np.broadcast_to(np.arange(CYC).reshape(1, CYC, 1), (2, CYC, MG)).reshape(-1)
    a_cols = np.repeat(np.arange(OUTER), CYC)
    cycle_cols = np.tile(np.arange(CYC), OUTER)
    angle = 2.0 * np.pi * (k_rows[:, None] * a_cols[None, :] % OUTER) / OUTER
    same = cycle_rows[:, None] == cycle_cols[None, :]
    outer = np.concatenate([np.cos(angle) * same, -np.sin(angle) * same], axis=0)
    twist = 2.0 * np.pi * (k_rows[:, None] * np.arange(INNER)[None, :]) / NPHI
    twist_table = np.stack([np.cos(twist), np.sin(twist)]).astype(np.float32)
    angle = 2.0 * np.pi * (np.arange(64)[:, None] * np.arange(INNER)[None, :] % INNER) / INNER
    cosine, sine = [math.sqrt(2.0 / NPHI) * f(angle) for f in (np.cos, np.sin)]
    upper_table = np_split(np.concatenate([cosine, sine, -sine, cosine], axis=1))
    return np_split(outer), np_split(outer.T), twist_table, upper_table


def column(half, j, p, upper):
    return ((half * 2 + j) * 2 + p) * 2 + upper


def forward_part(field_of, outer_ref, twist_ref, inner_ref, zero_ref, out_ref, turned, staged):
    outer = (outer_ref[0], outer_ref[1])
    cos_twist, sin_twist = twist_ref[0], twist_ref[1]
    for v in range(VEC):
        first = dot3(outer, split(field_of(v)))
        real, imag = first[:64], first[64:]
        turned_real = real * cos_twist + imag * sin_twist
        turned_imag = imag * cos_twist - real * sin_twist
        for half in range(2):
            for cycle in range(CYC):
                at = (half * 2 + cycle) * MG
                rows = pl.ds(cycle * 256 + v, MG, stride=VEC)
                turned[half, 0, rows, :] = turned_real[at : at + MG]
                turned[half, 1, rows, :] = turned_imag[at : at + MG]
    for half in range(2):
        inner = (inner_ref[0, half], inner_ref[1, half])
        both = jnp.concatenate([turned[half, 0], turned[half, 1]], axis=1)
        coeffs = dot3(inner, split(both), NT)
        if half == 0:
            coeffs = coeffs * zero_scale(zero_ref)
        for j in range(2):
            for p in range(2):
                for upper in range(2):
                    for cycle in range(CYC):
                        row = column(half, j, p, upper) * 2 + cycle
                        lanes = cycle * 256 + upper * 128
                        staged[:, row, :] = coeffs[
                            (j * 2 + p) * 32 : (j * 2 + p + 1) * 32, lanes : lanes + 128
                        ]
    out_ref[...] = staged[...].astype(BF16)


def zero_scale(zero_ref):
    lane = lax.broadcasted_iota(jnp.int32, (128, 512), 1)
    own = jnp.concatenate([zero_ref[...]] * 4, axis=1)
    return jnp.where(jnp.logical_and(lane % 256 < VEC, own > 0.0), math.sqrt(0.5), 1.0)


def fill_inner(group_ref, upper_ref, inner_ref, zero_ref):
    groups = [group_ref[s : s + 1, :] for s in range(SLOTS)]
    halves = [group % 2 for group in groups]
    ranks = []
    for s in range(SLOTS):
        rank = jnp.zeros_like(groups[s])
        for earlier in range(s):
            rank = rank + (halves[earlier] == halves[s]).astype(jnp.int32)
        ranks.append(rank)
    index = lax.broadcasted_iota(jnp.int32, (64, BLK), 0)
    is_first = (lax.broadcasted_iota(jnp.int32, (64, 128), 0) == 0).astype(BF16)
    for half in range(2):
        for j in range(2):
            upper = jnp.zeros_like(groups[0])
            for s in range(SLOTS):
                mine = jnp.logical_and(halves[s] == half, ranks[s] == j)
                upper = upper + jnp.where(mine, groups[s] // 2, 0)
            hot = (index == jnp.broadcast_to(upper, (64, BLK))).astype(F32).astype(BF16)
            for part in range(2):
                rows = dot(hot, upper_ref[part], TN).astype(BF16)
                for p in range(2):
                    at = (j * 2 + p) * BLK
                    inner_ref[part, half, at : at + BLK, :] = rows[:, p * 256 : (p + 1) * 256]
            if half == 0:
                zero = dot(hot, is_first, TN)
                for p in range(2):
                    at = (j * 2 + p) * BLK
                    zero_ref[at : at + BLK, :] = zero


def first_rows_kernel(
    group_ref, sky_ref, noise_ref, outer_ref, twist_ref, upper_ref,
    out_ref, inner_ref, zero_ref, turned, staged,
):
    fill_inner(group_ref, upper_ref, inner_ref, zero_ref)
    noise = noise_ref[...]
    forward_part(
        lambda v: noise * sky_ref[v],
        outer_ref, twist_ref, inner_ref, zero_ref, out_ref, turned, staged,
    )


def rows_kernel(
    sky_ref, noise_ref, outer_ref, outer_t_ref, twist_ref, inner_ref, zero_ref, coeff_ref,
    out_ref, turned, staged,
):
    staged[...] = coeff_ref[...].astype(F32)
    for half in range(2):
        rows = []
        for j in range(2):
            for p in range(2):
                rows.append(
                    jnp.concatenate(
                        [
                            staged[:, column(half, j, p, upper) * 2 + cycle, :]
                            for cycle in range(CYC)
                            for upper in range(2)
                        ],
                        axis=1,
                    )
                )
        coeffs = jnp.concatenate(rows, axis=0)
        if half == 0:
            coeffs = coeffs * zero_scale(zero_ref)
        coeffs = coeffs.astype(BF16)
        inner = dot(coeffs, inner_ref[0, half], TN) + dot(coeffs, inner_ref[1, half], TN)
        for i in range(MG):
            at = half * CYC * MG + i
            cos_twist = jnp.broadcast_to(twist_ref[0, at : at + 1], (VEC, 128))
            sin_twist = jnp.broadcast_to(twist_ref[1, at : at + 1], (VEC, 128))
            for cycle in range(CYC):
                rows = slice(cycle * 256 + i * VEC, cycle * 256 + (i + 1) * VEC)
                real, imag = inner[rows, :128], inner[rows, 128:]
                turned[half, 0, rows, :] = real * cos_twist - imag * sin_twist
                turned[half, 1, rows, :] = real * sin_twist + imag * cos_twist
    noise = noise_ref[...]
    outer_t = (outer_t_ref[0], outer_t_ref[1])
    fields = []
    for v in range(VEC):
        spectrum = jnp.concatenate(
            [
                turned[half, part, pl.ds(cycle * 256 + v, MG, stride=VEC), :]
                for part in range(2)
                for half in range(2)
                for cycle in range(CYC)
            ],
            axis=0,
        )
        fields.append(noise * (sky_ref[v] - dot3(outer_t, split(spectrum))))
    forward_part(
        lambda v: fields[v],
        outer_ref, twist_ref, inner_ref, zero_ref, out_ref, turned, staged,
    )


def own_slots(group_ref, own_ref):
    own = own_ref[0]
    groups = [group_ref[s, own] for s in range(SLOTS)]
    slots = []
    for s in range(SLOTS):
        half = groups[s] % 2
        rank = jnp.int32(0)
        for earlier in range(s):
            rank = rank + jnp.where(groups[earlier] % 2 == half, 1, 0)
        slots.append((2 * half + rank, groups[s]))
    return slots


def table_copy(legendre_ref, table, arrived, group, size):
    blocks = pl.ds(group * GROUP, size)
    return pltpu.make_async_copy(legendre_ref.at[blocks], table.at[blocks], arrived.at[group])


def by_groups(blocks, step):
    def body(group, carry):
        step(group, GROUP)
        return carry

    lax.fori_loop(0, blocks // GROUP, body, 0)
    if blocks % GROUP:
        step(blocks // GROUP, blocks % GROUP)


def mark_slots(group_ref, own_ref, new_slot, zero_slot):
    for s, (slot, group) in enumerate(own_slots(group_ref, own_ref)):
        new_slot[s] = slot
        zero_slot[s] = jnp.where(group == 0, 1, 0)


def find_pairs(group_ref, block_ref, own_ref, order, pair_slot, pair_live, counter):
    base = jnp.int32(0)
    for s, (slot, group) in enumerate(own_slots(group_ref, own_ref)):
        count = 16 - group // 8
        pairs = (count + 1) // 2
        counter[s] = 2 * base

        def mark(pair, carry, slot=slot):
            pair_slot[pair] = slot
            pair_live[pair] = 1
            return carry

        lax.fori_loop(base, base + pairs, mark, 0)
        base = base + pairs

    def place(block, carry):
        slot = block_ref[0, block]
        at = counter[slot]
        order[at] = block
        counter[slot] = at + 1
        return carry

    lax.fori_loop(0, block_ref.shape[1], place, 0)
    for s in range(SLOTS):
        at = counter[s]

        @pl.when(at % 2 == 1)
        def _():
            order[at] = order[at - 1]
            pair_live[at // 2] = 0


def products_kernel(
    group_ref, block_ref, own_ref, legendre_ref, signal_ref, out_ref,
    table, sums, order, pair_slot, pair_live, counter, arrived,
):
    find_pairs(group_ref, block_ref, own_ref, order, pair_slot, pair_live, counter)

    def place_copy(at):
        return pltpu.make_async_copy(legendre_ref.at[order[at]], table.at[at], arrived.at[at])

    def fetch(at, carry):
        place_copy(at).start()
        return carry

    lax.fori_loop(0, 2 * PAIRS, fetch, 0)
    sums[...] = jnp.zeros_like(sums)

    def pair_step(group, carry):
        pairs = [group * PAIR_GROUP + n for n in range(PAIR_GROUP)]
        for pair in pairs:
            place_copy(2 * pair).wait()
            place_copy(2 * pair + 1).wait()
        slots = [pair_slot[pair] for pair in pairs]
        lives = [pair_live[pair].astype(F32) for pair in pairs]
        degrees = [
            (block_ref[1, order[2 * pair]], block_ref[1, order[2 * pair + 1]]) for pair in pairs
        ]
        for pair, slot, live, (first, second) in zip(pairs, slots, lives, degrees):
            precond = [1.0 / (2.0 + signal_ref[pl.ds(degree, 1), :]) for degree in (first, second)]
            precond = jnp.concatenate(precond, axis=1)
            lane = lax.broadcasted_iota(jnp.int32, (1, 256), 1)
            weight = precond * jnp.where(lane < 128, 1.0, live)
            weights = []
            for _ in range(ITERS - 1):
                weights.append(jnp.broadcast_to(weight, (64, 256)))
                weight = weight * (2.0 * precond)
            for i in range(MG):
                values = jnp.concatenate([table[2 * pair, i], table[2 * pair + 1, i]], axis=1)
                wide = values.astype(F32)
                scaled = jnp.concatenate([(wide * w).astype(BF16) for w in weights], axis=0)
                sums[slot * MG + i] += dot(scaled, values, NT)
        return carry

    lax.fori_loop(0, PAIRS // PAIR_GROUP, pair_step, 0)
    for at in range(SLOTS * MG):
        out_ref[at // 8, (at % 8) * 64 : (at % 8 + 1) * 64, :] = jnp.concatenate(
            [sums[at, n * 64 : (n + 1) * 64] for n in range(ITERS - 1)], axis=1
        ).astype(BF16)


def apply_kernel(count, *refs):
    coeff_ref, product_ref = refs[:2]
    earlier = refs[2 : 1 + count]
    kept_ref, out_ref, staged, ordered = refs[1 + count :]
    staged[...] = coeff_ref[...].astype(F32)
    for c in range(16):
        for cycle in range(CYC):
            ordered[c, pl.ds(cycle, BLK, stride=2), :] = staged[:, 2 * c + cycle, :]
    kept_ref[...] = ordered[...].astype(BF16)
    history = [kept_ref] + list(earlier)[::-1]
    lane = lax.broadcasted_iota(jnp.int32, (64, 256), 1) % 128 // VEC
    for slot in range(SLOTS):
        for upper in range(2):
            at = [(slot * 2 + p) * 2 + upper for p in range(2)]
            right = jnp.concatenate(
                [jnp.concatenate([ref[at[0]], ref[at[1]]], axis=1) for ref in history], axis=0
            )
            mixed = dot(product_ref[slot * 2 + upper, :, : 64 * count], right)
            result = mixed[:64]
            for i in range(1, 8):
                result = jnp.where(lane == i, mixed[i * 64 : (i + 1) * 64], result)
            ordered[at[0]] = result[:, :128]
            ordered[at[1]] = result[:, 128:]
    for c in range(16):
        for cycle in range(CYC):
            staged[:, 2 * c + cycle, :] = ordered[c, pl.ds(cycle, BLK, stride=2), :]
    out_ref[...] = staged[...].astype(BF16)


def last_kernel(
    group_ref, block_ref, own_ref, coeff_ref, kept0_ref, kept1_ref, kept2_ref, legendre_ref,
    signal_ref, band_ref, state_ref, band_out,
    table, staged, mixed, packed, products, outgoing, new_slot, zero_slot, arrived, sent,
):
    blocks = legendre_ref.shape[0]

    by_groups(blocks, lambda g, n: table_copy(legendre_ref, table, arrived, g, n).start())
    mark_slots(group_ref, own_ref, new_slot, zero_slot)
    products[...] = jnp.zeros_like(products)
    staged[...] = coeff_ref[...].astype(F32)
    blank = jnp.zeros((64, 128), BF16)
    unit = (
        lax.broadcasted_iota(jnp.int32, (128, 128), 0)
        == lax.broadcasted_iota(jnp.int32, (128, 128), 1)
    ).astype(BF16)
    for slot in range(SLOTS):
        for upper in range(2):
            for sweep in range(ITERS):
                for p in range(2):
                    c = (slot * 2 + p) * 2 + upper
                    if sweep < ITERS - 1:
                        tile = (kept0_ref, kept1_ref, kept2_ref)[sweep][c]
                    else:
                        for cycle in range(CYC):
                            mixed[0, pl.ds(cycle, BLK, stride=2), :] = staged[:, 2 * c + cycle, :]
                        tile = mixed[0, 0:64, :].astype(BF16)
                    turned = dot(unit, jnp.concatenate([tile, blank], axis=0), NT)
                    for i in range(8):
                        rows = pl.ds(sweep * 32 + p, VEC, stride=2)
                        mixed[1 + i, rows, :] = turned[i * VEC : (i + 1) * VEC]
            for i in range(8):
                packed[slot * MG + upper * 8 + i] = mixed[1 + i, :, 0:64].astype(BF16)

    def out_copy(group, size):
        some = pl.ds(group * GROUP, size)
        return pltpu.make_async_copy(outgoing.at[some], state_ref.at[some], sent.at[group])

    def step(group, size):
        table_copy(legendre_ref, table, arrived, group, size).wait()
        some = [group * GROUP + n for n in range(size)]
        slots = [new_slot[block_ref[0, block]] for block in some]
        halves = [
            jnp.where(zero_slot[block_ref[0, block]] > 0, 0.5, 1.0) for block in some
        ]
        degrees = [block_ref[1, block] for block in some]
        for block, slot, half, degree in zip(some, slots, halves, degrees):
            precond = jnp.broadcast_to(1.0 / (2.0 + signal_ref[pl.ds(degree, 1), :]), (32, 128))
            damp = 2.0 * precond
            total = jnp.zeros((VEC, 128), F32)
            for i in range(MG):
                harmonic = dot(packed[slot * MG + i], table[block, i])
                state = harmonic[0:32]
                for sweep in range(1, ITERS):
                    state = harmonic[sweep * 32 : (sweep + 1) * 32] + damp * state
                state = precond * state
                outgoing[block, i * 32 : (i + 1) * 32, :] = state.astype(BF16)
                one = state[:VEC] * state[VEC:]
                if i == 0:
                    one = one * half
                total = total + one
            products[degree] += 2.0 * total
        out_copy(group, size).start()

    by_groups(blocks, step)
    raw = jnp.zeros((VEC, 128), F32)
    counts = jnp.zeros((VEC, 128), F32)
    bins = lax.broadcasted_iota(jnp.int32, (128, 128), 0) % BANDS
    lane = lax.broadcasted_iota(jnp.int32, (VEC, 128), 1)
    row = lax.broadcasted_iota(jnp.int32, (VEC, 128), 0)
    for e in range(16):
        member = (jnp.broadcast_to(band_ref[e : e + 1, :], (128, 128)) == bins).astype(F32)
        raw = raw + precise(products[e], member, NT)
        counts = counts + precise((2 * (e * 128 + lane) + 1).astype(F32), member, NT)
    terms = jnp.where(lane // BANDS == row // 2 % 4, raw * (1.0 / jnp.sqrt(counts)), 0.0)
    terms = jnp.concatenate(
        [jnp.sum(terms[h * 8 : (h + 1) * 8], axis=0, keepdims=True) for h in range(2)], axis=0
    )
    band_out[...] = jnp.broadcast_to(terms[None], band_out.shape)
    by_groups(blocks, lambda g, n: out_copy(g, n).wait())


def fisher_kernel(sim_ref, term_ref, band_out, fisher_out, rows_ref):
    sims = term_ref.shape[0] // BLK
    for part in range(sims):
        total = term_ref[part]
        for index in range(1, BLK):
            total = total + term_ref[index * sims + part]
        rows_ref[2 * part : 2 * part + 2, :] = total
    values = rows_ref[...]
    row = lax.broadcasted_iota(jnp.int32, (128, 128), 0)
    lane = lax.broadcasted_iota(jnp.int32, (128, 128), 1)
    count = sims * 8
    fold = jnp.where(row % BANDS == lane % BANDS, 1.0 / count, 0.0).astype(F32)
    mean = jnp.sum(precise(values, fold), axis=0, keepdims=True)
    center = values - jnp.broadcast_to(mean, values.shape)
    square = jnp.where(row // BANDS == lane // BANDS, precise(center, center, TN), 0.0)
    column = lax.broadcasted_iota(jnp.int32, (128, BANDS), 0) % BANDS
    pick = (column == lax.broadcasted_iota(jnp.int32, (128, BANDS), 1)).astype(F32)
    fisher_out[...] = precise(precise(pick, square, TN), pick) / count
    own = rows_ref[pl.ds(2 * sim_ref[0], 2), :]
    own = jnp.concatenate([jnp.broadcast_to(own[h : h + 1], (4, 128)) for h in range(2)], axis=0)
    keep = lane[:8] // BANDS == row[:8] % 4
    band_out[...] = precise(jnp.where(keep, own, 0.0), pick)


def params(megabytes, **more):
    return pltpu.CompilerParams(vmem_limit_bytes=megabytes << 20, **more)


def in_hbm(*arrays):
    return [pltpu.with_memory_space_constraint(array, pltpu.HBM) for array in arrays]


SENT = jax.ShapeDtypeStruct((BLK, 32, 128), BF16)
KEPT = jax.ShapeDtypeStruct((16, 64, 128), BF16)
SMEM = pl.BlockSpec(memory_space=pltpu.SMEM)
VMEM = pl.BlockSpec(memory_space=pltpu.VMEM)
ANY = pl.BlockSpec(memory_space=pl.ANY)


def row_scratch():
    return [pltpu.VMEM((2, 2, 512, 128), F32), pltpu.VMEM((BLK, 32, 128), F32)]


def first_transforms(groups, sky, noise, outer, twist, upper):
    return pl.pallas_call(
        first_rows_kernel,
        out_shape=(
            SENT,
            jax.ShapeDtypeStruct((2, 2, 128, 256), BF16),
            jax.ShapeDtypeStruct((128, 128), F32),
        ),
        scratch_shapes=row_scratch(),
        compiler_params=params(28),
        name="first_rows",
    )(*in_hbm(groups, sky, noise, outer, twist, upper))


def row_transforms(sky, noise, outer, outer_t, twist, inner, zero_rows, coeffs):
    return pl.pallas_call(
        rows_kernel,
        out_shape=SENT,
        scratch_shapes=row_scratch(),
        compiler_params=params(28),
        name="rows",
    )(sky, noise, outer, outer_t, twist, inner, zero_rows, coeffs)


def cycle_products(scalars, legendre, signal):
    return pl.pallas_call(
        products_kernel,
        out_shape=jax.ShapeDtypeStruct((8, 512, 192), BF16),
        in_specs=[SMEM, SMEM, SMEM, ANY, VMEM],
        scratch_shapes=[
            pltpu.VMEM((2 * PAIRS,) + legendre.shape[1:], BF16),
            pltpu.VMEM((SLOTS * MG, 192, 64), F32),
            pltpu.SMEM((2 * PAIRS,), jnp.int32),
            pltpu.SMEM((PAIRS,), jnp.int32),
            pltpu.SMEM((PAIRS,), jnp.int32),
            pltpu.SMEM((SLOTS,), jnp.int32),
            pltpu.SemaphoreType.DMA((2 * PAIRS,)),
        ],
        compiler_params=params(28),
        name="cycle_products",
    )(*in_hbm(*scalars, legendre, signal))


def apply_products(coeffs, products, kept):
    count = len(kept) + 1

    def body(*refs):
        apply_kernel(count, *refs)

    return pl.pallas_call(
        body,
        out_shape=(KEPT, SENT),
        scratch_shapes=[pltpu.VMEM((BLK, 32, 128), F32), pltpu.VMEM((16, 64, 128), F32)],
        compiler_params=params(28),
        name="apply_products_" + str(count),
    )(coeffs, products, *kept)


def last_step(copies, scalars, coeffs, kept, legendre, signal, bands):
    (legendre,) = in_hbm(legendre)
    return pl.pallas_call(
        last_kernel,
        out_shape=(
            jax.ShapeDtypeStruct((legendre.shape[0], 512, 128), BF16),
            jax.ShapeDtypeStruct((copies, 2, 128), F32),
        ),
        in_specs=[SMEM] * 3 + [VMEM] * 4 + [ANY, VMEM, VMEM],
        out_specs=(ANY, VMEM),
        scratch_shapes=[
            pltpu.VMEM(legendre.shape, BF16),
            pltpu.VMEM((BLK, 32, 128), F32),
            pltpu.VMEM((9, 128, 128), F32),
            pltpu.VMEM((SLOTS * MG, 128, 64), BF16),
            pltpu.VMEM((16, VEC, 128), F32),
            pltpu.VMEM((legendre.shape[0], 512, 128), BF16),
        ]
        + [
            pltpu.SMEM((SLOTS,), jnp.int32),
            pltpu.SMEM((SLOTS,), jnp.int32),
            pltpu.SemaphoreType.DMA((-(-legendre.shape[0] // GROUP),)),
            pltpu.SemaphoreType.DMA((-(-legendre.shape[0] // GROUP),)),
        ],
        compiler_params=params(28),
        name="last_modes",
    )(*scalars, coeffs, *kept, legendre, signal, bands)


def fisher_step(sim_index, terms):
    return pl.pallas_call(
        fisher_kernel,
        out_shape=(
            jax.ShapeDtypeStruct((8, BANDS), F32),
            jax.ShapeDtypeStruct((BANDS, BANDS), F32),
        ),
        in_specs=[SMEM, VMEM],
        scratch_shapes=[pltpu.VMEM((terms.shape[0] // BLK * 2, 128), F32)],
        compiler_params=params(28),
        name="fisher",
    )(sim_index, terms)


def exchange(rows):
    return lax.all_to_all(rows, "blk", 0, 0, tiled=True)


def shards(sky_maps, noise_weight, signal_inverse, legendre, m_groups, block_list, band_of_ell):
    blk_index = lax.axis_index("blk")
    set_count, sim_local, cycle_local, cycle_pixels = sky_maps.shape
    block_count = legendre.shape[0]
    outer, outer_t, twist, upper = [jnp.asarray(t) for t in constant_tables()]
    sky = sky_maps.reshape(set_count, sim_local, cycle_local, OUTER, INNER)
    sky = sky.transpose(0, 1, 3, 2, 4).reshape(VEC, OUTER * CYC, INNER)
    noise = noise_weight.reshape(CYC, OUTER, INNER).transpose(1, 0, 2).reshape(OUTER * CYC, INNER)
    scalars = (m_groups.T, block_list.T, blk_index.astype(jnp.int32).reshape(1))
    signal = signal_inverse.reshape(16, 128)
    bands = band_of_ell.reshape(16, 128)

    rows, inner, zero_rows = first_transforms(scalars[0], sky, noise, outer, twist, upper)
    own, rows = lax.optimization_barrier((scalars[2], rows))
    products = cycle_products(scalars[:2] + (own,), legendre, signal)
    kept = []
    for sweep in range(ITERS - 1):
        coeffs, rows = apply_products(exchange(rows), products, kept)
        kept.append(coeffs)
        rows = row_transforms(
            sky, noise, outer, outer_t, twist, inner, zero_rows, exchange(rows)
        )
    sims = lax.axis_size("sim")
    state, copies = last_step(BLK * sims, scalars, exchange(rows), kept, legendre, signal, bands)
    terms = lax.all_to_all(copies, ("blk", "sim"), 0, 0, tiled=True)
    sim_index = lax.axis_index("sim").astype(jnp.int32).reshape(1)
    band_proj, fisher = fisher_step(sim_index, terms)
    filtered = state.reshape(block_count, MG, set_count, sim_local, 2, 128)
    return (filtered, band_proj, fisher)


def solution(mesh):
    return jax.shard_map(
        shards,
        mesh=mesh,
        in_specs=(
            P(None, "sim", "blk", None),
            P("blk", None),
            P(),
            P("blk", None, None, None),
            P(),
            P("blk", None),
            P(),
        ),
        out_specs=(P("blk", None, None, "sim", None, None), P("sim", None), P()),
        check_vma=False,
    )
```

```python
import math

import jax
import jax.numpy as jnp
import numpy as np
from jax import lax
from jax.experimental import pallas as pl
from jax.experimental.pallas import tpu as pltpu
from jax.sharding import PartitionSpec as P

NPHI = 4096
BANDS = 32
ITERS = 4
BLK = 32
CYC = 2
VEC = 16
OUTER = 32
INNER = 128
MG = 16
SLOTS = 4
PAIRS = 18
PAIR_GROUP = 3
GROUP = 6
F32 = jnp.float32
BF16 = jnp.bfloat16
PRECISE = lax.Precision.HIGHEST
NT = (((1,), (1,)), ((), ()))
TN = (((0,), (0,)), ((), ()))
NN = (((1,), (0,)), ((), ()))


def split(value):
    high = value.astype(BF16)
    return high, (value - high.astype(F32)).astype(BF16)


def dot(left, right, dims=NN):
    return lax.dot_general(left, right, dims, preferred_element_type=F32)


def precise(left, right, dims=NN):
    return lax.dot_general(left, right, dims, precision=PRECISE, preferred_element_type=F32)


def rounded(value):
    return value.astype(np.float32).astype(jnp.bfloat16)


def constant_tables():
    k = np.arange(OUTER).reshape(2, 1, MG)
    k_rows = np.broadcast_to(k, (2, CYC, MG)).reshape(-1)
    cycle_rows = np.broadcast_to(np.arange(CYC).reshape(1, CYC, 1), (2, CYC, MG)).reshape(-1)
    a_cols = np.repeat(np.arange(OUTER), CYC)
    cycle_cols = np.tile(np.arange(CYC), OUTER)
    angle = 2.0 * np.pi * (k_rows[:, None] * a_cols[None, :] % OUTER) / OUTER
    same = cycle_rows[:, None] == cycle_cols[None, :]
    outer = np.concatenate([np.cos(angle) * same, -np.sin(angle) * same], axis=0)
    twist = 2.0 * np.pi * (k_rows[:, None] * np.arange(INNER)[None, :]) / NPHI
    twist_table = np.stack([np.cos(twist), np.sin(twist)]).astype(np.float32)
    angle = 2.0 * np.pi * (np.arange(64)[:, None] * np.arange(INNER)[None, :] % INNER) / INNER
    cosine, sine = [math.sqrt(2.0 / NPHI) * f(angle) for f in (np.cos, np.sin)]
    upper_table = rounded(np.concatenate([cosine, sine, -sine, cosine], axis=1))
    return rounded(outer), rounded(outer.T), twist_table, upper_table


def column(half, j, p, upper):
    return ((half * 2 + j) * 2 + p) * 2 + upper


def forward_part(field_of, outer_ref, twist_ref, inner_ref, zero_ref, out_ref, turned, staged):
    outer = outer_ref[...]
    cos_twist, sin_twist = twist_ref[0], twist_ref[1]
    for v in range(VEC):
        first = dot(outer, field_of(v).astype(BF16))
        real, imag = first[:64], first[64:]
        turned_real = real * cos_twist + imag * sin_twist
        turned_imag = imag * cos_twist - real * sin_twist
        for half in range(2):
            for cycle in range(CYC):
                at = (half * 2 + cycle) * MG
                rows = pl.ds(cycle * 256 + v, MG, stride=VEC)
                turned[half, 0, rows, :] = turned_real[at : at + MG]
                turned[half, 1, rows, :] = turned_imag[at : at + MG]
    for half in range(2):
        both = jnp.concatenate([turned[half, 0], turned[half, 1]], axis=1)
        coeffs = dot(inner_ref[half], both.astype(BF16), NT)
        if half == 0:
            coeffs = coeffs * zero_scale(zero_ref)
        for j in range(2):
            for p in range(2):
                for upper in range(2):
                    for cycle in range(CYC):
                        row = column(half, j, p, upper) * 2 + cycle
                        lanes = cycle * 256 + upper * 128
                        staged[:, row, :] = coeffs[
                            (j * 2 + p) * 32 : (j * 2 + p + 1) * 32, lanes : lanes + 128
                        ]
    out_ref[...] = staged[...].astype(BF16)


def zero_scale(zero_ref):
    lane = lax.broadcasted_iota(jnp.int32, (128, 512), 1)
    own = jnp.concatenate([zero_ref[...]] * 4, axis=1)
    return jnp.where(jnp.logical_and(lane % 256 < VEC, own > 0.0), math.sqrt(0.5), 1.0)


def fill_inner(group_ref, upper_ref, inner_ref, zero_ref):
    groups = [group_ref[s : s + 1, :] for s in range(SLOTS)]
    halves = [group % 2 for group in groups]
    ranks = []
    for s in range(SLOTS):
        rank = jnp.zeros_like(groups[s])
        for earlier in range(s):
            rank = rank + (halves[earlier] == halves[s]).astype(jnp.int32)
        ranks.append(rank)
    index = lax.broadcasted_iota(jnp.int32, (64, BLK), 0)
    is_first = (lax.broadcasted_iota(jnp.int32, (64, 128), 0) == 0).astype(BF16)
    for half in range(2):
        for j in range(2):
            upper = jnp.zeros_like(groups[0])
            for s in range(SLOTS):
                mine = jnp.logical_and(halves[s] == half, ranks[s] == j)
                upper = upper + jnp.where(mine, groups[s] // 2, 0)
            hot = (index == jnp.broadcast_to(upper, (64, BLK))).astype(F32).astype(BF16)
            rows = dot(hot, upper_ref[...], TN).astype(BF16)
            for p in range(2):
                at = (j * 2 + p) * BLK
                inner_ref[half, at : at + BLK, :] = rows[:, p * 256 : (p + 1) * 256]
            if half == 0:
                zero = dot(hot, is_first, TN)
                for p in range(2):
                    at = (j * 2 + p) * BLK
                    zero_ref[at : at + BLK, :] = zero


def first_rows_kernel(
    group_ref, sky_ref, noise_ref, outer_ref, twist_ref, upper_ref,
    out_ref, inner_ref, zero_ref, turned, staged,
):
    fill_inner(group_ref, upper_ref, inner_ref, zero_ref)
    noise = noise_ref[...]
    forward_part(
        lambda v: noise * sky_ref[v],
        outer_ref, twist_ref, inner_ref, zero_ref, out_ref, turned, staged,
    )


def rows_kernel(
    sky_ref, noise_ref, outer_ref, outer_t_ref, twist_ref, inner_ref, zero_ref, coeff_ref,
    out_ref, turned, staged,
):
    staged[...] = coeff_ref[...].astype(F32)
    for half in range(2):
        rows = []
        for j in range(2):
            for p in range(2):
                rows.append(
                    jnp.concatenate(
                        [
                            staged[:, column(half, j, p, upper) * 2 + cycle, :]
                            for cycle in range(CYC)
                            for upper in range(2)
                        ],
                        axis=1,
                    )
                )
        coeffs = jnp.concatenate(rows, axis=0)
        if half == 0:
            coeffs = coeffs * zero_scale(zero_ref)
        coeffs = coeffs.astype(BF16)
        inner = dot(coeffs, inner_ref[half], TN)
        for i in range(MG):
            at = half * CYC * MG + i
            cos_twist = jnp.broadcast_to(twist_ref[0, at : at + 1], (VEC, 128))
            sin_twist = jnp.broadcast_to(twist_ref[1, at : at + 1], (VEC, 128))
            for cycle in range(CYC):
                rows = slice(cycle * 256 + i * VEC, cycle * 256 + (i + 1) * VEC)
                real, imag = inner[rows, :128], inner[rows, 128:]
                turned[half, 0, rows, :] = real * cos_twist - imag * sin_twist
                turned[half, 1, rows, :] = real * sin_twist + imag * cos_twist
    noise = noise_ref[...]
    outer_t = outer_t_ref[...]
    fields = []
    for v in range(VEC):
        spectrum = jnp.concatenate(
            [
                turned[half, part, pl.ds(cycle * 256 + v, MG, stride=VEC), :]
                for part in range(2)
                for half in range(2)
                for cycle in range(CYC)
            ],
            axis=0,
        )
        fields.append(noise * (sky_ref[v] - dot(outer_t, spectrum.astype(BF16))))
    forward_part(
        lambda v: fields[v],
        outer_ref, twist_ref, inner_ref, zero_ref, out_ref, turned, staged,
    )


def own_slots(group_ref, own_ref):
    own = own_ref[0]
    groups = [group_ref[s, own] for s in range(SLOTS)]
    slots = []
    for s in range(SLOTS):
        half = groups[s] % 2
        rank = jnp.int32(0)
        for earlier in range(s):
            rank = rank + jnp.where(groups[earlier] % 2 == half, 1, 0)
        slots.append((2 * half + rank, groups[s]))
    return slots


def table_copy(legendre_ref, table, arrived, group, size):
    blocks = pl.ds(group * GROUP, size)
    return pltpu.make_async_copy(legendre_ref.at[blocks], table.at[blocks], arrived.at[group])


def by_groups(blocks, step):
    def body(group, carry):
        step(group, GROUP)
        return carry

    lax.fori_loop(0, blocks // GROUP, body, 0)
    if blocks % GROUP:
        step(blocks // GROUP, blocks % GROUP)


def mark_slots(group_ref, own_ref, new_slot, zero_slot):
    for s, (slot, group) in enumerate(own_slots(group_ref, own_ref)):
        new_slot[s] = slot
        zero_slot[s] = jnp.where(group == 0, 1, 0)


def find_pairs(group_ref, block_ref, own_ref, order, pair_slot, pair_live, counter):
    base = jnp.int32(0)
    for s, (slot, group) in enumerate(own_slots(group_ref, own_ref)):
        count = 16 - group // 8
        pairs = (count + 1) // 2
        counter[s] = 2 * base

        def mark(pair, carry, slot=slot):
            pair_slot[pair] = slot
            pair_live[pair] = 1
            return carry

        lax.fori_loop(base, base + pairs, mark, 0)
        base = base + pairs

    def place(block, carry):
        slot = block_ref[0, block]
        at = counter[slot]
        order[at] = block
        counter[slot] = at + 1
        return carry

    lax.fori_loop(0, block_ref.shape[1], place, 0)
    for s in range(SLOTS):
        at = counter[s]

        @pl.when(at % 2 == 1)
        def _():
            order[at] = order[at - 1]
            pair_live[at // 2] = 0


def products_kernel(
    group_ref, block_ref, own_ref, legendre_ref, signal_ref, out_ref,
    table, sums, order, pair_slot, pair_live, counter, arrived,
):
    find_pairs(group_ref, block_ref, own_ref, order, pair_slot, pair_live, counter)

    def place_copy(at):
        return pltpu.make_async_copy(legendre_ref.at[order[at]], table.at[at], arrived.at[at])

    def fetch(at, carry):
        place_copy(at).start()
        return carry

    lax.fori_loop(0, 2 * PAIRS, fetch, 0)
    sums[...] = jnp.zeros_like(sums)

    def pair_step(group, carry):
        pairs = [group * PAIR_GROUP + n for n in range(PAIR_GROUP)]
        for pair in pairs:
            place_copy(2 * pair).wait()
            place_copy(2 * pair + 1).wait()
        slots = [pair_slot[pair] for pair in pairs]
        lives = [pair_live[pair].astype(F32) for pair in pairs]
        degrees = [
            (block_ref[1, order[2 * pair]], block_ref[1, order[2 * pair + 1]]) for pair in pairs
        ]
        for pair, slot, live, (first, second) in zip(pairs, slots, lives, degrees):
            precond = [1.0 / (2.0 + signal_ref[pl.ds(degree, 1), :]) for degree in (first, second)]
            precond = jnp.concatenate(precond, axis=1)
            lane = lax.broadcasted_iota(jnp.int32, (1, 256), 1)
            weight = precond * jnp.where(lane < 128, 1.0, live)
            weights = []
            for _ in range(ITERS - 1):
                weights.append(jnp.broadcast_to(weight, (64, 256)))
                weight = weight * (2.0 * precond)
            for i in range(MG):
                values = jnp.concatenate([table[2 * pair, i], table[2 * pair + 1, i]], axis=1)
                wide = values.astype(F32)
                scaled = jnp.concatenate([(wide * w).astype(BF16) for w in weights], axis=0)
                sums[slot * MG + i] += dot(scaled, values, NT)
        return carry

    lax.fori_loop(0, PAIRS // PAIR_GROUP, pair_step, 0)
    for at in range(SLOTS * MG):
        out_ref[at // 8, (at % 8) * 64 : (at % 8 + 1) * 64, :] = jnp.concatenate(
            [sums[at, n * 64 : (n + 1) * 64] for n in range(ITERS - 1)], axis=1
        ).astype(BF16)


def apply_kernel(count, *refs):
    coeff_ref, product_ref = refs[:2]
    earlier = refs[2 : 1 + count]
    kept_ref, out_ref, staged, ordered = refs[1 + count :]
    staged[...] = coeff_ref[...].astype(F32)
    for c in range(16):
        for cycle in range(CYC):
            ordered[c, pl.ds(cycle, BLK, stride=2), :] = staged[:, 2 * c + cycle, :]
    kept_ref[...] = ordered[...].astype(BF16)
    history = [kept_ref] + list(earlier)[::-1]
    lane = lax.broadcasted_iota(jnp.int32, (64, 256), 1) % 128 // VEC
    for slot in range(SLOTS):
        for upper in range(2):
            at = [(slot * 2 + p) * 2 + upper for p in range(2)]
            right = jnp.concatenate(
                [jnp.concatenate([ref[at[0]], ref[at[1]]], axis=1) for ref in history], axis=0
            )
            mixed = dot(product_ref[slot * 2 + upper, :, : 64 * count], right)
            result = mixed[:64]
            for i in range(1, 8):
                result = jnp.where(lane == i, mixed[i * 64 : (i + 1) * 64], result)
            ordered[at[0]] = result[:, :128]
            ordered[at[1]] = result[:, 128:]
    for c in range(16):
        for cycle in range(CYC):
            staged[:, 2 * c + cycle, :] = ordered[c, pl.ds(cycle, BLK, stride=2), :]
    out_ref[...] = staged[...].astype(BF16)


def last_kernel(
    group_ref, block_ref, own_ref, coeff_ref, kept0_ref, kept1_ref, kept2_ref, legendre_ref,
    signal_ref, band_ref, state_ref, band_out,
    table, staged, mixed, packed, products, outgoing, new_slot, zero_slot, arrived, sent,
):
    blocks = legendre_ref.shape[0]

    by_groups(blocks, lambda g, n: table_copy(legendre_ref, table, arrived, g, n).start())
    mark_slots(group_ref, own_ref, new_slot, zero_slot)
    products[...] = jnp.zeros_like(products)
    staged[...] = coeff_ref[...].astype(F32)
    blank = jnp.zeros((64, 128), BF16)
    unit = (
        lax.broadcasted_iota(jnp.int32, (128, 128), 0)
        == lax.broadcasted_iota(jnp.int32, (128, 128), 1)
    ).astype(BF16)
    for slot in range(SLOTS):
        for upper in range(2):
            for sweep in range(ITERS):
                for p in range(2):
                    c = (slot * 2 + p) * 2 + upper
                    if sweep < ITERS - 1:
                        tile = (kept0_ref, kept1_ref, kept2_ref)[sweep][c]
                    else:
                        for cycle in range(CYC):
                            mixed[0, pl.ds(cycle, BLK, stride=2), :] = staged[:, 2 * c + cycle, :]
                        tile = mixed[0, 0:64, :].astype(BF16)
                    turned = dot(unit, jnp.concatenate([tile, blank], axis=0), NT)
                    for i in range(8):
                        rows = pl.ds(sweep * 32 + p, VEC, stride=2)
                        mixed[1 + i, rows, :] = turned[i * VEC : (i + 1) * VEC]
            for i in range(8):
                packed[slot * MG + upper * 8 + i] = mixed[1 + i, :, 0:64].astype(BF16)

    def out_copy(group, size):
        some = pl.ds(group * GROUP, size)
        return pltpu.make_async_copy(outgoing.at[some], state_ref.at[some], sent.at[group])

    def step(group, size):
        table_copy(legendre_ref, table, arrived, group, size).wait()
        some = [group * GROUP + n for n in range(size)]
        slots = [new_slot[block_ref[0, block]] for block in some]
        halves = [
            jnp.where(zero_slot[block_ref[0, block]] > 0, 0.5, 1.0) for block in some
        ]
        degrees = [block_ref[1, block] for block in some]
        for block, slot, half, degree in zip(some, slots, halves, degrees):
            precond = jnp.broadcast_to(1.0 / (2.0 + signal_ref[pl.ds(degree, 1), :]), (32, 128))
            damp = 2.0 * precond
            total = jnp.zeros((VEC, 128), F32)
            for i in range(MG):
                harmonic = dot(packed[slot * MG + i], table[block, i])
                state = harmonic[0:32]
                for sweep in range(1, ITERS):
                    state = harmonic[sweep * 32 : (sweep + 1) * 32] + damp * state
                state = precond * state
                outgoing[block, i * 32 : (i + 1) * 32, :] = state.astype(BF16)
                one = state[:VEC] * state[VEC:]
                if i == 0:
                    one = one * half
                total = total + one
            products[degree] += 2.0 * total
        out_copy(group, size).start()

    by_groups(blocks, step)
    bins = lax.broadcasted_iota(jnp.int32, (128, 128), 0) % BANDS
    lane = lax.broadcasted_iota(jnp.int32, (VEC, 128), 1)
    row = lax.broadcasted_iota(jnp.int32, (VEC, 128), 0)
    sums = jnp.zeros((80, 128), F32)
    for e in range(16):
        member = (jnp.broadcast_to(band_ref[e : e + 1, :], (128, 128)) == bins).astype(F32)
        high = products[e].astype(BF16)
        middle, low = split(products[e] - high.astype(F32))
        weight = split((2 * (e * 128 + lane) + 1).astype(F32))
        left = jnp.concatenate([high, middle, low, weight[0], weight[1]], axis=0)
        sums = sums + dot(left, member.astype(BF16), NT)
    raw = sums[0:16] + (sums[16:32] + sums[32:48])
    counts = sums[48:64] + sums[64:80]
    terms = jnp.where(lane // BANDS == row // 2 % 4, raw * (1.0 / jnp.sqrt(counts)), 0.0)
    terms = jnp.concatenate(
        [jnp.sum(terms[h * 8 : (h + 1) * 8], axis=0, keepdims=True) for h in range(2)], axis=0
    )
    band_out[...] = jnp.broadcast_to(terms[None], band_out.shape)
    by_groups(blocks, lambda g, n: out_copy(g, n).wait())


def fisher_kernel(sim_ref, term_ref, band_out, fisher_out, rows_ref):
    sims = term_ref.shape[0] // BLK
    for part in range(sims):
        total = term_ref[part]
        for index in range(1, BLK):
            total = total + term_ref[index * sims + part]
        rows_ref[2 * part : 2 * part + 2, :] = total
    values = rows_ref[...]
    row = lax.broadcasted_iota(jnp.int32, (128, 128), 0)
    lane = lax.broadcasted_iota(jnp.int32, (128, 128), 1)
    count = sims * 8
    fold = jnp.where(row % BANDS == lane % BANDS, 1.0 / count, 0.0).astype(F32)
    mean = jnp.sum(precise(values, fold), axis=0, keepdims=True)
    center = values - jnp.broadcast_to(mean, values.shape)
    square = jnp.where(row // BANDS == lane // BANDS, precise(center, center, TN), 0.0)
    column = lax.broadcasted_iota(jnp.int32, (128, BANDS), 0) % BANDS
    pick = (column == lax.broadcasted_iota(jnp.int32, (128, BANDS), 1)).astype(F32)
    fisher_out[...] = precise(precise(pick, square, TN), pick) / count
    own = rows_ref[pl.ds(2 * sim_ref[0], 2), :]
    own = jnp.concatenate([jnp.broadcast_to(own[h : h + 1], (4, 128)) for h in range(2)], axis=0)
    keep = lane[:8] // BANDS == row[:8] % 4
    band_out[...] = precise(jnp.where(keep, own, 0.0), pick)


def params(megabytes, **more):
    return pltpu.CompilerParams(vmem_limit_bytes=megabytes << 20, **more)


def in_hbm(*arrays):
    return [pltpu.with_memory_space_constraint(array, pltpu.HBM) for array in arrays]


SENT = jax.ShapeDtypeStruct((BLK, 32, 128), BF16)
KEPT = jax.ShapeDtypeStruct((16, 64, 128), BF16)
SMEM = pl.BlockSpec(memory_space=pltpu.SMEM)
VMEM = pl.BlockSpec(memory_space=pltpu.VMEM)
ANY = pl.BlockSpec(memory_space=pl.ANY)


def row_scratch():
    return [pltpu.VMEM((2, 2, 512, 128), F32), pltpu.VMEM((BLK, 32, 128), F32)]


def first_transforms(groups, sky, noise, outer, twist, upper):
    return pl.pallas_call(
        first_rows_kernel,
        out_shape=(
            SENT,
            jax.ShapeDtypeStruct((2, 128, 256), BF16),
            jax.ShapeDtypeStruct((128, 128), F32),
        ),
        scratch_shapes=row_scratch(),
        compiler_params=params(28),
        name="first_rows",
    )(*in_hbm(groups, sky, noise, outer, twist, upper))


def row_transforms(sky, noise, outer, outer_t, twist, inner, zero_rows, coeffs):
    return pl.pallas_call(
        rows_kernel,
        out_shape=SENT,
        scratch_shapes=row_scratch(),
        compiler_params=params(28),
        name="rows",
    )(sky, noise, outer, outer_t, twist, inner, zero_rows, coeffs)


def cycle_products(scalars, legendre, signal):
    return pl.pallas_call(
        products_kernel,
        out_shape=jax.ShapeDtypeStruct((8, 512, 192), BF16),
        in_specs=[SMEM, SMEM, SMEM, ANY, VMEM],
        scratch_shapes=[
            pltpu.VMEM((2 * PAIRS,) + legendre.shape[1:], BF16),
            pltpu.VMEM((SLOTS * MG, 192, 64), F32),
            pltpu.SMEM((2 * PAIRS,), jnp.int32),
            pltpu.SMEM((PAIRS,), jnp.int32),
            pltpu.SMEM((PAIRS,), jnp.int32),
            pltpu.SMEM((SLOTS,), jnp.int32),
            pltpu.SemaphoreType.DMA((2 * PAIRS,)),
        ],
        compiler_params=params(28),
        name="cycle_products",
    )(*in_hbm(*scalars, legendre, signal))


def apply_products(coeffs, products, kept):
    count = len(kept) + 1

    def body(*refs):
        apply_kernel(count, *refs)

    return pl.pallas_call(
        body,
        out_shape=(KEPT, SENT),
        scratch_shapes=[pltpu.VMEM((BLK, 32, 128), F32), pltpu.VMEM((16, 64, 128), F32)],
        compiler_params=params(28),
        name="apply_products_" + str(count),
    )(coeffs, products, *kept)


def last_step(copies, scalars, coeffs, kept, legendre, signal, bands):
    (legendre,) = in_hbm(legendre)
    return pl.pallas_call(
        last_kernel,
        out_shape=(
            jax.ShapeDtypeStruct((legendre.shape[0], 512, 128), BF16),
            jax.ShapeDtypeStruct((copies, 2, 128), F32),
        ),
        in_specs=[SMEM] * 3 + [VMEM] * 4 + [ANY, VMEM, VMEM],
        out_specs=(ANY, VMEM),
        scratch_shapes=[
            pltpu.VMEM(legendre.shape, BF16),
            pltpu.VMEM((BLK, 32, 128), F32),
            pltpu.VMEM((9, 128, 128), F32),
            pltpu.VMEM((SLOTS * MG, 128, 64), BF16),
            pltpu.VMEM((16, VEC, 128), F32),
            pltpu.VMEM((legendre.shape[0], 512, 128), BF16),
        ]
        + [
            pltpu.SMEM((SLOTS,), jnp.int32),
            pltpu.SMEM((SLOTS,), jnp.int32),
            pltpu.SemaphoreType.DMA((-(-legendre.shape[0] // GROUP),)),
            pltpu.SemaphoreType.DMA((-(-legendre.shape[0] // GROUP),)),
        ],
        compiler_params=params(28),
        name="last_modes",
    )(*scalars, coeffs, *kept, legendre, signal, bands)


def fisher_step(sim_index, terms):
    return pl.pallas_call(
        fisher_kernel,
        out_shape=(
            jax.ShapeDtypeStruct((8, BANDS), F32),
            jax.ShapeDtypeStruct((BANDS, BANDS), F32),
        ),
        in_specs=[SMEM, VMEM],
        scratch_shapes=[pltpu.VMEM((terms.shape[0] // BLK * 2, 128), F32)],
        compiler_params=params(28),
        name="fisher",
    )(sim_index, terms)


def exchange(rows):
    return lax.all_to_all(rows, "blk", 0, 0, tiled=True)


def shards(sky_maps, noise_weight, signal_inverse, legendre, m_groups, block_list, band_of_ell):
    blk_index = lax.axis_index("blk")
    set_count, sim_local, cycle_local, cycle_pixels = sky_maps.shape
    block_count = legendre.shape[0]
    outer, outer_t, twist, upper = [jnp.asarray(t) for t in constant_tables()]
    sky = sky_maps.reshape(set_count, sim_local, cycle_local, OUTER, INNER)
    sky = sky.transpose(0, 1, 3, 2, 4).reshape(VEC, OUTER * CYC, INNER)
    noise = noise_weight.reshape(CYC, OUTER, INNER).transpose(1, 0, 2).reshape(OUTER * CYC, INNER)
    scalars = (m_groups.T, block_list.T, blk_index.astype(jnp.int32).reshape(1))
    signal = signal_inverse.reshape(16, 128)
    bands = band_of_ell.reshape(16, 128)

    rows, inner, zero_rows = first_transforms(scalars[0], sky, noise, outer, twist, upper)
    own, rows = lax.optimization_barrier((scalars[2], rows))
    products = cycle_products(scalars[:2] + (own,), legendre, signal)
    kept = []
    for sweep in range(ITERS - 1):
        coeffs, rows = apply_products(exchange(rows), products, kept)
        kept.append(coeffs)
        rows = row_transforms(
            sky, noise, outer, outer_t, twist, inner, zero_rows, exchange(rows)
        )
    sims = lax.axis_size("sim")
    state, copies = last_step(BLK * sims, scalars, exchange(rows), kept, legendre, signal, bands)
    terms = lax.all_to_all(copies, ("blk", "sim"), 0, 0, tiled=True)
    sim_index = lax.axis_index("sim").astype(jnp.int32).reshape(1)
    band_proj, fisher = fisher_step(sim_index, terms)
    filtered = state.reshape(block_count, MG, set_count, sim_local, 2, 128)
    return (filtered, band_proj, fisher)


def solution(mesh):
    return jax.shard_map(
        shards,
        mesh=mesh,
        in_specs=(
            P(None, "sim", "blk", None),
            P("blk", None),
            P(),
            P("blk", None, None, None),
            P(),
            P("blk", None),
            P(),
        ),
        out_specs=(P("blk", None, None, "sim", None, None), P("sim", None), P()),
        check_vma=False,
    )
```

```python
import math

import jax
import jax.numpy as jnp
import numpy as np
from jax import lax
from jax.experimental import pallas as pl
from jax.experimental.pallas import tpu as pltpu
from jax.sharding import PartitionSpec as P

NPHI = 4096
BANDS = 32
ITERS = 4
BLK = 32
CYC = 2
VEC = 16
OUTER = 32
INNER = 128
MG = 16
SLOTS = 4
PAIRS = 18
PAIR_GROUP = 3
GROUP = 6
F32 = jnp.float32
BF16 = jnp.bfloat16
PRECISE = lax.Precision.HIGHEST
NT = (((1,), (1,)), ((), ()))
TN = (((0,), (0,)), ((), ()))
NN = (((1,), (0,)), ((), ()))


def split(value):
    high = value.astype(BF16)
    return high, (value - high.astype(F32)).astype(BF16)


def dot(left, right, dims=NN):
    return lax.dot_general(left, right, dims, preferred_element_type=F32)


def precise(left, right, dims=NN):
    return lax.dot_general(left, right, dims, precision=PRECISE, preferred_element_type=F32)


def rounded(value):
    return value.astype(np.float32).astype(jnp.bfloat16)


def constant_tables():
    k = np.arange(OUTER).reshape(2, 1, MG)
    k_rows = np.broadcast_to(k, (2, CYC, MG)).reshape(-1)
    cycle_rows = np.broadcast_to(np.arange(CYC).reshape(1, CYC, 1), (2, CYC, MG)).reshape(-1)
    a_cols = np.repeat(np.arange(OUTER), CYC)
    cycle_cols = np.tile(np.arange(CYC), OUTER)
    angle = 2.0 * np.pi * (k_rows[:, None] * a_cols[None, :] % OUTER) / OUTER
    same = cycle_rows[:, None] == cycle_cols[None, :]
    outer = np.concatenate([np.cos(angle) * same, -np.sin(angle) * same], axis=0)
    twist = 2.0 * np.pi * (k_rows[:, None] * np.arange(INNER)[None, :]) / NPHI
    twist_table = np.stack([np.cos(twist), np.sin(twist)]).astype(np.float32)
    angle = 2.0 * np.pi * (np.arange(64)[:, None] * np.arange(INNER)[None, :] % INNER) / INNER
    cosine, sine = [math.sqrt(2.0 / NPHI) * f(angle) for f in (np.cos, np.sin)]
    upper_table = rounded(np.concatenate([cosine, sine, -sine, cosine], axis=1))
    return rounded(outer), rounded(outer.T), twist_table, upper_table


def column(half, j, p, upper):
    return ((half * 2 + j) * 2 + p) * 2 + upper


def forward_part(field_of, outer_ref, twist_ref, inner_ref, zero_ref, out_ref, turned, staged):
    outer = outer_ref[...]
    cos_twist, sin_twist = twist_ref[0], twist_ref[1]
    for v in range(VEC):
        first = dot(outer, field_of(v).astype(BF16))
        real, imag = first[:64], first[64:]
        turned_real = real * cos_twist + imag * sin_twist
        turned_imag = imag * cos_twist - real * sin_twist
        for half in range(2):
            for cycle in range(CYC):
                at = (half * 2 + cycle) * MG
                rows = pl.ds(cycle * 256 + v, MG, stride=VEC)
                turned[half, 0, rows, :] = turned_real[at : at + MG]
                turned[half, 1, rows, :] = turned_imag[at : at + MG]
    for half in range(2):
        both = jnp.concatenate([turned[half, 0], turned[half, 1]], axis=1)
        coeffs = dot(inner_ref[half], both.astype(BF16), NT)
        if half == 0:
            coeffs = coeffs * zero_scale(zero_ref)
        for j in range(2):
            for p in range(2):
                for upper in range(2):
                    for cycle in range(CYC):
                        row = column(half, j, p, upper) * 2 + cycle
                        lanes = cycle * 256 + upper * 128
                        staged[:, row, :] = coeffs[
                            (j * 2 + p) * 32 : (j * 2 + p + 1) * 32, lanes : lanes + 128
                        ]
    out_ref[...] = staged[...].astype(BF16)


def zero_scale(zero_ref):
    lane = lax.broadcasted_iota(jnp.int32, (128, 512), 1)
    own = jnp.concatenate([zero_ref[...]] * 4, axis=1)
    return jnp.where(jnp.logical_and(lane % 256 < VEC, own > 0.0), math.sqrt(0.5), 1.0)


def fill_inner(group_ref, upper_ref, inner_ref, zero_ref):
    groups = [group_ref[s : s + 1, :] for s in range(SLOTS)]
    halves = [group % 2 for group in groups]
    ranks = []
    for s in range(SLOTS):
        rank = jnp.zeros_like(groups[s])
        for earlier in range(s):
            rank = rank + (halves[earlier] == halves[s]).astype(jnp.int32)
        ranks.append(rank)
    index = lax.broadcasted_iota(jnp.int32, (64, BLK), 0)
    is_first = (lax.broadcasted_iota(jnp.int32, (64, 128), 0) == 0).astype(BF16)
    for half in range(2):
        for j in range(2):
            upper = jnp.zeros_like(groups[0])
            for s in range(SLOTS):
                mine = jnp.logical_and(halves[s] == half, ranks[s] == j)
                upper = upper + jnp.where(mine, groups[s] // 2, 0)
            hot = (index == jnp.broadcast_to(upper, (64, BLK))).astype(F32).astype(BF16)
            rows = dot(hot, upper_ref[...], TN).astype(BF16)
            for p in range(2):
                at = (j * 2 + p) * BLK
                inner_ref[half, at : at + BLK, :] = rows[:, p * 256 : (p + 1) * 256]
            if half == 0:
                zero = dot(hot, is_first, TN)
                for p in range(2):
                    at = (j * 2 + p) * BLK
                    zero_ref[at : at + BLK, :] = zero


def first_rows_kernel(
    group_ref, sky_ref, noise_ref, outer_ref, twist_ref, upper_ref,
    out_ref, inner_ref, zero_ref, turned, staged,
):
    fill_inner(group_ref, upper_ref, inner_ref, zero_ref)
    noise = noise_ref[...]
    forward_part(
        lambda v: noise * sky_ref[v],
        outer_ref, twist_ref, inner_ref, zero_ref, out_ref, turned, staged,
    )


def rows_kernel(
    sky_ref, noise_ref, outer_ref, outer_t_ref, twist_ref, inner_ref, zero_ref, coeff_ref,
    out_ref, turned, staged,
):
    staged[...] = coeff_ref[...].astype(F32)
    for half in range(2):
        rows = []
        for j in range(2):
            for p in range(2):
                rows.append(
                    jnp.concatenate(
                        [
                            staged[:, column(half, j, p, upper) * 2 + cycle, :]
                            for cycle in range(CYC)
                            for upper in range(2)
                        ],
                        axis=1,
                    )
                )
        coeffs = jnp.concatenate(rows, axis=0)
        if half == 0:
            coeffs = coeffs * zero_scale(zero_ref)
        coeffs = coeffs.astype(BF16)
        inner = dot(coeffs, inner_ref[half], TN)
        for i in range(MG):
            at = half * CYC * MG + i
            cos_twist = jnp.broadcast_to(twist_ref[0, at : at + 1], (VEC, 128))
            sin_twist = jnp.broadcast_to(twist_ref[1, at : at + 1], (VEC, 128))
            for cycle in range(CYC):
                rows = slice(cycle * 256 + i * VEC, cycle * 256 + (i + 1) * VEC)
                real, imag = inner[rows, :128], inner[rows, 128:]
                turned[half, 0, rows, :] = real * cos_twist - imag * sin_twist
                turned[half, 1, rows, :] = real * sin_twist + imag * cos_twist
    noise = noise_ref[...]
    outer_t = outer_t_ref[...]
    fields = []
    for v in range(VEC):
        spectrum = jnp.concatenate(
            [
                turned[half, part, pl.ds(cycle * 256 + v, MG, stride=VEC), :]
                for part in range(2)
                for half in range(2)
                for cycle in range(CYC)
            ],
            axis=0,
        )
        fields.append(noise * (sky_ref[v] - dot(outer_t, spectrum.astype(BF16))))
    forward_part(
        lambda v: fields[v],
        outer_ref, twist_ref, inner_ref, zero_ref, out_ref, turned, staged,
    )


def own_slots(group_ref, own_ref):
    own = own_ref[0]
    groups = [group_ref[s, own] for s in range(SLOTS)]
    slots = []
    for s in range(SLOTS):
        half = groups[s] % 2
        rank = jnp.int32(0)
        for earlier in range(s):
            rank = rank + jnp.where(groups[earlier] % 2 == half, 1, 0)
        slots.append((2 * half + rank, groups[s]))
    return slots


def table_copy(legendre_ref, table, arrived, group, size):
    blocks = pl.ds(group * GROUP, size)
    return pltpu.make_async_copy(legendre_ref.at[blocks], table.at[blocks], arrived.at[group])


def by_groups(blocks, step):
    def body(group, carry):
        step(group, GROUP)
        return carry

    lax.fori_loop(0, blocks // GROUP, body, 0)
    if blocks % GROUP:
        step(blocks // GROUP, blocks % GROUP)


def mark_slots(group_ref, own_ref, new_slot, zero_slot):
    for s, (slot, group) in enumerate(own_slots(group_ref, own_ref)):
        new_slot[s] = slot
        zero_slot[s] = jnp.where(group == 0, 1, 0)


def products_kernel(
    group_ref, block_ref, own_ref, legendre_ref, signal_ref, out_ref,
    table, sums, order, sequence, pair_slot, pair_live, counter, arrived,
):
    def place_copy(at):
        return pltpu.make_async_copy(legendre_ref.at[order[at]], table.at[at], arrived.at[at])

    base = jnp.int32(0)
    for s, (slot, group) in enumerate(own_slots(group_ref, own_ref)):
        pairs = (17 - group // 8) // 2
        counter[s] = 2 * base

        def mark(pair, carry, slot=slot):
            pair_slot[pair] = slot
            pair_live[pair] = 1
            return carry

        lax.fori_loop(base, base + pairs, mark, 0)
        base = base + pairs

    def place(block, complete):
        slot = block_ref[0, block]
        at = counter[slot]
        order[at] = block
        counter[slot] = at + 1
        place_copy(at).start()
        sequence[complete] = at // 2
        return complete + at % 2

    complete = lax.fori_loop(0, block_ref.shape[1], place, jnp.int32(0))
    for s in range(SLOTS):
        at = counter[s]
        sequence[complete] = at // 2

        @pl.when(at % 2 == 1)
        def _():
            order[at] = order[at - 1]
            pair_live[at // 2] = 0
            place_copy(at).start()

        complete = complete + at % 2
    sums[...] = jnp.zeros_like(sums)

    def pair_step(group, carry):
        pairs = [sequence[group * PAIR_GROUP + n] for n in range(PAIR_GROUP)]
        for pair in pairs:
            place_copy(2 * pair).wait()
            place_copy(2 * pair + 1).wait()
        slots = [pair_slot[pair] for pair in pairs]
        lives = [pair_live[pair].astype(F32) for pair in pairs]
        degrees = [
            (block_ref[1, order[2 * pair]], block_ref[1, order[2 * pair + 1]]) for pair in pairs
        ]
        for pair, slot, live, (first, second) in zip(pairs, slots, lives, degrees):
            precond = [1.0 / (2.0 + signal_ref[pl.ds(degree, 1), :]) for degree in (first, second)]
            precond = jnp.concatenate(precond, axis=1)
            lane = lax.broadcasted_iota(jnp.int32, (1, 256), 1)
            weight = precond * jnp.where(lane < 128, 1.0, live)
            weights = []
            for _ in range(ITERS - 1):
                weights.append(jnp.broadcast_to(weight, (64, 256)))
                weight = weight * (2.0 * precond)
            for i in range(MG):
                values = jnp.concatenate([table[2 * pair, i], table[2 * pair + 1, i]], axis=1)
                wide = values.astype(F32)
                scaled = jnp.concatenate([(wide * w).astype(BF16) for w in weights], axis=0)
                sums[slot * MG + i] += dot(scaled, values, NT)
        return carry

    lax.fori_loop(0, PAIRS // PAIR_GROUP, pair_step, 0)
    for at in range(SLOTS * MG):
        out_ref[at // 8, (at % 8) * 64 : (at % 8 + 1) * 64, :] = jnp.concatenate(
            [sums[at, n * 64 : (n + 1) * 64] for n in range(ITERS - 1)], axis=1
        ).astype(BF16)


def apply_kernel(count, *refs):
    coeff_ref, product_ref = refs[:2]
    earlier = refs[2 : 1 + count]
    kept_ref, out_ref, staged, ordered = refs[1 + count :]
    staged[...] = coeff_ref[...].astype(F32)
    for c in range(16):
        for cycle in range(CYC):
            ordered[c, pl.ds(cycle, BLK, stride=2), :] = staged[:, 2 * c + cycle, :]
    kept_ref[...] = ordered[...].astype(BF16)
    history = [kept_ref] + list(earlier)[::-1]
    lane = lax.broadcasted_iota(jnp.int32, (64, 256), 1) % 128 // VEC
    for slot in range(SLOTS):
        for upper in range(2):
            at = [(slot * 2 + p) * 2 + upper for p in range(2)]
            right = jnp.concatenate(
                [jnp.concatenate([ref[at[0]], ref[at[1]]], axis=1) for ref in history], axis=0
            )
            mixed = dot(product_ref[slot * 2 + upper, :, : 64 * count], right)
            result = mixed[:64]
            for i in range(1, 8):
                result = jnp.where(lane == i, mixed[i * 64 : (i + 1) * 64], result)
            ordered[at[0]] = result[:, :128]
            ordered[at[1]] = result[:, 128:]
    for c in range(16):
        for cycle in range(CYC):
            staged[:, 2 * c + cycle, :] = ordered[c, pl.ds(cycle, BLK, stride=2), :]
    out_ref[...] = staged[...].astype(BF16)


def last_kernel(
    group_ref, block_ref, own_ref, coeff_ref, kept0_ref, kept1_ref, kept2_ref, legendre_ref,
    signal_ref, band_ref, state_ref, band_out,
    table, staged, mixed, packed, products, outgoing, new_slot, zero_slot, arrived, sent,
):
    blocks = legendre_ref.shape[0]

    by_groups(blocks, lambda g, n: table_copy(legendre_ref, table, arrived, g, n).start())
    mark_slots(group_ref, own_ref, new_slot, zero_slot)
    products[...] = jnp.zeros_like(products)
    staged[...] = coeff_ref[...].astype(F32)
    blank = jnp.zeros((64, 128), BF16)
    unit = (
        lax.broadcasted_iota(jnp.int32, (128, 128), 0)
        == lax.broadcasted_iota(jnp.int32, (128, 128), 1)
    ).astype(BF16)
    for slot in range(SLOTS):
        for upper in range(2):
            for sweep in range(ITERS):
                for p in range(2):
                    c = (slot * 2 + p) * 2 + upper
                    if sweep < ITERS - 1:
                        tile = (kept0_ref, kept1_ref, kept2_ref)[sweep][c]
                    else:
                        for cycle in range(CYC):
                            mixed[0, pl.ds(cycle, BLK, stride=2), :] = staged[:, 2 * c + cycle, :]
                        tile = mixed[0, 0:64, :].astype(BF16)
                    turned = dot(unit, jnp.concatenate([tile, blank], axis=0), NT)
                    for i in range(8):
                        rows = pl.ds(sweep * 32 + p, VEC, stride=2)
                        mixed[1 + i, rows, :] = turned[i * VEC : (i + 1) * VEC]
            for i in range(8):
                packed[slot * MG + upper * 8 + i] = mixed[1 + i, :, 0:64].astype(BF16)

    def out_copy(group, size):
        some = pl.ds(group * GROUP, size)
        return pltpu.make_async_copy(outgoing.at[some], state_ref.at[some], sent.at[group])

    def step(group, size):
        table_copy(legendre_ref, table, arrived, group, size).wait()
        some = [group * GROUP + n for n in range(size)]
        slots = [new_slot[block_ref[0, block]] for block in some]
        halves = [
            jnp.where(zero_slot[block_ref[0, block]] > 0, 0.5, 1.0) for block in some
        ]
        degrees = [block_ref[1, block] for block in some]
        for block, slot, half, degree in zip(some, slots, halves, degrees):
            precond = jnp.broadcast_to(1.0 / (2.0 + signal_ref[pl.ds(degree, 1), :]), (32, 128))
            damp = 2.0 * precond
            total = jnp.zeros((VEC, 128), F32)
            for i in range(MG):
                harmonic = dot(packed[slot * MG + i], table[block, i])
                state = harmonic[0:32]
                for sweep in range(1, ITERS):
                    state = harmonic[sweep * 32 : (sweep + 1) * 32] + damp * state
                state = precond * state
                outgoing[block, i * 32 : (i + 1) * 32, :] = state.astype(BF16)
                one = state[:VEC] * state[VEC:]
                if i == 0:
                    one = one * half
                total = total + one
            products[degree] += 2.0 * total
        out_copy(group, size).start()

    by_groups(blocks, step)
    bins = lax.broadcasted_iota(jnp.int32, (128, 128), 0) % BANDS
    lane = lax.broadcasted_iota(jnp.int32, (VEC, 128), 1)
    row = lax.broadcasted_iota(jnp.int32, (VEC, 128), 0)
    sums = jnp.zeros((80, 128), F32)
    for e in range(16):
        member = (jnp.broadcast_to(band_ref[e : e + 1, :], (128, 128)) == bins).astype(F32)
        high = products[e].astype(BF16)
        middle, low = split(products[e] - high.astype(F32))
        weight = split((2 * (e * 128 + lane) + 1).astype(F32))
        left = jnp.concatenate([high, middle, low, weight[0], weight[1]], axis=0)
        sums = sums + dot(left, member.astype(BF16), NT)
    raw = sums[0:16] + (sums[16:32] + sums[32:48])
    counts = sums[48:64] + sums[64:80]
    terms = jnp.where(lane // BANDS == row // 2 % 4, raw * (1.0 / jnp.sqrt(counts)), 0.0)
    terms = jnp.concatenate(
        [jnp.sum(terms[h * 8 : (h + 1) * 8], axis=0, keepdims=True) for h in range(2)], axis=0
    )
    band_out[...] = jnp.broadcast_to(terms[None], band_out.shape)
    by_groups(blocks, lambda g, n: out_copy(g, n).wait())


def fisher_kernel(sim_ref, term_ref, band_out, fisher_out, rows_ref):
    sims = term_ref.shape[0] // BLK
    for part in range(sims):
        total = term_ref[part]
        for index in range(1, BLK):
            total = total + term_ref[index * sims + part]
        rows_ref[2 * part : 2 * part + 2, :] = total
    values = rows_ref[...]
    count = sims * 8
    total = jnp.sum(values, axis=0, keepdims=True)
    total = jnp.broadcast_to(total, (8, 128))
    total = total + pltpu.roll(total, 64, 1)
    total = total + pltpu.roll(total, 32, 1)
    mean = total[:1] * (1.0 / count)
    center = values - jnp.broadcast_to(mean, values.shape)
    square = precise(center, center, TN)
    fisher = square[:BANDS]
    for s in range(1, 4):
        fisher = fisher + pltpu.roll(square[s * BANDS : (s + 1) * BANDS], 128 - s * BANDS, 1)
    fisher_out[...] = fisher[:, :BANDS] * (1.0 / count)
    own = rows_ref[pl.ds(2 * sim_ref[0], 2), :]
    own = jnp.concatenate([jnp.broadcast_to(own[h : h + 1], (4, 128)) for h in range(2)], axis=0)
    row = lax.broadcasted_iota(jnp.int32, (8, 128), 0) % 4
    band = own
    for s in range(1, 4):
        band = jnp.where(row == s, pltpu.roll(own, 128 - s * BANDS, 1), band)
    band_out[...] = band[:, :BANDS]


def params(megabytes, **more):
    return pltpu.CompilerParams(vmem_limit_bytes=megabytes << 20, **more)


def in_hbm(*arrays):
    return [pltpu.with_memory_space_constraint(array, pltpu.HBM) for array in arrays]


SENT = jax.ShapeDtypeStruct((BLK, 32, 128), BF16)
KEPT = jax.ShapeDtypeStruct((16, 64, 128), BF16)
SMEM = pl.BlockSpec(memory_space=pltpu.SMEM)
VMEM = pl.BlockSpec(memory_space=pltpu.VMEM)
ANY = pl.BlockSpec(memory_space=pl.ANY)


def row_scratch():
    return [pltpu.VMEM((2, 2, 512, 128), F32), pltpu.VMEM((BLK, 32, 128), F32)]


def first_transforms(groups, sky, noise, outer, twist, upper):
    return pl.pallas_call(
        first_rows_kernel,
        out_shape=(
            SENT,
            jax.ShapeDtypeStruct((2, 128, 256), BF16),
            jax.ShapeDtypeStruct((128, 128), F32),
        ),
        scratch_shapes=row_scratch(),
        compiler_params=params(28),
        name="first_rows",
    )(*in_hbm(groups, sky, noise, outer, twist, upper))


def row_transforms(sky, noise, outer, outer_t, twist, inner, zero_rows, coeffs):
    return pl.pallas_call(
        rows_kernel,
        out_shape=SENT,
        scratch_shapes=row_scratch(),
        compiler_params=params(28),
        name="rows",
    )(sky, noise, outer, outer_t, twist, inner, zero_rows, coeffs)


def cycle_products(scalars, legendre, signal):
    return pl.pallas_call(
        products_kernel,
        out_shape=jax.ShapeDtypeStruct((8, 512, 192), BF16),
        in_specs=[SMEM, SMEM, SMEM, ANY, VMEM],
        scratch_shapes=[
            pltpu.VMEM((2 * PAIRS,) + legendre.shape[1:], BF16),
            pltpu.VMEM((SLOTS * MG, 192, 64), F32),
            pltpu.SMEM((2 * PAIRS,), jnp.int32),
            pltpu.SMEM((PAIRS + 2,), jnp.int32),
            pltpu.SMEM((PAIRS,), jnp.int32),
            pltpu.SMEM((PAIRS,), jnp.int32),
            pltpu.SMEM((SLOTS,), jnp.int32),
            pltpu.SemaphoreType.DMA((2 * PAIRS,)),
        ],
        compiler_params=params(28),
        name="cycle_products",
    )(*in_hbm(*scalars, legendre, signal))


def apply_products(coeffs, products, kept):
    count = len(kept) + 1

    def body(*refs):
        apply_kernel(count, *refs)

    return pl.pallas_call(
        body,
        out_shape=(KEPT, SENT),
        scratch_shapes=[pltpu.VMEM((BLK, 32, 128), F32), pltpu.VMEM((16, 64, 128), F32)],
        compiler_params=params(28),
        name="apply_products_" + str(count),
    )(coeffs, products, *kept)


def last_step(copies, scalars, coeffs, kept, legendre, signal, bands):
    (legendre,) = in_hbm(legendre)
    return pl.pallas_call(
        last_kernel,
        out_shape=(
            jax.ShapeDtypeStruct((legendre.shape[0], 512, 128), BF16),
            jax.ShapeDtypeStruct((copies, 2, 128), F32),
        ),
        in_specs=[SMEM] * 3 + [VMEM] * 4 + [ANY, VMEM, VMEM],
        out_specs=(ANY, VMEM),
        scratch_shapes=[
            pltpu.VMEM(legendre.shape, BF16),
            pltpu.VMEM((BLK, 32, 128), F32),
            pltpu.VMEM((9, 128, 128), F32),
            pltpu.VMEM((SLOTS * MG, 128, 64), BF16),
            pltpu.VMEM((16, VEC, 128), F32),
            pltpu.VMEM((legendre.shape[0], 512, 128), BF16),
        ]
        + [
            pltpu.SMEM((SLOTS,), jnp.int32),
            pltpu.SMEM((SLOTS,), jnp.int32),
            pltpu.SemaphoreType.DMA((-(-legendre.shape[0] // GROUP),)),
            pltpu.SemaphoreType.DMA((-(-legendre.shape[0] // GROUP),)),
        ],
        compiler_params=params(28),
        name="last_modes",
    )(*scalars, coeffs, *kept, legendre, signal, bands)


def fisher_step(sim_index, terms):
    return pl.pallas_call(
        fisher_kernel,
        out_shape=(
            jax.ShapeDtypeStruct((8, BANDS), F32),
            jax.ShapeDtypeStruct((BANDS, BANDS), F32),
        ),
        in_specs=[SMEM, VMEM],
        scratch_shapes=[pltpu.VMEM((terms.shape[0] // BLK * 2, 128), F32)],
        compiler_params=params(28),
        name="fisher",
    )(sim_index, terms)


def exchange(rows):
    return lax.all_to_all(rows, "blk", 0, 0, tiled=True)


def shards(sky_maps, noise_weight, signal_inverse, legendre, m_groups, block_list, band_of_ell):
    blk_index = lax.axis_index("blk")
    set_count, sim_local, cycle_local, cycle_pixels = sky_maps.shape
    block_count = legendre.shape[0]
    outer, outer_t, twist, upper = [jnp.asarray(t) for t in constant_tables()]
    sky = sky_maps.reshape(set_count, sim_local, cycle_local, OUTER, INNER)
    sky = sky.transpose(0, 1, 3, 2, 4).reshape(VEC, OUTER * CYC, INNER)
    noise = noise_weight.reshape(CYC, OUTER, INNER).transpose(1, 0, 2).reshape(OUTER * CYC, INNER)
    scalars = (m_groups.T, block_list.T, blk_index.astype(jnp.int32).reshape(1))
    signal = signal_inverse.reshape(16, 128)
    bands = band_of_ell.reshape(16, 128)

    rows, inner, zero_rows = first_transforms(scalars[0], sky, noise, outer, twist, upper)
    sim_index = lax.axis_index("sim").astype(jnp.int32).reshape(1)
    own, sim_index, rows = lax.optimization_barrier((scalars[2], sim_index, rows))
    products = cycle_products(scalars[:2] + (own,), legendre, signal)
    kept = []
    for sweep in range(ITERS - 1):
        coeffs, rows = apply_products(exchange(rows), products, kept)
        kept.append(coeffs)
        rows = row_transforms(
            sky, noise, outer, outer_t, twist, inner, zero_rows, exchange(rows)
        )
    sims = lax.axis_size("sim")
    state, copies = last_step(BLK * sims, scalars, exchange(rows), kept, legendre, signal, bands)
    terms = lax.all_to_all(copies, ("blk", "sim"), 0, 0, tiled=True)
    band_proj, fisher = fisher_step(sim_index, terms)
    filtered = state.reshape(block_count, MG, set_count, sim_local, 2, 128)
    return (filtered, band_proj, fisher)


def solution(mesh):
    return jax.shard_map(
        shards,
        mesh=mesh,
        in_specs=(
            P(None, "sim", "blk", None),
            P("blk", None),
            P(),
            P("blk", None, None, None),
            P(),
            P("blk", None),
            P(),
        ),
        out_specs=(P("blk", None, None, "sim", None, None), P("sim", None), P()),
        check_vma=False,
    )
```

```python
import math

import jax
import jax.numpy as jnp
import numpy as np
from jax import lax
from jax.experimental import pallas as pl
from jax.experimental.pallas import tpu as pltpu
from jax.sharding import PartitionSpec as P

NPHI = 4096
BANDS = 32
ITERS = 4
BLK = 32
CYC = 2
VEC = 16
OUTER = 32
INNER = 128
MG = 16
SLOTS = 4
PAIRS = 18
PAIR_GROUP = 6
GROUP = 6
F32 = jnp.float32
BF16 = jnp.bfloat16
PRECISE = lax.Precision.HIGHEST
NT = (((1,), (1,)), ((), ()))
TN = (((0,), (0,)), ((), ()))
NN = (((1,), (0,)), ((), ()))


def split(value):
    high = value.astype(BF16)
    return high, (value - high.astype(F32)).astype(BF16)


def dot(left, right, dims=NN):
    return lax.dot_general(left, right, dims, preferred_element_type=F32)


def precise(left, right, dims=NN):
    return lax.dot_general(left, right, dims, precision=PRECISE, preferred_element_type=F32)


def rounded(value):
    return value.astype(np.float32).astype(jnp.bfloat16)


def constant_tables():
    k = np.arange(OUTER).reshape(2, 1, MG)
    k_rows = np.broadcast_to(k, (2, CYC, MG)).reshape(-1)
    cycle_rows = np.broadcast_to(np.arange(CYC).reshape(1, CYC, 1), (2, CYC, MG)).reshape(-1)
    a_cols = np.repeat(np.arange(OUTER), CYC)
    cycle_cols = np.tile(np.arange(CYC), OUTER)
    angle = 2.0 * np.pi * (k_rows[:, None] * a_cols[None, :] % OUTER) / OUTER
    same = cycle_rows[:, None] == cycle_cols[None, :]
    outer = np.concatenate([np.cos(angle) * same, -np.sin(angle) * same], axis=0)
    twist = 2.0 * np.pi * (k_rows[:, None] * np.arange(INNER)[None, :]) / NPHI
    twist_table = np.stack([np.cos(twist), np.sin(twist)]).astype(np.float32)
    angle = 2.0 * np.pi * (np.arange(64)[:, None] * np.arange(INNER)[None, :] % INNER) / INNER
    cosine, sine = [math.sqrt(2.0 / NPHI) * f(angle) for f in (np.cos, np.sin)]
    upper_table = rounded(np.concatenate([cosine, sine, -sine, cosine], axis=1))
    return rounded(outer), rounded(outer.T), twist_table, upper_table


def column(half, j, p, upper):
    return ((half * 2 + j) * 2 + p) * 2 + upper


def forward_part(field_of, outer_ref, twist_ref, inner_ref, zero_ref, out_ref, turned, staged):
    outer = outer_ref[...]
    cos_twist, sin_twist = twist_ref[0], twist_ref[1]
    for v in range(VEC):
        first = dot(outer, field_of(v).astype(BF16))
        real, imag = first[:64], first[64:]
        turned_real = real * cos_twist + imag * sin_twist
        turned_imag = imag * cos_twist - real * sin_twist
        for half in range(2):
            for cycle in range(CYC):
                at = (half * 2 + cycle) * MG
                rows = pl.ds(cycle * 256 + v, MG, stride=VEC)
                turned[half, 0, rows, :] = turned_real[at : at + MG]
                turned[half, 1, rows, :] = turned_imag[at : at + MG]
    for half in range(2):
        both = jnp.concatenate([turned[half, 0], turned[half, 1]], axis=1)
        coeffs = dot(inner_ref[half], both.astype(BF16), NT)
        if half == 0:
            coeffs = coeffs * zero_scale(zero_ref)
        for j in range(2):
            for p in range(2):
                for upper in range(2):
                    for cycle in range(CYC):
                        row = column(half, j, p, upper) * 2 + cycle
                        lanes = cycle * 256 + upper * 128
                        staged[:, row, :] = coeffs[
                            (j * 2 + p) * 32 : (j * 2 + p + 1) * 32, lanes : lanes + 128
                        ]
    out_ref[...] = staged[...].astype(BF16)


def zero_scale(zero_ref):
    lane = lax.broadcasted_iota(jnp.int32, (128, 512), 1)
    own = jnp.concatenate([zero_ref[...]] * 4, axis=1)
    return jnp.where(jnp.logical_and(lane % 256 < VEC, own > 0.0), math.sqrt(0.5), 1.0)


def fill_inner(group_ref, upper_ref, inner_ref, zero_ref):
    groups = [group_ref[s : s + 1, :] for s in range(SLOTS)]
    halves = [group % 2 for group in groups]
    ranks = []
    for s in range(SLOTS):
        rank = jnp.zeros_like(groups[s])
        for earlier in range(s):
            rank = rank + (halves[earlier] == halves[s]).astype(jnp.int32)
        ranks.append(rank)
    index = lax.broadcasted_iota(jnp.int32, (64, BLK), 0)
    is_first = (lax.broadcasted_iota(jnp.int32, (64, 128), 0) == 0).astype(BF16)
    for half in range(2):
        for j in range(2):
            upper = jnp.zeros_like(groups[0])
            for s in range(SLOTS):
                mine = jnp.logical_and(halves[s] == half, ranks[s] == j)
                upper = upper + jnp.where(mine, groups[s] // 2, 0)
            hot = (index == jnp.broadcast_to(upper, (64, BLK))).astype(F32).astype(BF16)
            rows = dot(hot, upper_ref[...], TN).astype(BF16)
            for p in range(2):
                at = (j * 2 + p) * BLK
                inner_ref[half, at : at + BLK, :] = rows[:, p * 256 : (p + 1) * 256]
            if half == 0:
                zero = dot(hot, is_first, TN)
                for p in range(2):
                    at = (j * 2 + p) * BLK
                    zero_ref[at : at + BLK, :] = zero


def first_rows_kernel(
    group_ref, sky_ref, noise_ref, outer_ref, twist_ref, upper_ref,
    out_ref, inner_ref, zero_ref, turned, staged,
):
    fill_inner(group_ref, upper_ref, inner_ref, zero_ref)
    noise = noise_ref[...]
    forward_part(
        lambda v: noise * sky_ref[v],
        outer_ref, twist_ref, inner_ref, zero_ref, out_ref, turned, staged,
    )


def rows_kernel(
    sky_ref, noise_ref, outer_ref, outer_t_ref, twist_ref, inner_ref, zero_ref, coeff_ref,
    out_ref, turned, staged,
):
    staged[...] = coeff_ref[...].astype(F32)
    for half in range(2):
        rows = []
        for j in range(2):
            for p in range(2):
                rows.append(
                    jnp.concatenate(
                        [
                            staged[:, column(half, j, p, upper) * 2 + cycle, :]
                            for cycle in range(CYC)
                            for upper in range(2)
                        ],
                        axis=1,
                    )
                )
        coeffs = jnp.concatenate(rows, axis=0)
        if half == 0:
            coeffs = coeffs * zero_scale(zero_ref)
        coeffs = coeffs.astype(BF16)
        inner = dot(coeffs, inner_ref[half], TN)
        for i in range(MG):
            at = half * CYC * MG + i
            cos_twist = jnp.broadcast_to(twist_ref[0, at : at + 1], (VEC, 128))
            sin_twist = jnp.broadcast_to(twist_ref[1, at : at + 1], (VEC, 128))
            for cycle in range(CYC):
                rows = slice(cycle * 256 + i * VEC, cycle * 256 + (i + 1) * VEC)
                real, imag = inner[rows, :128], inner[rows, 128:]
                turned[half, 0, rows, :] = real * cos_twist - imag * sin_twist
                turned[half, 1, rows, :] = real * sin_twist + imag * cos_twist
    noise = noise_ref[...]
    outer_t = outer_t_ref[...]
    fields = []
    for v in range(VEC):
        spectrum = jnp.concatenate(
            [
                turned[half, part, pl.ds(cycle * 256 + v, MG, stride=VEC), :]
                for part in range(2)
                for half in range(2)
                for cycle in range(CYC)
            ],
            axis=0,
        )
        fields.append(noise * (sky_ref[v] - dot(outer_t, spectrum.astype(BF16))))
    forward_part(
        lambda v: fields[v],
        outer_ref, twist_ref, inner_ref, zero_ref, out_ref, turned, staged,
    )


def own_slots(group_ref, own_ref):
    own = own_ref[0]
    groups = [group_ref[s, own] for s in range(SLOTS)]
    slots = []
    for s in range(SLOTS):
        half = groups[s] % 2
        rank = jnp.int32(0)
        for earlier in range(s):
            rank = rank + jnp.where(groups[earlier] % 2 == half, 1, 0)
        slots.append((2 * half + rank, groups[s]))
    return slots


def table_copy(legendre_ref, table, arrived, group, size):
    blocks = pl.ds(group * GROUP, size)
    return pltpu.make_async_copy(legendre_ref.at[blocks], table.at[blocks], arrived.at[group])


def by_groups(blocks, step):
    def body(group, carry):
        step(group, GROUP)
        return carry

    lax.fori_loop(0, blocks // GROUP, body, 0)
    if blocks % GROUP:
        step(blocks // GROUP, blocks % GROUP)


def mark_slots(group_ref, own_ref, new_slot, zero_slot):
    for s, (slot, group) in enumerate(own_slots(group_ref, own_ref)):
        new_slot[s] = slot
        zero_slot[s] = jnp.where(group == 0, 1, 0)


def products_kernel(
    group_ref, block_ref, own_ref, legendre_ref, signal_ref, out_ref,
    table, sums, order, sequence, pair_slot, pair_live, counter, arrived,
):
    def place_copy(at):
        return pltpu.make_async_copy(legendre_ref.at[order[at]], table.at[at], arrived.at[at])

    base = jnp.int32(0)
    for s, (slot, group) in enumerate(own_slots(group_ref, own_ref)):
        pairs = (17 - group // 8) // 2
        counter[s] = 2 * base

        def mark(pair, carry, slot=slot):
            pair_slot[pair] = slot
            pair_live[pair] = 1
            return carry

        lax.fori_loop(base, base + pairs, mark, 0)
        base = base + pairs

    def place(block, complete):
        slot = block_ref[0, block]
        at = counter[slot]
        order[at] = block
        counter[slot] = at + 1
        place_copy(at).start()
        sequence[complete] = at // 2
        return complete + at % 2

    complete = lax.fori_loop(0, block_ref.shape[1], place, jnp.int32(0))
    for s in range(SLOTS):
        at = counter[s]
        sequence[complete] = at // 2

        @pl.when(at % 2 == 1)
        def _():
            order[at] = order[at - 1]
            pair_live[at // 2] = 0
            place_copy(at).start()

        complete = complete + at % 2
    sums[...] = jnp.zeros_like(sums)

    def pair_step(group, carry):
        pairs = [sequence[group * PAIR_GROUP + n] for n in range(PAIR_GROUP)]
        for pair in pairs:
            place_copy(2 * pair).wait()
            place_copy(2 * pair + 1).wait()
        slots = [pair_slot[pair] for pair in pairs]
        lives = [pair_live[pair].astype(F32) for pair in pairs]
        degrees = [
            (block_ref[1, order[2 * pair]], block_ref[1, order[2 * pair + 1]]) for pair in pairs
        ]
        for pair, slot, live, (first, second) in zip(pairs, slots, lives, degrees):
            precond = [1.0 / (2.0 + signal_ref[pl.ds(degree, 1), :]) for degree in (first, second)]
            precond = jnp.concatenate(precond, axis=1)
            lane = lax.broadcasted_iota(jnp.int32, (1, 256), 1)
            weight = precond * jnp.where(lane < 128, 1.0, live)
            weights = [weight, weight * (2.0 * precond)]
            weights = [jnp.broadcast_to(w, (64, 256)) for w in weights]
            for i in range(MG):
                values = jnp.concatenate([table[2 * pair, i], table[2 * pair + 1, i]], axis=1)
                wide = values.astype(F32)
                once, twice = [(wide * w).astype(BF16) for w in weights]
                left = jnp.concatenate([once, twice], axis=0)
                right = jnp.concatenate([values, once], axis=0)
                sums[slot * MG + i] += dot(left, right, NT)
        return carry

    lax.fori_loop(0, PAIRS // PAIR_GROUP, pair_step, 0)
    lane = lax.broadcasted_iota(jnp.int32, (64, 128), 1)
    double = jnp.where(lane < 64, 1.0, 2.0)
    for at in range(SLOTS * MG):
        rows = slice((at % 8) * 64, (at % 8 + 1) * 64)
        out_ref[at // 8, rows, 0:128] = (sums[at, 0:64] * double).astype(BF16)
        out_ref[at // 8, rows, 128:192] = pltpu.roll(2.0 * sums[at, 64:128], 64, 1)[:, :64].astype(BF16)


def apply_kernel(count, *refs):
    coeff_ref, product_ref = refs[:2]
    earlier = refs[2 : 1 + count]
    kept_ref, out_ref, staged, ordered = refs[1 + count :]
    staged[...] = coeff_ref[...].astype(F32)
    for c in range(16):
        for cycle in range(CYC):
            ordered[c, pl.ds(cycle, BLK, stride=2), :] = staged[:, 2 * c + cycle, :]
    kept_ref[...] = ordered[...].astype(BF16)
    history = [kept_ref] + list(earlier)[::-1]
    lane = lax.broadcasted_iota(jnp.int32, (64, 256), 1) % 128 // VEC
    for slot in range(SLOTS):
        for upper in range(2):
            at = [(slot * 2 + p) * 2 + upper for p in range(2)]
            right = jnp.concatenate(
                [jnp.concatenate([ref[at[0]], ref[at[1]]], axis=1) for ref in history], axis=0
            )
            mixed = dot(product_ref[slot * 2 + upper, :, : 64 * count], right)
            result = mixed[:64]
            for i in range(1, 8):
                result = jnp.where(lane == i, mixed[i * 64 : (i + 1) * 64], result)
            ordered[at[0]] = result[:, :128]
            ordered[at[1]] = result[:, 128:]
    for c in range(16):
        for cycle in range(CYC):
            staged[:, 2 * c + cycle, :] = ordered[c, pl.ds(cycle, BLK, stride=2), :]
    out_ref[...] = staged[...].astype(BF16)


def last_kernel(
    group_ref, block_ref, own_ref, coeff_ref, kept0_ref, kept1_ref, kept2_ref, legendre_ref,
    signal_ref, band_ref, state_ref, band_out,
    table, staged, mixed, packed, products, outgoing, new_slot, zero_slot, arrived, sent,
):
    blocks = legendre_ref.shape[0]

    by_groups(blocks, lambda g, n: table_copy(legendre_ref, table, arrived, g, n).start())
    mark_slots(group_ref, own_ref, new_slot, zero_slot)
    products[...] = jnp.zeros_like(products)
    staged[...] = coeff_ref[...].astype(F32)
    blank = jnp.zeros((64, 128), BF16)
    unit = (
        lax.broadcasted_iota(jnp.int32, (128, 128), 0)
        == lax.broadcasted_iota(jnp.int32, (128, 128), 1)
    ).astype(BF16)
    for slot in range(SLOTS):
        for upper in range(2):
            for sweep in range(ITERS):
                for p in range(2):
                    c = (slot * 2 + p) * 2 + upper
                    if sweep < ITERS - 1:
                        tile = (kept0_ref, kept1_ref, kept2_ref)[sweep][c]
                    else:
                        for cycle in range(CYC):
                            mixed[0, pl.ds(cycle, BLK, stride=2), :] = staged[:, 2 * c + cycle, :]
                        tile = mixed[0, 0:64, :].astype(BF16)
                    turned = dot(unit, jnp.concatenate([tile, blank], axis=0), NT)
                    for i in range(8):
                        rows = pl.ds(sweep * 32 + p, VEC, stride=2)
                        mixed[1 + i, rows, :] = turned[i * VEC : (i + 1) * VEC]
            for i in range(8):
                packed[slot * MG + upper * 8 + i] = mixed[1 + i, :, 0:64].astype(BF16)

    def out_copy(group, size):
        some = pl.ds(group * GROUP, size)
        return pltpu.make_async_copy(outgoing.at[some], state_ref.at[some], sent.at[group])

    def step(group, size):
        table_copy(legendre_ref, table, arrived, group, size).wait()
        some = [group * GROUP + n for n in range(size)]
        slots = [new_slot[block_ref[0, block]] for block in some]
        halves = [
            jnp.where(zero_slot[block_ref[0, block]] > 0, 0.5, 1.0) for block in some
        ]
        degrees = [block_ref[1, block] for block in some]
        for block, slot, half, degree in zip(some, slots, halves, degrees):
            precond = jnp.broadcast_to(1.0 / (2.0 + signal_ref[pl.ds(degree, 1), :]), (32, 128))
            damp = 2.0 * precond
            total = jnp.zeros((VEC, 128), F32)
            for i in range(MG):
                harmonic = dot(packed[slot * MG + i], table[block, i])
                state = harmonic[0:32]
                for sweep in range(1, ITERS):
                    state = harmonic[sweep * 32 : (sweep + 1) * 32] + damp * state
                state = precond * state
                outgoing[block, i * 32 : (i + 1) * 32, :] = state.astype(BF16)
                one = state[:VEC] * state[VEC:]
                if i == 0:
                    one = one * half
                total = total + one
            products[degree] += 2.0 * total
        out_copy(group, size).start()

    by_groups(blocks, step)
    bins = lax.broadcasted_iota(jnp.int32, (128, 128), 0) % BANDS
    lane = lax.broadcasted_iota(jnp.int32, (VEC, 128), 1)
    row = lax.broadcasted_iota(jnp.int32, (VEC, 128), 0)
    sums = jnp.zeros((80, 128), F32)
    for e in range(16):
        member = (jnp.broadcast_to(band_ref[e : e + 1, :], (128, 128)) == bins).astype(F32)
        high = products[e].astype(BF16)
        middle, low = split(products[e] - high.astype(F32))
        weight = split((2 * (e * 128 + lane) + 1).astype(F32))
        left = jnp.concatenate([high, middle, low, weight[0], weight[1]], axis=0)
        sums = sums + dot(left, member.astype(BF16), NT)
    raw = sums[0:16] + (sums[16:32] + sums[32:48])
    counts = sums[48:64] + sums[64:80]
    terms = jnp.where(lane // BANDS == row // 2 % 4, raw * (1.0 / jnp.sqrt(counts)), 0.0)
    terms = jnp.concatenate(
        [jnp.sum(terms[h * 8 : (h + 1) * 8], axis=0, keepdims=True) for h in range(2)], axis=0
    )
    band_out[...] = jnp.broadcast_to(terms[None], band_out.shape)
    by_groups(blocks, lambda g, n: out_copy(g, n).wait())


def fisher_kernel(sim_ref, term_ref, band_out, fisher_out, rows_ref):
    sims = term_ref.shape[0] // BLK
    for part in range(sims):
        total = term_ref[part]
        for index in range(1, BLK):
            total = total + term_ref[index * sims + part]
        rows_ref[2 * part : 2 * part + 2, :] = total
    values = rows_ref[...]
    count = sims * 8
    total = jnp.sum(values, axis=0, keepdims=True)
    total = jnp.broadcast_to(total, (8, 128))
    total = total + pltpu.roll(total, 64, 1)
    total = total + pltpu.roll(total, 32, 1)
    mean = total[:1] * (1.0 / count)
    center = values - jnp.broadcast_to(mean, values.shape)
    square = precise(center, center, TN)
    fisher = square[:BANDS]
    for s in range(1, 4):
        fisher = fisher + pltpu.roll(square[s * BANDS : (s + 1) * BANDS], 128 - s * BANDS, 1)
    fisher_out[...] = fisher[:, :BANDS] * (1.0 / count)
    own = rows_ref[pl.ds(2 * sim_ref[0], 2), :]
    own = jnp.concatenate([jnp.broadcast_to(own[h : h + 1], (4, 128)) for h in range(2)], axis=0)
    row = lax.broadcasted_iota(jnp.int32, (8, 128), 0) % 4
    band = own
    for s in range(1, 4):
        band = jnp.where(row == s, pltpu.roll(own, 128 - s * BANDS, 1), band)
    band_out[...] = band[:, :BANDS]


def params(megabytes, **more):
    return pltpu.CompilerParams(vmem_limit_bytes=megabytes << 20, **more)


def in_hbm(*arrays):
    return [pltpu.with_memory_space_constraint(array, pltpu.HBM) for array in arrays]


SENT = jax.ShapeDtypeStruct((BLK, 32, 128), BF16)
KEPT = jax.ShapeDtypeStruct((16, 64, 128), BF16)
SMEM = pl.BlockSpec(memory_space=pltpu.SMEM)
VMEM = pl.BlockSpec(memory_space=pltpu.VMEM)
ANY = pl.BlockSpec(memory_space=pl.ANY)


def row_scratch():
    return [pltpu.VMEM((2, 2, 512, 128), F32), pltpu.VMEM((BLK, 32, 128), F32)]


def first_transforms(groups, sky, noise, outer, twist, upper):
    return pl.pallas_call(
        first_rows_kernel,
        out_shape=(
            SENT,
            jax.ShapeDtypeStruct((2, 128, 256), BF16),
            jax.ShapeDtypeStruct((128, 128), F32),
        ),
        scratch_shapes=row_scratch(),
        compiler_params=params(28),
        name="first_rows",
    )(*in_hbm(groups, sky, noise, outer, twist, upper))


def row_transforms(sky, noise, outer, outer_t, twist, inner, zero_rows, coeffs):
    return pl.pallas_call(
        rows_kernel,
        out_shape=SENT,
        scratch_shapes=row_scratch(),
        compiler_params=params(28),
        name="rows",
    )(sky, noise, outer, outer_t, twist, inner, zero_rows, coeffs)


def cycle_products(scalars, legendre, signal):
    return pl.pallas_call(
        products_kernel,
        out_shape=jax.ShapeDtypeStruct((8, 512, 192), BF16),
        in_specs=[SMEM, SMEM, SMEM, ANY, VMEM],
        scratch_shapes=[
            pltpu.VMEM((2 * PAIRS,) + legendre.shape[1:], BF16),
            pltpu.VMEM((SLOTS * MG, 128, 128), F32),
            pltpu.SMEM((2 * PAIRS,), jnp.int32),
            pltpu.SMEM((PAIRS + 2,), jnp.int32),
            pltpu.SMEM((PAIRS,), jnp.int32),
            pltpu.SMEM((PAIRS,), jnp.int32),
            pltpu.SMEM((SLOTS,), jnp.int32),
            pltpu.SemaphoreType.DMA((2 * PAIRS,)),
        ],
        compiler_params=params(28),
        name="cycle_products",
    )(*in_hbm(*scalars, legendre, signal))


def apply_products(coeffs, products, kept):
    count = len(kept) + 1

    def body(*refs):
        apply_kernel(count, *refs)

    return pl.pallas_call(
        body,
        out_shape=(KEPT, SENT),
        scratch_shapes=[pltpu.VMEM((BLK, 32, 128), F32), pltpu.VMEM((16, 64, 128), F32)],
        compiler_params=params(28),
        name="apply_products_" + str(count),
    )(coeffs, products, *kept)


def last_step(copies, scalars, coeffs, kept, legendre, signal, bands):
    (legendre,) = in_hbm(legendre)
    return pl.pallas_call(
        last_kernel,
        out_shape=(
            jax.ShapeDtypeStruct((legendre.shape[0], 512, 128), BF16),
            jax.ShapeDtypeStruct((copies, 2, 128), F32),
        ),
        in_specs=[SMEM] * 3 + [VMEM] * 4 + [ANY, VMEM, VMEM],
        out_specs=(ANY, VMEM),
        scratch_shapes=[
            pltpu.VMEM(legendre.shape, BF16),
            pltpu.VMEM((BLK, 32, 128), F32),
            pltpu.VMEM((9, 128, 128), F32),
            pltpu.VMEM((SLOTS * MG, 128, 64), BF16),
            pltpu.VMEM((16, VEC, 128), F32),
            pltpu.VMEM((legendre.shape[0], 512, 128), BF16),
        ]
        + [
            pltpu.SMEM((SLOTS,), jnp.int32),
            pltpu.SMEM((SLOTS,), jnp.int32),
            pltpu.SemaphoreType.DMA((-(-legendre.shape[0] // GROUP),)),
            pltpu.SemaphoreType.DMA((-(-legendre.shape[0] // GROUP),)),
        ],
        compiler_params=params(28),
        name="last_modes",
    )(*scalars, coeffs, *kept, legendre, signal, bands)


def fisher_step(sim_index, terms):
    return pl.pallas_call(
        fisher_kernel,
        out_shape=(
            jax.ShapeDtypeStruct((8, BANDS), F32),
            jax.ShapeDtypeStruct((BANDS, BANDS), F32),
        ),
        in_specs=[SMEM, VMEM],
        scratch_shapes=[pltpu.VMEM((terms.shape[0] // BLK * 2, 128), F32)],
        compiler_params=params(28),
        name="fisher",
    )(sim_index, terms)


def exchange(rows):
    return lax.all_to_all(rows, "blk", 0, 0, tiled=True)


def shards(sky_maps, noise_weight, signal_inverse, legendre, m_groups, block_list, band_of_ell):
    blk_index = lax.axis_index("blk")
    set_count, sim_local, cycle_local, cycle_pixels = sky_maps.shape
    block_count = legendre.shape[0]
    outer, outer_t, twist, upper = [jnp.asarray(t) for t in constant_tables()]
    sky = sky_maps.reshape(set_count, sim_local, cycle_local, OUTER, INNER)
    sky = sky.transpose(0, 1, 3, 2, 4).reshape(VEC, OUTER * CYC, INNER)
    noise = noise_weight.reshape(CYC, OUTER, INNER).transpose(1, 0, 2).reshape(OUTER * CYC, INNER)
    scalars = (m_groups.T, block_list.T, blk_index.astype(jnp.int32).reshape(1))
    signal = signal_inverse.reshape(16, 128)
    bands = band_of_ell.reshape(16, 128)

    rows, inner, zero_rows = first_transforms(scalars[0], sky, noise, outer, twist, upper)
    sim_index = lax.axis_index("sim").astype(jnp.int32).reshape(1)
    own, sim_index, rows = lax.optimization_barrier((scalars[2], sim_index, rows))
    products = cycle_products(scalars[:2] + (own,), legendre, signal)
    kept = []
    for sweep in range(ITERS - 1):
        coeffs, rows = apply_products(exchange(rows), products, kept)
        kept.append(coeffs)
        rows = row_transforms(
            sky, noise, outer, outer_t, twist, inner, zero_rows, exchange(rows)
        )
    sims = lax.axis_size("sim")
    state, copies = last_step(BLK * sims, scalars, exchange(rows), kept, legendre, signal, bands)
    terms = lax.all_to_all(copies, ("blk", "sim"), 0, 0, tiled=True)
    band_proj, fisher = fisher_step(sim_index, terms)
    filtered = state.reshape(block_count, MG, set_count, sim_local, 2, 128)
    return (filtered, band_proj, fisher)


def solution(mesh):
    return jax.shard_map(
        shards,
        mesh=mesh,
        in_specs=(
            P(None, "sim", "blk", None),
            P("blk", None),
            P(),
            P("blk", None, None, None),
            P(),
            P("blk", None),
            P(),
        ),
        out_specs=(P("blk", None, None, "sim", None, None), P("sim", None), P()),
        check_vma=False,
    )
```

```python
import math

import jax
import jax.numpy as jnp
import numpy as np
from jax import lax
from jax.experimental import pallas as pl
from jax.experimental.pallas import tpu as pltpu
from jax.sharding import PartitionSpec as P

NPHI = 4096
BANDS = 32
ITERS = 4
BLK = 32
CYC = 2
VEC = 16
OUTER = 32
INNER = 128
MG = 16
SLOTS = 4
PAIRS = 18
PAIR_GROUP = 6
GROUP = 6
F32 = jnp.float32
BF16 = jnp.bfloat16
PRECISE = lax.Precision.HIGHEST
NT = (((1,), (1,)), ((), ()))
TN = (((0,), (0,)), ((), ()))
NN = (((1,), (0,)), ((), ()))


def split(value):
    high = value.astype(BF16)
    return high, (value - high.astype(F32)).astype(BF16)


def dot(left, right, dims=NN):
    return lax.dot_general(left, right, dims, preferred_element_type=F32)


def precise(left, right, dims=NN):
    return lax.dot_general(left, right, dims, precision=PRECISE, preferred_element_type=F32)


def rounded(value):
    return value.astype(np.float32).astype(jnp.bfloat16)


def constant_tables():
    k = np.arange(OUTER).reshape(2, 1, MG)
    k_rows = np.broadcast_to(k, (2, CYC, MG)).reshape(-1)
    cycle_rows = np.broadcast_to(np.arange(CYC).reshape(1, CYC, 1), (2, CYC, MG)).reshape(-1)
    a_cols = np.repeat(np.arange(OUTER), CYC)
    cycle_cols = np.tile(np.arange(CYC), OUTER)
    angle = 2.0 * np.pi * (k_rows[:, None] * a_cols[None, :] % OUTER) / OUTER
    same = cycle_rows[:, None] == cycle_cols[None, :]
    outer = np.concatenate([np.cos(angle) * same, -np.sin(angle) * same], axis=0)
    twist = 2.0 * np.pi * (k_rows[:, None] * np.arange(INNER)[None, :]) / NPHI
    twist_table = np.stack([np.cos(twist), np.sin(twist)]).astype(np.float32)
    angle = 2.0 * np.pi * (np.arange(64)[:, None] * np.arange(INNER)[None, :] % INNER) / INNER
    cosine, sine = [math.sqrt(2.0 / NPHI) * f(angle) for f in (np.cos, np.sin)]
    upper_table = rounded(np.concatenate([cosine, sine, -sine, cosine], axis=1))
    return rounded(outer), rounded(outer.T), twist_table, upper_table


def column(half, j, p, upper):
    return ((half * 2 + j) * 2 + p) * 2 + upper


def forward_part(field_of, outer_ref, twist_ref, inner_ref, zero_ref, out_ref, turned, staged):
    outer = outer_ref[...]
    cos_twist, sin_twist = twist_ref[0], twist_ref[1]
    for v in range(VEC):
        first = dot(outer, field_of(v).astype(BF16))
        real, imag = first[:64], first[64:]
        turned_real = real * cos_twist + imag * sin_twist
        turned_imag = imag * cos_twist - real * sin_twist
        for half in range(2):
            for cycle in range(CYC):
                at = (half * 2 + cycle) * MG
                rows = pl.ds(cycle * 256 + v, MG, stride=VEC)
                turned[half, 0, rows, :] = turned_real[at : at + MG]
                turned[half, 1, rows, :] = turned_imag[at : at + MG]
    for half in range(2):
        both = jnp.concatenate([turned[half, 0], turned[half, 1]], axis=1)
        coeffs = dot(inner_ref[half], both.astype(BF16), NT)
        if half == 0:
            coeffs = coeffs * zero_scale(zero_ref)
        for j in range(2):
            for p in range(2):
                for upper in range(2):
                    for cycle in range(CYC):
                        row = column(half, j, p, upper) * 2 + cycle
                        lanes = cycle * 256 + upper * 128
                        staged[:, row, :] = coeffs[
                            (j * 2 + p) * 32 : (j * 2 + p + 1) * 32, lanes : lanes + 128
                        ]
    out_ref[...] = staged[...].astype(BF16)


def zero_scale(zero_ref):
    lane = lax.broadcasted_iota(jnp.int32, (128, 512), 1)
    own = jnp.concatenate([zero_ref[...]] * 4, axis=1)
    return jnp.where(jnp.logical_and(lane % 256 < VEC, own > 0.0), math.sqrt(0.5), 1.0)


def fill_inner(group_ref, upper_ref, inner_ref, zero_ref):
    groups = [group_ref[s : s + 1, :] for s in range(SLOTS)]
    halves = [group % 2 for group in groups]
    ranks = []
    for s in range(SLOTS):
        rank = jnp.zeros_like(groups[s])
        for earlier in range(s):
            rank = rank + (halves[earlier] == halves[s]).astype(jnp.int32)
        ranks.append(rank)
    index = lax.broadcasted_iota(jnp.int32, (64, BLK), 0)
    is_first = (lax.broadcasted_iota(jnp.int32, (64, 128), 0) == 0).astype(BF16)
    for half in range(2):
        for j in range(2):
            upper = jnp.zeros_like(groups[0])
            for s in range(SLOTS):
                mine = jnp.logical_and(halves[s] == half, ranks[s] == j)
                upper = upper + jnp.where(mine, groups[s] // 2, 0)
            hot = (index == jnp.broadcast_to(upper, (64, BLK))).astype(F32).astype(BF16)
            rows = dot(hot, upper_ref[...], TN).astype(BF16)
            for p in range(2):
                at = (j * 2 + p) * BLK
                inner_ref[half, at : at + BLK, :] = rows[:, p * 256 : (p + 1) * 256]
            if half == 0:
                zero = dot(hot, is_first, TN)
                for p in range(2):
                    at = (j * 2 + p) * BLK
                    zero_ref[at : at + BLK, :] = zero


def first_rows_kernel(
    group_ref, sky_ref, noise_ref, outer_ref, twist_ref, upper_ref,
    out_ref, inner_ref, zero_ref, turned, staged,
):
    fill_inner(group_ref, upper_ref, inner_ref, zero_ref)
    noise = noise_ref[...]
    forward_part(
        lambda v: noise * sky_ref[v],
        outer_ref, twist_ref, inner_ref, zero_ref, out_ref, turned, staged,
    )


def rows_kernel(
    sky_ref, noise_ref, outer_ref, outer_t_ref, twist_ref, inner_ref, zero_ref, coeff_ref,
    out_ref, turned, staged,
):
    staged[...] = coeff_ref[...].astype(F32)
    for half in range(2):
        rows = []
        for j in range(2):
            for p in range(2):
                rows.append(
                    jnp.concatenate(
                        [
                            staged[:, column(half, j, p, upper) * 2 + cycle, :]
                            for cycle in range(CYC)
                            for upper in range(2)
                        ],
                        axis=1,
                    )
                )
        coeffs = jnp.concatenate(rows, axis=0)
        if half == 0:
            coeffs = coeffs * zero_scale(zero_ref)
        coeffs = coeffs.astype(BF16)
        inner = dot(coeffs, inner_ref[half], TN)
        for i in range(MG):
            at = half * CYC * MG + i
            cos_twist = jnp.broadcast_to(twist_ref[0, at : at + 1], (VEC, 128))
            sin_twist = jnp.broadcast_to(twist_ref[1, at : at + 1], (VEC, 128))
            for cycle in range(CYC):
                rows = slice(cycle * 256 + i * VEC, cycle * 256 + (i + 1) * VEC)
                real, imag = inner[rows, :128], inner[rows, 128:]
                turned[half, 0, rows, :] = real * cos_twist - imag * sin_twist
                turned[half, 1, rows, :] = real * sin_twist + imag * cos_twist
    noise = noise_ref[...]
    outer_t = outer_t_ref[...]
    fields = []
    for v in range(VEC):
        spectrum = jnp.concatenate(
            [
                turned[half, part, pl.ds(cycle * 256 + v, MG, stride=VEC), :]
                for part in range(2)
                for half in range(2)
                for cycle in range(CYC)
            ],
            axis=0,
        )
        fields.append(noise * (sky_ref[v] - dot(outer_t, spectrum.astype(BF16))))
    forward_part(
        lambda v: fields[v],
        outer_ref, twist_ref, inner_ref, zero_ref, out_ref, turned, staged,
    )


def own_slots(group_ref, own_ref):
    own = own_ref[0]
    groups = [group_ref[s, own] for s in range(SLOTS)]
    slots = []
    for s in range(SLOTS):
        half = groups[s] % 2
        rank = jnp.int32(0)
        for earlier in range(s):
            rank = rank + jnp.where(groups[earlier] % 2 == half, 1, 0)
        slots.append((2 * half + rank, groups[s]))
    return slots


def table_copy(legendre_ref, table, arrived, group, size):
    blocks = pl.ds(group * GROUP, size)
    return pltpu.make_async_copy(legendre_ref.at[blocks], table.at[blocks], arrived.at[group])


def by_groups(blocks, step):
    def body(group, carry):
        step(group, GROUP)
        return carry

    lax.fori_loop(0, blocks // GROUP, body, 0)
    if blocks % GROUP:
        step(blocks // GROUP, blocks % GROUP)


def mark_slots(group_ref, own_ref, new_slot, zero_slot):
    for s, (slot, group) in enumerate(own_slots(group_ref, own_ref)):
        new_slot[s] = slot
        zero_slot[s] = jnp.where(group == 0, 1, 0)


def products_kernel(
    group_ref, block_ref, own_ref, legendre_ref, signal_ref, out_ref,
    table, sums, order, sequence, pair_slot, pair_live, counter, arrived,
):
    def place_copy(at):
        return pltpu.make_async_copy(legendre_ref.at[order[at]], table.at[at], arrived.at[at])

    base = jnp.int32(0)
    for s, (slot, group) in enumerate(own_slots(group_ref, own_ref)):
        pairs = (17 - group // 8) // 2
        counter[s] = 2 * base

        def mark(pair, carry, slot=slot):
            pair_slot[pair] = slot
            pair_live[pair] = 1
            return carry

        lax.fori_loop(base, base + pairs, mark, 0)
        base = base + pairs

    def place(block, complete):
        slot = block_ref[0, block]
        at = counter[slot]
        order[at] = block
        counter[slot] = at + 1
        place_copy(at).start()
        sequence[complete] = at // 2
        return complete + at % 2

    complete = lax.fori_loop(0, block_ref.shape[1], place, jnp.int32(0))
    for s in range(SLOTS):
        at = counter[s]
        sequence[complete] = at // 2

        @pl.when(at % 2 == 1)
        def _():
            order[at] = order[at - 1]
            pair_live[at // 2] = 0
            place_copy(at).start()

        complete = complete + at % 2
    sums[...] = jnp.zeros_like(sums)

    def pair_step(group, carry):
        pairs = [sequence[group * PAIR_GROUP + n] for n in range(PAIR_GROUP)]
        for pair in pairs:
            place_copy(2 * pair).wait()
            place_copy(2 * pair + 1).wait()
        slots = [pair_slot[pair] for pair in pairs]
        lives = [pair_live[pair].astype(F32) for pair in pairs]
        degrees = [
            (block_ref[1, order[2 * pair]], block_ref[1, order[2 * pair + 1]]) for pair in pairs
        ]
        for pair, slot, live, (first, second) in zip(pairs, slots, lives, degrees):
            precond = [1.0 / (2.0 + signal_ref[pl.ds(degree, 1), :]) for degree in (first, second)]
            precond = jnp.concatenate(precond, axis=1)
            lane = lax.broadcasted_iota(jnp.int32, (1, 256), 1)
            weight = precond * jnp.where(lane < 128, 1.0, live)
            weights = [weight, weight * (2.0 * precond)]
            weights = [jnp.broadcast_to(w, (64, 256)) for w in weights]
            for i in range(MG):
                values = jnp.concatenate([table[2 * pair, i], table[2 * pair + 1, i]], axis=1)
                wide = values.astype(F32)
                once, twice = [(wide * w).astype(BF16) for w in weights]
                left = jnp.concatenate([once, twice], axis=0)
                right = jnp.concatenate([values, once], axis=0)
                sums[slot * MG + i] += dot(left, right, NT)
        return carry

    lax.fori_loop(0, PAIRS // PAIR_GROUP, pair_step, 0)
    lane = lax.broadcasted_iota(jnp.int32, (64, 128), 1)
    double = jnp.where(lane < 64, 1.0, 2.0)
    for at in range(SLOTS * MG):
        rows = slice((at % 8) * 64, (at % 8 + 1) * 64)
        out_ref[at // 8, rows, 0:128] = (sums[at, 0:64] * double).astype(BF16)
        out_ref[at // 8, rows, 128:192] = pltpu.roll(2.0 * sums[at, 64:128], 64, 1)[:, :64].astype(BF16)


def apply_kernel(count, *refs):
    coeff_ref, product_ref = refs[:2]
    earlier = refs[2 : 1 + count]
    kept_ref, out_ref, staged, ordered = refs[1 + count :]
    staged[...] = coeff_ref[...].astype(F32)
    for c in range(16):
        for cycle in range(CYC):
            ordered[c, pl.ds(cycle, BLK, stride=2), :] = staged[:, 2 * c + cycle, :]
    kept_ref[...] = ordered[...].astype(BF16)
    history = [kept_ref] + list(earlier)[::-1]
    lane = lax.broadcasted_iota(jnp.int32, (64, 256), 1) % 128 // VEC
    for slot in range(SLOTS):
        for upper in range(2):
            at = [(slot * 2 + p) * 2 + upper for p in range(2)]
            right = jnp.concatenate(
                [jnp.concatenate([ref[at[0]], ref[at[1]]], axis=1) for ref in history], axis=0
            )
            mixed = dot(product_ref[slot * 2 + upper, :, : 64 * count], right)
            result = mixed[:64]
            for i in range(1, 8):
                result = jnp.where(lane == i, mixed[i * 64 : (i + 1) * 64], result)
            ordered[at[0]] = result[:, :128]
            ordered[at[1]] = result[:, 128:]
    for c in range(16):
        for cycle in range(CYC):
            staged[:, 2 * c + cycle, :] = ordered[c, pl.ds(cycle, BLK, stride=2), :]
    out_ref[...] = staged[...].astype(BF16)


def last_kernel(
    group_ref, block_ref, own_ref, coeff_ref, kept0_ref, kept1_ref, kept2_ref, legendre_ref,
    signal_ref, band_ref, state_ref, band_out,
    table, staged, mixed, packed, products, outgoing, new_slot, zero_slot, arrived, sent,
):
    blocks = legendre_ref.shape[0]

    by_groups(blocks, lambda g, n: table_copy(legendre_ref, table, arrived, g, n).start())
    mark_slots(group_ref, own_ref, new_slot, zero_slot)
    products[...] = jnp.zeros_like(products)
    staged[...] = coeff_ref[...].astype(F32)
    blank = jnp.zeros((64, 128), BF16)
    unit = (
        lax.broadcasted_iota(jnp.int32, (128, 128), 0)
        == lax.broadcasted_iota(jnp.int32, (128, 128), 1)
    ).astype(BF16)
    for slot in range(SLOTS):
        for upper in range(2):
            for sweep in range(ITERS):
                for p in range(2):
                    c = (slot * 2 + p) * 2 + upper
                    if sweep < ITERS - 1:
                        tile = (kept0_ref, kept1_ref, kept2_ref)[sweep][c]
                    else:
                        for cycle in range(CYC):
                            mixed[0, pl.ds(cycle, BLK, stride=2), :] = staged[:, 2 * c + cycle, :]
                        tile = mixed[0, 0:64, :].astype(BF16)
                    turned = dot(unit, jnp.concatenate([tile, blank], axis=0), NT)
                    for i in range(8):
                        rows = pl.ds(sweep * 32 + p, VEC, stride=2)
                        mixed[1 + i, rows, :] = turned[i * VEC : (i + 1) * VEC]
            for i in range(8):
                packed[slot * MG + upper * 8 + i] = mixed[1 + i, :, 0:64].astype(BF16)

    def out_copy(group, size):
        some = pl.ds(group * GROUP, size)
        return pltpu.make_async_copy(outgoing.at[some], state_ref.at[some], sent.at[group])

    def step(group, size):
        table_copy(legendre_ref, table, arrived, group, size).wait()
        some = [group * GROUP + n for n in range(size)]
        slots = [new_slot[block_ref[0, block]] for block in some]
        halves = [
            jnp.where(zero_slot[block_ref[0, block]] > 0, 0.5, 1.0) for block in some
        ]
        degrees = [block_ref[1, block] for block in some]
        for block, slot, half, degree in zip(some, slots, halves, degrees):
            precond = jnp.broadcast_to(1.0 / (2.0 + signal_ref[pl.ds(degree, 1), :]), (32, 128))
            damp = 2.0 * precond
            total = jnp.zeros((VEC, 128), F32)
            for i in range(MG):
                harmonic = dot(packed[slot * MG + i], table[block, i])
                state = harmonic[0:32]
                for sweep in range(1, ITERS):
                    state = harmonic[sweep * 32 : (sweep + 1) * 32] + damp * state
                state = precond * state
                outgoing[block, i * 32 : (i + 1) * 32, :] = state.astype(BF16)
                one = state[:VEC] * state[VEC:]
                if i == 0:
                    one = one * half
                total = total + one
            products[degree] += 2.0 * total
        out_copy(group, size).start()

    by_groups(blocks, step)
    bins = lax.broadcasted_iota(jnp.int32, (128, 128), 0) % BANDS
    lane = lax.broadcasted_iota(jnp.int32, (VEC, 128), 1)
    row = lax.broadcasted_iota(jnp.int32, (VEC, 128), 0)
    sums = jnp.zeros((80, 128), F32)
    for e in range(16):
        member = (jnp.broadcast_to(band_ref[e : e + 1, :], (128, 128)) == bins).astype(F32)
        high = products[e].astype(BF16)
        middle, low = split(products[e] - high.astype(F32))
        weight = split((2 * (e * 128 + lane) + 1).astype(F32))
        left = jnp.concatenate([high, middle, low, weight[0], weight[1]], axis=0)
        sums = sums + dot(left, member.astype(BF16), NT)
    raw = sums[0:16] + (sums[16:32] + sums[32:48])
    counts = sums[48:64] + sums[64:80]
    terms = jnp.where(lane // BANDS == row // 2 % 4, raw * (1.0 / jnp.sqrt(counts)), 0.0)
    terms = jnp.concatenate(
        [jnp.sum(terms[h * 8 : (h + 1) * 8], axis=0, keepdims=True) for h in range(2)], axis=0
    )
    band_out[...] = jnp.broadcast_to(terms[None], band_out.shape)
    by_groups(blocks, lambda g, n: out_copy(g, n).wait())


def fisher_kernel(sim_ref, term_ref, band_out, fisher_out, rows_ref):
    total = term_ref[0]
    for index in range(1, BLK):
        total = total + term_ref[index]
    rows_ref[...] = total
    values = total
    count = values.shape[0] * 4
    total = jnp.sum(values, axis=0, keepdims=True)
    total = jnp.broadcast_to(total, (8, 128))
    total = total + pltpu.roll(total, 64, 1)
    total = total + pltpu.roll(total, 32, 1)
    mean = total[:1] * (1.0 / count)
    center = values - jnp.broadcast_to(mean, values.shape)
    square = precise(center, center, TN)
    fisher = square[:BANDS]
    for s in range(1, 4):
        fisher = fisher + pltpu.roll(square[s * BANDS : (s + 1) * BANDS], 128 - s * BANDS, 1)
    fisher_out[...] = fisher[:, :BANDS] * (1.0 / count)
    own = rows_ref[pl.ds(2 * sim_ref[0], 2), :]
    own = jnp.concatenate([jnp.broadcast_to(own[h : h + 1], (4, 128)) for h in range(2)], axis=0)
    row = lax.broadcasted_iota(jnp.int32, (8, 128), 0) % 4
    band = own
    for s in range(1, 4):
        band = jnp.where(row == s, pltpu.roll(own, 128 - s * BANDS, 1), band)
    band_out[...] = band[:, :BANDS]


def params(megabytes, **more):
    return pltpu.CompilerParams(vmem_limit_bytes=megabytes << 20, **more)


def in_hbm(*arrays):
    return [pltpu.with_memory_space_constraint(array, pltpu.HBM) for array in arrays]


SENT = jax.ShapeDtypeStruct((BLK, 32, 128), BF16)
KEPT = jax.ShapeDtypeStruct((16, 64, 128), BF16)
SMEM = pl.BlockSpec(memory_space=pltpu.SMEM)
VMEM = pl.BlockSpec(memory_space=pltpu.VMEM)
ANY = pl.BlockSpec(memory_space=pl.ANY)


def row_scratch():
    return [pltpu.VMEM((2, 2, 512, 128), F32), pltpu.VMEM((BLK, 32, 128), F32)]


def first_transforms(groups, sky, noise, outer, twist, upper):
    return pl.pallas_call(
        first_rows_kernel,
        out_shape=(
            SENT,
            jax.ShapeDtypeStruct((2, 128, 256), BF16),
            jax.ShapeDtypeStruct((128, 128), F32),
        ),
        scratch_shapes=row_scratch(),
        compiler_params=params(28),
        name="first_rows",
    )(*in_hbm(groups, sky, noise, outer, twist, upper))


def row_transforms(sky, noise, outer, outer_t, twist, inner, zero_rows, coeffs):
    return pl.pallas_call(
        rows_kernel,
        out_shape=SENT,
        scratch_shapes=row_scratch(),
        compiler_params=params(28),
        name="rows",
    )(sky, noise, outer, outer_t, twist, inner, zero_rows, coeffs)


def cycle_products(scalars, legendre, signal):
    return pl.pallas_call(
        products_kernel,
        out_shape=jax.ShapeDtypeStruct((8, 512, 192), BF16),
        in_specs=[SMEM, SMEM, SMEM, ANY, VMEM],
        scratch_shapes=[
            pltpu.VMEM((2 * PAIRS,) + legendre.shape[1:], BF16),
            pltpu.VMEM((SLOTS * MG, 128, 128), F32),
            pltpu.SMEM((2 * PAIRS,), jnp.int32),
            pltpu.SMEM((PAIRS + 2,), jnp.int32),
            pltpu.SMEM((PAIRS,), jnp.int32),
            pltpu.SMEM((PAIRS,), jnp.int32),
            pltpu.SMEM((SLOTS,), jnp.int32),
            pltpu.SemaphoreType.DMA((2 * PAIRS,)),
        ],
        compiler_params=params(28),
        name="cycle_products",
    )(*in_hbm(*scalars, legendre, signal))


def apply_products(coeffs, products, kept):
    count = len(kept) + 1

    def body(*refs):
        apply_kernel(count, *refs)

    return pl.pallas_call(
        body,
        out_shape=(KEPT, SENT),
        scratch_shapes=[pltpu.VMEM((BLK, 32, 128), F32), pltpu.VMEM((16, 64, 128), F32)],
        compiler_params=params(28),
        name="apply_products_" + str(count),
    )(coeffs, products, *kept)


def last_step(copies, scalars, coeffs, kept, legendre, signal, bands):
    (legendre,) = in_hbm(legendre)
    return pl.pallas_call(
        last_kernel,
        out_shape=(
            jax.ShapeDtypeStruct((legendre.shape[0], 512, 128), BF16),
            jax.ShapeDtypeStruct((copies, 2, 128), F32),
        ),
        in_specs=[SMEM] * 3 + [VMEM] * 4 + [ANY, VMEM, VMEM],
        out_specs=(ANY, VMEM),
        scratch_shapes=[
            pltpu.VMEM(legendre.shape, BF16),
            pltpu.VMEM((BLK, 32, 128), F32),
            pltpu.VMEM((9, 128, 128), F32),
            pltpu.VMEM((SLOTS * MG, 128, 64), BF16),
            pltpu.VMEM((16, VEC, 128), F32),
            pltpu.VMEM((legendre.shape[0], 512, 128), BF16),
        ]
        + [
            pltpu.SMEM((SLOTS,), jnp.int32),
            pltpu.SMEM((SLOTS,), jnp.int32),
            pltpu.SemaphoreType.DMA((-(-legendre.shape[0] // GROUP),)),
            pltpu.SemaphoreType.DMA((-(-legendre.shape[0] // GROUP),)),
        ],
        compiler_params=params(28),
        name="last_modes",
    )(*scalars, coeffs, *kept, legendre, signal, bands)


def fisher_step(sim_index, terms):
    return pl.pallas_call(
        fisher_kernel,
        out_shape=(
            jax.ShapeDtypeStruct((8, BANDS), F32),
            jax.ShapeDtypeStruct((BANDS, BANDS), F32),
        ),
        in_specs=[SMEM, VMEM],
        scratch_shapes=[pltpu.VMEM(terms.shape[1:], F32)],
        compiler_params=params(28),
        name="fisher",
    )(sim_index, terms)


def exchange(rows):
    return lax.all_to_all(rows, "blk", 0, 0, tiled=True)


def shards(sky_maps, noise_weight, signal_inverse, legendre, m_groups, block_list, band_of_ell):
    blk_index = lax.axis_index("blk")
    set_count, sim_local, cycle_local, cycle_pixels = sky_maps.shape
    block_count = legendre.shape[0]
    outer, outer_t, twist, upper = [jnp.asarray(t) for t in constant_tables()]
    sky = sky_maps.reshape(set_count, sim_local, cycle_local, OUTER, INNER)
    sky = sky.transpose(0, 1, 3, 2, 4).reshape(VEC, OUTER * CYC, INNER)
    noise = noise_weight.reshape(CYC, OUTER, INNER).transpose(1, 0, 2).reshape(OUTER * CYC, INNER)
    scalars = (m_groups.T, block_list.T, blk_index.astype(jnp.int32).reshape(1))
    signal = signal_inverse.reshape(16, 128)
    bands = band_of_ell.reshape(16, 128)

    rows, inner, zero_rows = first_transforms(scalars[0], sky, noise, outer, twist, upper)
    sim_index = lax.axis_index("sim").astype(jnp.int32).reshape(1)
    own, sim_index, rows = lax.optimization_barrier((scalars[2], sim_index, rows))
    products = cycle_products(scalars[:2] + (own,), legendre, signal)
    kept = []
    for sweep in range(ITERS - 1):
        coeffs, rows = apply_products(exchange(rows), products, kept)
        kept.append(coeffs)
        rows = row_transforms(
            sky, noise, outer, outer_t, twist, inner, zero_rows, exchange(rows)
        )
    sims = lax.axis_size("sim")
    state, copies = last_step(BLK * sims, scalars, exchange(rows), kept, legendre, signal, bands)
    terms = lax.all_to_all(copies, ("blk", "sim"), 0, 0, tiled=True)
    band_proj, fisher = fisher_step(sim_index, terms.reshape(BLK, 2 * sims, 128))
    filtered = state.reshape(block_count, MG, set_count, sim_local, 2, 128)
    return (filtered, band_proj, fisher)


def solution(mesh):
    return jax.shard_map(
        shards,
        mesh=mesh,
        in_specs=(
            P(None, "sim", "blk", None),
            P("blk", None),
            P(),
            P("blk", None, None, None),
            P(),
            P("blk", None),
            P(),
        ),
        out_specs=(P("blk", None, None, "sim", None, None), P("sim", None), P()),
        check_vma=False,
    )
```
